32 devices in a mesh: dp: 4 (over y, x), tm: 8 (over z, core).
Axes of the slice: x: 2, y: 2, z: 4, core: 2. Of those that a mesh axis runs over, the one named last changes fastest.
Arguments:
- frames: bfloat16 [4, 8, 4, 128, 1536], P('dp', 'tm'), may hold values from -6 to 6
- route: int32 [4, 8, 4], P('dp', 'tm'), may hold values from 0 to 31, as said below
- utterance: int32 [4, 8, 4], P('dp', 'tm'), may hold values from 0 to 2, as said below
- gain: float32 [1536], replicated, may hold values from 0.5 to 1.5
- w_in: bfloat16 [1536, 3072], P('dp'), may hold values from -0.15625 to 0.15625
- kernel: float32 [31, 1536], replicated, may hold values from -3 to 3
- cotangent: bfloat16 [4, 8, 4, 128, 1536], P('dp', 'tm'), may hold values from -4 to 4
Outputs:
- grad_frames: bfloat16 [4, 8, 4, 128, 1536], P('dp', 'tm')
- grad_w_in: float32 [1536, 3072], P('dp', 'tm')
- grad_kernel: float32 [31, 1536], replicated
- grad_gain: float32 [1536], replicated
The draws below stay inside these ranges and needn't reach their ends.
Inputs may be any that keep to these rules, and one draw needn't show every extreme that they name: route[g, s, j] is owner * 4 + slot for panel j of loader s of data group g; over one data group every stream position appears exactly once, and the 4 panels of one loader go to 4 different owners. Utterance ids never fall along a data group's stream (owner after owner, slot after slot), start at 0 in each group, each utterance is a run of whole panels, and every group holds exactly 3 utterances.
All inputs are finite; a program needn't handle non-finite values.
Results may differ from the reference program's by a relative error of at most 0.015.
Values may be sent and summed in bfloat16 or wider, within the bound.
No kernel may reach another device: no remote copies, remote signals or barrier semaphores. Data moves between devices by JAX's collectives and lax.ppermute only.
A program may use at most 128 MiB of HBM per device.

```python
import jax
import jax.numpy as jnp
from jax import lax

D = 1536
KERNEL = 31
PANEL = 128
PANELS = 4
N_DP = 4
N_TM = 8


def packing_plan(key):

    def draw_group(group_key):
        key_owner, key_loader, key_offset, key_slot, key_first, key_second = jax.random.split(group_key, 6)
        owner_perm = jax.random.permutation(key_owner, N_TM)
        loader_perm = jax.random.permutation(key_loader, N_TM)
        offsets = jax.random.permutation(key_offset, N_TM)[:PANELS]
        slot_order = jax.random.permutation(key_slot, PANELS)
        owners = owner_perm[(loader_perm[:, None] + offsets[None, :]) % N_TM]
        target = (owners * PANELS + slot_order[None, :]).astype(jnp.int32)
        total_panels = N_TM * PANELS
        half = total_panels // 2
        first = jax.random.randint(key_first, (), 1, half + 1)
        second = jax.random.randint(key_second, (), half + 1, total_panels)
        starts = jnp.zeros((total_panels,), jnp.int32).at[0].set(1).at[first].set(1).at[second].set(1)
        utterances = (jnp.cumsum(starts) - 1).astype(jnp.int32)
        return (target, utterances[target].astype(jnp.int32))
    group_keys = jax.random.split(jax.random.fold_in(key, 7), N_DP)
    return jax.vmap(draw_group)(group_keys)


def draw_route(key, part):
    return packing_plan(key)[0]


def draw_utterance(key, part):
    return packing_plan(key)[1]


def levels(stream_key, shape, cuts, smallest, largest):
    def one(position, blocks):
        heights = jax.random.uniform(jax.random.fold_in(jax.random.fold_in(stream_key, 6), position), (blocks,), jnp.float32, smallest / len(cuts), largest / len(cuts))
        return jnp.repeat(jnp.exp(heights), shape[position] // blocks).reshape((-1,) + (1,) * (len(shape) - position - 1))

    loudness = one(*cuts[0])
    for cut in cuts[1:]:
        loudness = loudness * one(*cut)
    return loudness


def noise(rng, shape, width, limit, cuts=(), dtype=jnp.bfloat16):
    factor_of = levels(rng, shape, cuts, -0.22, 0.18) if cuts else 1.0
    entries = jax.random.normal(rng, shape, jnp.float32) * width * factor_of
    return jnp.minimum(jnp.maximum(entries, -limit), limit).astype(dtype)


def setup_inputs(seed: int = 0) -> dict:
    key_of = jax.random.split(jax.random.key(seed), 8)
    frames = noise(key_of[0], (N_DP, N_TM, PANELS, PANEL, D), 1.0, 6.0, ((0, 4), (1, 8)))
    route = draw_route(jax.random.fold_in(key_of[7], 71), 0)
    utterance = draw_utterance(jax.random.fold_in(key_of[7], 71), 0)
    gain = jnp.clip(1.0 + 0.1 * jax.random.normal(key_of[3], (D,), jnp.float32), 0.5, 1.5)
    w_in = noise(key_of[4], (D, 2 * D), D ** -0.5, 0.15625, ((0, 4),))
    kernel = noise(key_of[5], (KERNEL, D), 0.2, 3.0, (), jnp.float32)
    cotangent = noise(key_of[6], (N_DP, N_TM, PANELS, PANEL, D), 0.25, 4.0, ((0, 4), (1, 8)))
    return dict(frames=frames, route=route, utterance=utterance, gain=gain, w_in=w_in, kernel=kernel, cotangent=cotangent)


def outer_sum(left, right):
    return lax.dot_general(left, right, (((0,), (0,)), ((), ())), preferred_element_type=jnp.float32)

def times_transposed(left, right):
    return lax.dot_general(left, right, (((1,), (1,)), ((), ())), preferred_element_type=jnp.float32)

def rounded(term):
    return lax.optimization_barrier(term.astype(jnp.bfloat16)).astype(jnp.float32)

def masked_taps(padded, masks, kernel, rows, flip):
    taps = kernel.shape[0]
    total = jnp.zeros((rows, kernel.shape[1]), jnp.float32)
    for tap in range(taps):
        source = taps - 1 - tap if flip else tap
        piece = jnp.where(masks[source], padded[source:source + rows].astype(jnp.float32), 0.0)
        total = total + kernel[tap] * piece
    return total

def reference(frames, route, utterance, gain, w_in, kernel, cotangent):
    reach = KERNEL // 2
    count = N_TM * PANELS
    total_rows = count * PANEL
    owner_rows = PANELS * PANEL

    def group_step(carry, pieces):
        frames_g, route_g, labels_g, upstream_g = pieces
        flat_target = route_g.reshape(-1).astype(jnp.int32)
        stream = jnp.zeros((count, PANEL, D), jnp.bfloat16).at[flat_target].set(frames_g.reshape(count, PANEL, D))
        panel_ids = jnp.zeros((count,), jnp.int32).at[flat_target].set(labels_g.reshape(-1).astype(jnp.int32))
        row_ids = jnp.repeat(panel_ids, PANEL)
        padded_ids = jnp.concatenate([jnp.full((reach,), -1, jnp.int32), row_ids, jnp.full((reach,), -1, jnp.int32)])
        masks = [(padded_ids[tap:tap + total_rows] == row_ids)[:, None] for tap in range(KERNEL)]
        values = stream.reshape(total_rows, D).astype(jnp.float32)
        center = lax.optimization_barrier(jnp.mean(values, axis=1, keepdims=True))
        variance = lax.optimization_barrier(jnp.mean((values - center) ** 2, axis=1, keepdims=True))
        inv_scale = lax.rsqrt(variance + 1e-05)
        unit = (values - center) * inv_scale
        normed = (unit * gain).astype(jnp.bfloat16)
        pre = jnp.dot(normed, w_in, preferred_element_type=jnp.float32)
        linear = pre[:, :D]
        gate_sig = jax.nn.sigmoid(pre[:, D:])
        glu = (linear * gate_sig).astype(jnp.bfloat16)
        zeros_rim = jnp.zeros((reach, D), jnp.bfloat16)
        glu_padded = jnp.concatenate([zeros_rim, glu, zeros_rim])
        depth = masked_taps(glu_padded, masks, kernel, total_rows, False)
        depth_sig = jax.nn.sigmoid(depth)
        upstream = upstream_g.reshape(total_rows, D)
        grad_depth = (upstream.astype(jnp.float32) * depth_sig * (1.0 + depth * (1.0 - depth_sig))).astype(jnp.bfloat16)
        grad_padded = jnp.concatenate([zeros_rim, grad_depth, zeros_rim])
        grad_depth_f = grad_depth.astype(jnp.float32)
        kernel_term = jnp.stack([lax.optimization_barrier(jnp.sum(grad_depth_f * jnp.where(masks[tap], glu_padded[tap:tap + total_rows].astype(jnp.float32), 0.0), axis=0)) for tap in range(KERNEL)])
        grad_glu = masked_taps(grad_padded, masks, kernel, total_rows, True)
        grad_pre = jnp.concatenate([grad_glu * gate_sig, grad_glu * linear * gate_sig * (1.0 - gate_sig)], axis=1).astype(jnp.bfloat16)
        grad_normed = times_transposed(grad_pre, w_in)
        gain_term = lax.optimization_barrier(jnp.sum(grad_normed * unit, axis=0))
        scaled = grad_normed * gain
        grad_x = upstream.astype(jnp.float32) + inv_scale * (scaled - lax.optimization_barrier(jnp.mean(scaled, axis=1, keepdims=True)) - unit * lax.optimization_barrier(jnp.mean(scaled * unit, axis=1, keepdims=True)))
        grad_x = grad_x.astype(jnp.bfloat16)

        def owner_step(accum, blocks):
            normed_b, grad_pre_b = blocks
            return (accum + rounded(outer_sum(normed_b, grad_pre_b)), None)
        owner_blocks = (normed.reshape(N_TM, owner_rows, D), grad_pre.reshape(N_TM, owner_rows, 2 * D))
        sums_in = lax.scan(owner_step, carry[0], owner_blocks)[0]
        grad_frames_g = grad_x.reshape(count, PANEL, D)[flat_target].reshape(N_TM, PANELS, PANEL, D)
        return ((sums_in, carry[1] + kernel_term, carry[2] + gain_term), grad_frames_g)
    start = (jnp.zeros((D, 2 * D), jnp.float32), jnp.zeros((KERNEL, D), jnp.float32), jnp.zeros((D,), jnp.float32))
    totals, grad_frames = lax.scan(group_step, start, (frames, route, utterance, cotangent))
    return (grad_frames, totals[0], totals[1], totals[2])
```

```python
import functools

import jax
import jax.numpy as jnp
from jax import lax
from jax.experimental import pallas as pl
from jax.experimental.pallas import tpu as pltpu
from jax.sharding import PartitionSpec as P

BF = jnp.bfloat16
F32 = jnp.float32
RIM = 16
LANES = 128
TILE = 32


def params(count, mib=48):
    return pltpu.CompilerParams(
        dimension_semantics=("arbitrary",) * count, vmem_limit_bytes=mib << 20
    )


def flip(axis, mask):
    return [(i, i ^ mask) for i in range(lax.axis_size(axis))]


def flip_bit(axis, bit):
    return flip(axis, 1 << bit)


def bits_of(count):
    bits = count.bit_length() - 1
    assert 1 << bits == count
    return list(range(bits))


def copy_body(_, source, target):
    target[...] = source[...]


def pick_panels(source, index, count):
    _, rows, width = source.shape
    return pl.pallas_call(
        copy_body,
        grid_spec=pltpu.PrefetchScalarGridSpec(
            num_scalar_prefetch=1,
            grid=(count,),
            in_specs=[pl.BlockSpec((1, rows, width), lambda i, idx: (idx[i], 0, 0))],
            out_specs=pl.BlockSpec((1, rows, width), lambda i, idx: (i, 0, 0)),
        ),
        out_shape=jax.ShapeDtypeStruct((count, rows, width), source.dtype),
        compiler_params=params(1),
        name="pick_panels",
    )(index, source)


def gather_order(block, order):
    have = block[None]
    relative = [0]
    for bit in order:
        got = lax.ppermute(have, "dp", flip_bit("dp", bit))
        have = jnp.concatenate([have, got], axis=0)
        relative = relative + [r ^ (1 << bit) for r in relative]
    return have, relative


def gather_weights(w_in, core):
    shard, width = w_in.shape
    quarter = shard // 4
    count = lax.axis_size("dp")
    place = lax.axis_index("dp")
    bits = bits_of(count)
    half = lax.dynamic_slice_in_dim(w_in, core * (2 * quarter), 2 * quarter, axis=0)
    first, first_rel = gather_order(half[:quarter], bits)
    second, second_rel = gather_order(half[quarter:], bits[::-1])
    other_first = lax.ppermute(first, "tm", flip_bit("tm", 0))
    other_second = lax.ppermute(second, "tm", flip_bit("tm", 0))
    rels = [first_rel, second_rel]

    def out_index(side):
        index = []
        for source in range(2):
            for position in range(count):
                index.append(((place ^ rels[source][position]) * 2 + side) * 2 + source)
        return jnp.stack(index).astype(jnp.int32)

    def body(_, a, b, *rest):
        target = rest[-1]
        for number, ref in enumerate((a, b)):

            @pl.when(pl.program_id(0) == number)
            def _():
                target[...] = ref[...]

    def spec(number):
        def index(source, position, _):
            last = count - 1 if number == 0 else 0
            return (jnp.where(source == number, position, last), 0, 0)

        return pl.BlockSpec((1, quarter, width), index)

    def put(side, pair, *base):
        return pl.pallas_call(
            body,
            grid_spec=pltpu.PrefetchScalarGridSpec(
                num_scalar_prefetch=1,
                grid=(2, count),
                in_specs=[spec(0), spec(1)] + [pl.BlockSpec(memory_space=pl.ANY) for _ in base],
                out_specs=pl.BlockSpec(
                    (1, quarter, width),
                    lambda source, position, idx: (idx[source * count + position], 0, 0),
                ),
            ),
            out_shape=jax.ShapeDtypeStruct((4 * count, quarter, width), w_in.dtype),
            input_output_aliases={3: 0} if base else {},
            compiler_params=params(2),
            name="put_weights",
        )(out_index(side), *pair, *base)

    full = put(core, (first, second))
    full = put(1 - core, (other_first, other_second), full)
    return full.reshape(4 * quarter * count, width)


def forward_body(source, x_hbm, gain_ref, lin_w, gate_w, normed, pair, lin_out, gate_out, glu_out, xs, sems, *, panels):
    rows = xs.shape[1]

    def fetch(s):
        return pltpu.make_async_copy(x_hbm.at[source[s]], xs.at[s], sems.at[s])

    @pl.when(pl.program_id(0) == 0)
    def _():
        for s in range(panels):
            fetch(s).start()
        for s in range(panels):
            fetch(s).wait()

            x = xs[s].astype(F32)
            x = x - jnp.mean(x, axis=1, keepdims=True)
            scale = lax.rsqrt(jnp.mean(x * x, axis=1, keepdims=True) + 1e-05)
            normed[s * rows : (s + 1) * rows, :] = (x * scale * gain_ref[...]).astype(BF)

        pair[...] = normed[...]

    lin = jnp.dot(normed[...], lin_w[...], preferred_element_type=F32)
    lin_out[...] = lin
    gate = jnp.dot(normed[...], gate_w[...], preferred_element_type=F32)
    gate_out[...] = gate
    glu_out[...] = (lin * jax.nn.sigmoid(gate)).astype(BF)


def forward(arrived, source, gain, full_in, panels, block):
    _, rows, width = arrived.shape
    blocks = width // block
    column = pl.BlockSpec((panels * rows, block), lambda j, idx: (0, j))
    whole = pl.BlockSpec((panels * rows, width), lambda j, idx: (0, 0))
    wide = lambda dtype, times=1: jax.ShapeDtypeStruct((times * panels * rows, width), dtype)
    return pl.pallas_call(
        functools.partial(forward_body, panels=panels),
        grid_spec=pltpu.PrefetchScalarGridSpec(
            num_scalar_prefetch=1,
            grid=(blocks,),
            in_specs=[
                pl.BlockSpec(memory_space=pl.ANY),
                pl.BlockSpec((1, width), lambda j, idx: (0, 0)),
                pl.BlockSpec((width, block), lambda j, idx: (0, j)),
                pl.BlockSpec((width, block), lambda j, idx: (0, blocks + j)),
            ],
            out_specs=[
                whole,
                whole,
                column,
                column,
                column,
            ],
            scratch_shapes=[
                pltpu.VMEM((panels, rows, width), BF),
                pltpu.SemaphoreType.DMA((panels,)),
            ],
        ),
        out_shape=[wide(BF), wide(BF, 2), wide(F32), wide(F32), wide(BF)],
        compiler_params=params(1),
        name="forward",
    )(source, arrived, gain.reshape(1, width), full_in, full_in)


def fill_padded(flags, padded, main, low, high, panels, length):
    for s in range(panels):
        at = s * length
        middle = main[at : at + length, :].astype(F32)
        before = low[...] if s == 0 else main[at - RIM : at, :]
        after = high[...] if s == panels - 1 else main[at + length : at + length + RIM, :]
        before = jnp.where(flags[s] > 0, before.astype(F32), 0.0)
        after = jnp.where(flags[panels + s] > 0, after.astype(F32), 0.0)
        for chunk in range(main.shape[1] // LANES):
            lanes = slice(chunk * LANES, (chunk + 1) * LANES)
            padded[chunk, s, RIM : RIM + length, :] = middle[:, lanes]
            padded[chunk, s, 0:RIM, :] = before[:, lanes]
            padded[chunk, s, RIM + length :, :] = after[:, lanes]


def shifted_sum(padded, weights, chunk, s, start, taps, flip):
    lanes = pl.ds(chunk * LANES, LANES)
    total = jnp.zeros((TILE, LANES), F32)
    for tap in range(taps):
        offset = taps - tap if flip else tap + 1
        view = padded[chunk, s, pl.ds(start + offset, TILE), :]
        total = total + weights[pl.ds(tap, 1), lanes] * view
    return total


def tiles(width, panels, length, work):
    for chunk in range(width // LANES):

        def step(s, carry):
            for start in range(0, length, TILE):
                rows = pl.ds(pl.multiple_of(s * length + start, TILE), TILE)
                work(chunk, s, start, rows, pl.ds(chunk * LANES, LANES))
            return carry

        lax.fori_loop(0, panels, step, 0)


def depth_body(flags, glu, low, high, upstream, weights, out, padded, *, panels, length, taps):
    fill_padded(flags, padded, glu, low, high, panels, length)

    def work(chunk, s, start, rows, lanes):
        depth = shifted_sum(padded, weights, chunk, s, start, taps, False)
        sig = jax.nn.sigmoid(depth)
        up = upstream[rows, lanes].astype(F32)
        out[rows, lanes] = (up * sig * (1.0 + depth * (1.0 - sig))).astype(BF)

    tiles(glu.shape[1], panels, length, work)


def taps_body(flags, glu, low, high, grad, out, padded, partial, *, panels, length, taps):
    fill_padded(flags, padded, glu, low, high, panels, length)
    for chunk in range(glu.shape[1] // LANES):
        lanes = pl.ds(chunk * LANES, LANES)
        partial[...] = jnp.zeros_like(partial)

        def step(s, carry):
            rows = pl.ds(pl.multiple_of(s * length, length), length)
            g = grad[rows, lanes].astype(F32)
            for tap in range(taps):
                product = g * padded[chunk, s, pl.ds(tap + 1, length), :]
                partial[tap] += jnp.sum(product.reshape(length // 8, 8, LANES), axis=0)
            return carry

        lax.fori_loop(0, panels, step, 0)
        out[:, lanes] = jnp.sum(partial[...], axis=1)


def gated_body(flags, grad, low, high, lin, gate, weights, *refs, panels, length, taps):
    *outs, padded = refs
    fill_padded(flags, padded, grad, low, high, panels, length)

    def work(chunk, s, start, rows, lanes):
        total = shifted_sum(padded, weights, chunk, s, start, taps, True)
        sig = jax.nn.sigmoid(gate[rows, lanes])
        scaled = total * sig
        results = (scaled.astype(BF), (scaled * lin[rows, lanes] * (1.0 - sig)).astype(BF))
        for number, out in enumerate(outs):
            out[rows, lanes] = results[number % 2]

    tiles(grad.shape[1], panels, length, work)


def gated(flags, grad_depth, low, high, lin, gate, kernel, block, parities, parity, sizes, twice=False):
    rows, width = grad_depth.shape
    panels = sizes["panels"]
    column = lambda height: pl.BlockSpec((height, block), lambda j, idx: (0, j * parities + idx[2 * panels]))
    shapes = [jax.ShapeDtypeStruct((rows * times, width // parities), BF) for times in (1, 1, 2, 2)]
    shapes = shapes[: 4 if twice else 2]
    return pl.pallas_call(
        functools.partial(gated_body, **sizes),
        grid_spec=pltpu.PrefetchScalarGridSpec(
            num_scalar_prefetch=1,
            grid=(width // block // parities,),
            in_specs=[column(h) for h in (rows, RIM, RIM, rows, rows, kernel.shape[0])],
            out_specs=[pl.BlockSpec((rows, block), lambda j, idx: (0, j)) for _ in shapes],
            scratch_shapes=[
                pltpu.VMEM((block // LANES, panels, sizes["length"] + 2 * RIM, LANES), F32)
            ],
        ),
        out_shape=shapes,
        compiler_params=params(1),
        name="gated",
    )(jnp.append(flags, parity), grad_depth, low, high, lin, gate, kernel)


def back_body(source, *refs, grads, block, panels, piece):
    gradients = refs[:grads]
    w_ref, x_hbm, up_hbm, gain_ref, out_hbm, gain_out, total, xs, ups, outs, sems = refs[grads:]
    step = pl.program_id(0)

    def fetch(s):
        return (
            pltpu.make_async_copy(x_hbm.at[source[s]], xs.at[s], sems.at[s]),
            pltpu.make_async_copy(up_hbm.at[s], ups.at[s], sems.at[panels + s]),
        )

    def put(s):
        return pltpu.make_async_copy(outs.at[s], out_hbm.at[source[s]], sems.at[2 * panels + s])

    @pl.when(step == 0)
    def _():
        for s in range(panels):
            for copy in fetch(s):
                copy.start()

    acc = None
    for number, grad in enumerate(gradients):
        pieces = grad.shape[1] // piece
        for i in range(pieces):
            column = (number % 2 * pieces + i) * (grads // 2) * piece
            if grads > 2:
                column = column + (source[panels] ^ (number // 2)) * piece
                column = pl.multiple_of(column, LANES)
            term = lax.dot_general(
                grad[:, i * piece : (i + 1) * piece],
                w_ref[:, pl.ds(column, piece)],
                (((1,), (1,)), ((), ())),
                preferred_element_type=F32,
            )
            acc = term if acc is None else acc + term
    total[:, pl.ds(pl.multiple_of(step * block, block), block)] = acc

    @pl.when(step == pl.num_programs(0) - 1)
    def _():
        rows = xs.shape[1]
        gain = gain_ref[...]
        gain_sum = jnp.zeros_like(gain)
        for s in range(panels):
            for copy in fetch(s):
                copy.wait()

            x = xs[s].astype(F32)
            x = x - jnp.mean(x, axis=1, keepdims=True)
            scale = lax.rsqrt(jnp.mean(x * x, axis=1, keepdims=True) + 1e-05)
            unit = x * scale
            g = total[s * rows : (s + 1) * rows, :]
            gain_sum = gain_sum + jnp.sum(g * unit, axis=0, keepdims=True)
            q = g * gain
            mean_q = jnp.mean(q, axis=1, keepdims=True)
            mean_u = jnp.mean(q * unit, axis=1, keepdims=True)
            outs[s] = (ups[s].astype(F32) + scale * (q - mean_q - unit * mean_u)).astype(BF)
            put(s).start()
        gain_out[...] = gain_sum
        for s in range(panels):
            put(s).wait()


def back(gradients, core, full_in, arrived, source, upstream, gain, piece, block):
    _, rows, width = arrived.shape
    panels = upstream.shape[0]
    constant = lambda rank: (lambda n, idx: (0,) * rank)
    hbm = pl.BlockSpec(memory_space=pl.ANY)
    panel_scratch = pltpu.VMEM((panels, rows, width), BF)
    return pl.pallas_call(
        functools.partial(back_body, grads=len(gradients), block=block, panels=panels, piece=piece),
        grid_spec=pltpu.PrefetchScalarGridSpec(
            num_scalar_prefetch=1,
            grid=(width // block,),
            in_specs=[pl.BlockSpec(g.shape, constant(2)) for g in gradients]
            + [
                pl.BlockSpec((block, full_in.shape[1]), lambda n, idx: (n, 0)),
                hbm,
                hbm,
                pl.BlockSpec((1, width), constant(2)),
            ],
            out_specs=[hbm, pl.BlockSpec((1, width), constant(2))],
            scratch_shapes=[
                pltpu.VMEM((panels * rows, width), F32),
                panel_scratch,
                panel_scratch,
                panel_scratch,
                pltpu.SemaphoreType.DMA((3 * panels,)),
            ],
        ),
        out_shape=[
            jax.ShapeDtypeStruct(arrived.shape, BF),
            jax.ShapeDtypeStruct((1, width), F32),
        ],
        compiler_params=params(1),
        name="back",
    )(jnp.append(source, core), *gradients, full_in, arrived, upstream, gain.reshape(1, width))


def outer_sum(left, right):
    return lax.dot_general(
        left, right, (((0,), (0,)), ((), ())), preferred_element_type=F32
    ).astype(BF)


def halve(block, order):
    place = lax.axis_index("dp")
    count = lax.axis_size("dp")
    bits = len(bits_of(count))
    shape = block.shape[1:]
    block = block.reshape((2,) * bits + shape)
    live = list(reversed(range(bits)))
    for bit in order:
        dim = live.index(bit)
        mine = (place >> bit) & 1
        keep = lax.dynamic_index_in_dim(block, mine, dim, keepdims=False)
        send = lax.dynamic_index_in_dim(block, 1 - mine, dim, keepdims=False)
        got = lax.ppermute(send, "dp", flip_bit("dp", bit))
        block = (keep.astype(F32) + got.astype(F32)).astype(BF)
        live.remove(bit)
    return block


def sum_everywhere(values):
    steps = [("dp", bit) for bit in bits_of(lax.axis_size("dp"))] + [("tm", 0)]
    pad = -values.shape[0] % (1 << len(steps))
    rows = values.shape[0]
    values = jnp.pad(values, ((0, pad), (0, 0)))
    side = lambda axis, bit: (lax.axis_index(axis) >> bit) & 1
    for axis, bit in steps:
        halves = values.reshape(2, values.shape[0] // 2, values.shape[1])
        mine = side(axis, bit)
        send = lax.dynamic_index_in_dim(halves, 1 - mine, 0, keepdims=False)
        keep = lax.dynamic_index_in_dim(halves, mine, 0, keepdims=False)
        values = keep + lax.ppermute(send, axis, flip_bit(axis, bit))
    terms = [values]
    for mask in range(2, lax.axis_size("tm"), 2):
        terms.append(lax.ppermute(values, "tm", flip("tm", mask)))
    while len(terms) > 1:
        terms = [a + b for a, b in zip(terms[::2], terms[1::2])]
    values = terms[0]
    for axis, bit in steps[::-1]:
        got = lax.ppermute(values, axis, flip_bit(axis, bit))
        first = side(axis, bit) == 0
        values = jnp.concatenate([jnp.where(first, values, got), jnp.where(first, got, values)])
    return values[:rows]


def sum_across(share):
    count = share.shape[0]
    place = lax.axis_index("tm") // 2
    total = lax.dynamic_index_in_dim(share, place, 0, keepdims=False).astype(F32)
    for turn in range(1, count):
        piece = lax.dynamic_index_in_dim(share, place ^ turn, 0, keepdims=False)
        pairs = [(i, i ^ (2 * turn)) for i in range(2 * count)]
        total = total + lax.ppermute(piece, "tm", pairs).astype(F32)
    return total


def edges(values, width):
    count = lax.axis_size("tm")
    low = lax.ppermute(values[-width:], "tm", [(i, i + 1) for i in range(count - 1)])
    high = lax.ppermute(values[:width], "tm", [(i + 1, i) for i in range(count - 1)])
    return low, high


def local(frames, route, utterance, gain, w_in, kernel, cotangent):
    panels, length, width = frames.shape[2:]
    owners = lax.axis_size("tm")
    rows = panels * length
    taps = kernel.shape[0]
    reach = taps // 2
    assert reach < RIM and taps == 31
    loaded = frames[0, 0]
    target = route[0, 0]
    labels = utterance[0, 0]
    upstream = cotangent[0, 0]
    core = lax.axis_index("tm") % 2
    owner_of = target // panels
    pick = owner_of[None, :] == jnp.arange(owners, dtype=jnp.int32)[:, None]
    panel_of = jnp.sum(jnp.where(pick, jnp.arange(panels, dtype=jnp.int32)[None, :], 0), axis=1)
    outgoing = pick_panels(loaded, panel_of.astype(jnp.int32), owners)
    arrived = lax.all_to_all(outgoing, "tm", split_axis=0, concat_axis=0, tiled=True)
    me = lax.axis_index("tm")
    tags = jnp.stack([target, labels + 1])[None]
    tags = jnp.concatenate([tags, lax.ppermute(tags, "tm", flip_bit("tm", 0))])
    rest = [lax.ppermute(tags, "tm", flip("tm", i)) for i in range(2, owners, 2)]
    tags = jnp.concatenate([tags] + rest)
    loader = (jnp.arange(owners, dtype=jnp.int32) ^ me)[None, :, None]
    position = me * panels - 1 + jnp.arange(panels + 2, dtype=jnp.int32)
    found = tags[None, :, 0] == position[:, None, None]
    line = jnp.sum(jnp.where(found, tags[None, :, 1], 0), axis=(1, 2))
    source = jnp.sum(jnp.where(found[1:-1], loader, 0), axis=(1, 2)).astype(jnp.int32)
    flags = jnp.concatenate([line[1:-1] == line[:-2], line[1:-1] == line[2:]]).astype(jnp.int32)

    full_in = gather_weights(w_in, core)
    normed, both_normed, lin, gate, glu = forward(arrived, source, gain, full_in, panels, 2 * LANES)
    other_normed = lax.ppermute(normed, "tm", flip_bit("tm", 0))
    glu_low, glu_high = edges(glu, RIM)

    lane_block = 2 * LANES
    column = lambda height: pl.BlockSpec((height, lane_block), lambda j, idx: (0, j))
    sizes = dict(panels=panels, length=length, taps=taps)
    padded_of = lambda lanes: pltpu.VMEM((lanes // LANES, panels, length + 2 * RIM, LANES), F32)
    grad_depth = pl.pallas_call(
        functools.partial(depth_body, **sizes),
        grid_spec=pltpu.PrefetchScalarGridSpec(
            num_scalar_prefetch=1,
            grid=(width // lane_block,),
            in_specs=[column(rows), column(RIM), column(RIM), column(rows), column(taps)],
            out_specs=column(rows),
            scratch_shapes=[padded_of(lane_block)],
        ),
        out_shape=jax.ShapeDtypeStruct((rows, width), BF),
        compiler_params=params(1),
        name="depth",
    )(flags, glu, glu_low, glu_high, upstream.reshape(rows, width), kernel)
    grad_low, grad_high = edges(grad_depth, RIM)
    kernel_term = pl.pallas_call(
        functools.partial(taps_body, **sizes),
        grid_spec=pltpu.PrefetchScalarGridSpec(
            num_scalar_prefetch=1,
            grid=(width // lane_block,),
            in_specs=[column(rows), column(RIM), column(RIM), column(rows)],
            out_specs=column(taps + 1),
            scratch_shapes=[padded_of(lane_block), pltpu.VMEM((taps + 1, 8, LANES), F32)],
        ),
        out_shape=jax.ShapeDtypeStruct((taps + 1, width), F32),
        compiler_params=params(1),
        name="taps",
    )(flags, glu, glu_low, glu_high, grad_depth)

    piece = 2 * width // owners
    arguments = (flags, grad_depth, grad_low, grad_high, lin, gate, kernel)
    if piece % LANES == 0:
        give = gated(*arguments, piece, 2, 1 - core, sizes)
        others = [lax.ppermute(g, "tm", flip_bit("tm", 0)) for g in give]
        *own, first, second = gated(*arguments, piece, 2, core, sizes, True)
        gradients, run = (*own, *give), piece
        join = lambda base, other: lax.dynamic_update_slice(base, other, (rows, 0))
        mine = (first, second)
    else:
        gradients, run = tuple(gated(*arguments, lane_block, 1, 0, sizes)), width
        pick_parity = lambda values, parity: lax.dynamic_index_in_dim(
            values.reshape(rows, owners // 4, 2, piece), parity, 2, keepdims=False
        ).reshape(rows, width // 2)
        give = [pick_parity(g, 1 - core) for g in gradients]
        others = [lax.ppermute(g, "tm", flip_bit("tm", 0)) for g in give]
        mine = [pick_parity(g, core) for g in gradients]
        join = lambda base, other: jnp.concatenate([base, other], axis=0)
    both_normed = lax.dynamic_update_slice(both_normed, other_normed, (rows, 0))
    grad_slots, gain_term = back(
        gradients, core, full_in, arrived, source, upstream, gain, run, 2 * LANES
    )
    returned = lax.all_to_all(grad_slots, "tm", split_axis=0, concat_axis=0, tiled=True)
    count = lax.axis_size("dp")
    bits = bits_of(count)
    shares = []
    for side, order in ((0, bits), (1, bits[::-1])):
        term = outer_sum(both_normed, join(mine[side], others[side]))
        shares.append(halve(term.reshape(count, width // count, -1), order))
    share = jnp.concatenate(shares, axis=1)
    share = share.reshape(width // count, owners // 2, piece).transpose(1, 0, 2)
    shard_in = sum_across(share)
    grad_loaded = pick_panels(returned, owner_of.astype(jnp.int32), panels)
    sums = sum_everywhere(jnp.concatenate([kernel_term[:taps], gain_term], axis=0))
    return (grad_loaded[None, None], shard_in, sums[:taps], sums[taps])


def solution(mesh):
    in_specs = (
        P("dp", "tm", None, None, None),
        P("dp", "tm", None),
        P("dp", "tm", None),
        P(),
        P("dp", None),
        P(),
        P("dp", "tm", None, None, None),
    )
    out_specs = (P("dp", "tm", None, None, None), P("dp", "tm"), P(), P())
    return jax.shard_map(local, mesh=mesh, in_specs=in_specs, out_specs=out_specs, check_vma=False)
```

```python
import functools

import jax
import jax.numpy as jnp
from jax import lax
from jax.experimental import pallas as pl
from jax.experimental.pallas import tpu as pltpu
from jax.sharding import PartitionSpec as P

BF = jnp.bfloat16
F32 = jnp.float32
RIM = 16
LANES = 128
TILE = 32


def params(count, mib=48):
    return pltpu.CompilerParams(
        dimension_semantics=("arbitrary",) * count, vmem_limit_bytes=mib << 20
    )


def flip(axis, mask):
    return [(i, i ^ mask) for i in range(lax.axis_size(axis))]


def flip_bit(axis, bit):
    return flip(axis, 1 << bit)


def bits_of(count):
    bits = count.bit_length() - 1
    assert 1 << bits == count
    return list(range(bits))


def pick_body(index, source, target, sems, *, count):
    copies = [
        pltpu.make_async_copy(source.at[index[i]], target.at[i], sems.at[i]) for i in range(count)
    ]
    for copy in copies:
        copy.start()
    for copy in copies:
        copy.wait()


def pick_panels(source, index, count):
    _, rows, width = source.shape
    hbm = pl.BlockSpec(memory_space=pl.ANY)
    return pl.pallas_call(
        functools.partial(pick_body, count=count),
        grid_spec=pltpu.PrefetchScalarGridSpec(
            num_scalar_prefetch=1,
            grid=(1,),
            in_specs=[hbm],
            out_specs=hbm,
            scratch_shapes=[pltpu.SemaphoreType.DMA((count,))],
        ),
        out_shape=jax.ShapeDtypeStruct((count, rows, width), source.dtype),
        compiler_params=params(1),
        name="pick_panels",
    )(index, source)


def gather_order(block, order):
    have = block[None]
    relative = [0]
    for bit in order:
        got = lax.ppermute(have, "dp", flip_bit("dp", bit))
        have = jnp.concatenate([have, got], axis=0)
        relative = relative + [r ^ (1 << bit) for r in relative]
    return have, relative


def gather_weights(w_in, core):
    shard, width = w_in.shape
    quarter = shard // 4
    count = lax.axis_size("dp")
    place = lax.axis_index("dp")
    bits = bits_of(count)
    half = lax.dynamic_slice_in_dim(w_in, core * (2 * quarter), 2 * quarter, axis=0)
    first, first_rel = gather_order(half[:quarter], bits)
    second, second_rel = gather_order(half[quarter:], bits[::-1])
    other_first = lax.ppermute(first, "tm", flip_bit("tm", 0))
    other_second = lax.ppermute(second, "tm", flip_bit("tm", 0))
    rels = [first_rel, second_rel]

    def out_index(side):
        index = []
        for source in range(2):
            for position in range(count):
                index.append(((place ^ rels[source][position]) * 2 + side) * 2 + source)
        return jnp.stack(index).astype(jnp.int32)

    def body(_, a, b, *rest):
        target = rest[-1]
        for number, ref in enumerate((a, b)):

            @pl.when(pl.program_id(0) == number)
            def _():
                target[...] = ref[...]

    def spec(number):
        def index(source, position, _):
            last = count - 1 if number == 0 else 0
            return (jnp.where(source == number, position, last), 0, 0)

        return pl.BlockSpec((1, quarter, width), index)

    def put(side, pair, *base):
        return pl.pallas_call(
            body,
            grid_spec=pltpu.PrefetchScalarGridSpec(
                num_scalar_prefetch=1,
                grid=(2, count),
                in_specs=[spec(0), spec(1)] + [pl.BlockSpec(memory_space=pl.ANY) for _ in base],
                out_specs=pl.BlockSpec(
                    (1, quarter, width),
                    lambda source, position, idx: (idx[source * count + position], 0, 0),
                ),
            ),
            out_shape=jax.ShapeDtypeStruct((4 * count, quarter, width), w_in.dtype),
            input_output_aliases={3: 0} if base else {},
            compiler_params=params(2),
            name="put_weights",
        )(out_index(side), *pair, *base)

    full = put(core, (first, second))
    full = put(1 - core, (other_first, other_second), full)
    return full.reshape(4 * quarter * count, width)


def forward_body(source, x_hbm, gain_ref, lin_w, gate_w, parts, lin_out, gate_out, glu_out, normed, xs, sems, *, panels):
    rows = xs.shape[1]

    def fetch(s):
        return pltpu.make_async_copy(x_hbm.at[source[s]], xs.at[s], sems.at[s])

    @pl.when(pl.program_id(0) == 0)
    def _():
        for s in range(panels):
            fetch(s).start()
        for s in range(panels):
            fetch(s).wait()

            x = xs[s].astype(F32)
            x = x - jnp.mean(x, axis=1, keepdims=True)
            scale = lax.rsqrt(jnp.mean(x * x, axis=1, keepdims=True) + 1e-05)
            normed[s * rows : (s + 1) * rows, :] = (x * scale * gain_ref[...]).astype(BF)

        count, _, shard = parts.shape
        for block in range(count):
            parts[block ^ source[panels]] = normed[:, block * shard : (block + 1) * shard]

    lin = jnp.dot(normed[...], lin_w[...], preferred_element_type=F32)
    lin_out[...] = lin
    gate = jnp.dot(normed[...], gate_w[...], preferred_element_type=F32)
    gate_out[...] = gate
    glu_out[...] = (lin * jax.nn.sigmoid(gate)).astype(BF)


def forward(arrived, source, gain, full_in, panels, block):
    _, rows, width = arrived.shape
    blocks = width // block
    column = pl.BlockSpec((panels * rows, block), lambda j, idx: (0, j))
    wide = lambda dtype: jax.ShapeDtypeStruct((panels * rows, width), dtype)
    count = lax.axis_size("dp")
    parts = jax.ShapeDtypeStruct((count, panels * rows, width // count), BF)
    return pl.pallas_call(
        functools.partial(forward_body, panels=panels),
        grid_spec=pltpu.PrefetchScalarGridSpec(
            num_scalar_prefetch=1,
            grid=(blocks,),
            in_specs=[
                pl.BlockSpec(memory_space=pl.ANY),
                pl.BlockSpec((1, width), lambda j, idx: (0, 0)),
                pl.BlockSpec((width, block), lambda j, idx: (0, j)),
                pl.BlockSpec((width, block), lambda j, idx: (0, blocks + j)),
            ],
            out_specs=[
                pl.BlockSpec(parts.shape, lambda j, idx: (0, 0, 0)),
                column,
                column,
                column,
            ],
            scratch_shapes=[
                pltpu.VMEM((panels * rows, width), BF),
                pltpu.VMEM((panels, rows, width), BF),
                pltpu.SemaphoreType.DMA((panels,)),
            ],
        ),
        out_shape=[parts, wide(F32), wide(F32), wide(BF)],
        compiler_params=params(1),
        name="forward",
    )(jnp.append(source, lax.axis_index("dp")), arrived, gain.reshape(1, width), full_in, full_in)


def fill_padded(flags, padded, main, low, high, panels, length):
    for s in range(panels):
        at = s * length
        middle = main[at : at + length, :].astype(F32)
        before = low[low.shape[0] - RIM :, :] if s == 0 else main[at - RIM : at, :]
        after = high[:RIM, :] if s == panels - 1 else main[at + length : at + length + RIM, :]
        before = jnp.where(flags[s] > 0, before.astype(F32), 0.0)
        after = jnp.where(flags[panels + s] > 0, after.astype(F32), 0.0)
        for chunk in range(main.shape[1] // LANES):
            lanes = slice(chunk * LANES, (chunk + 1) * LANES)
            padded[chunk, s, RIM : RIM + length, :] = middle[:, lanes]
            padded[chunk, s, 0:RIM, :] = before[:, lanes]
            padded[chunk, s, RIM + length :, :] = after[:, lanes]


def shifted_sum(padded, weights, chunk, s, start, taps, flip, height=TILE):
    lanes = pl.ds(chunk * LANES, LANES)
    total = jnp.zeros((height, LANES), F32)
    for tap in range(taps):
        offset = taps - tap if flip else tap + 1
        view = padded[chunk, s, pl.ds(start + offset, height), :]
        total = total + weights[pl.ds(tap, 1), lanes] * view
    return total


def tiles(width, panels, length, work):
    for chunk in range(width // LANES):

        def step(s, carry):
            for start in range(0, length, TILE):
                rows = pl.ds(pl.multiple_of(s * length + start, TILE), TILE)
                work(chunk, s, start, rows, pl.ds(chunk * LANES, LANES))
            return carry

        lax.fori_loop(0, panels, step, 0)


def depth_body(
    flags, glu, low, high, upstream, up_low, up_high, weights, out, out_low, out_high, padded, ends, *, panels, length, taps
):
    fill_padded(flags, padded, glu, low, high, panels, length)
    rows = panels * length

    def grad(depth, up):
        sig = jax.nn.sigmoid(depth)
        return (up.astype(F32) * sig * (1.0 + depth * (1.0 - sig))).astype(BF)

    for chunk in range(glu.shape[1] // LANES):
        lanes = slice(chunk * LANES, (chunk + 1) * LANES)
        ends[chunk, 0, 0 : 2 * RIM, :] = low[:, lanes].astype(F32)
        ends[chunk, 0, 2 * RIM :, :] = glu[0:RIM, lanes].astype(F32)
        ends[chunk, 1, 0:RIM, :] = glu[rows - RIM : rows, lanes].astype(F32)
        ends[chunk, 1, RIM:, :] = high[:, lanes].astype(F32)
        for side, up, to in ((0, up_low, out_low), (1, up_high, out_high)):
            depth = shifted_sum(ends, weights, chunk, side, 0, taps, False, RIM)
            to[:, lanes] = grad(depth, up[:, lanes])

    def work(chunk, s, start, at, lanes):
        depth = shifted_sum(padded, weights, chunk, s, start, taps, False)
        out[at, lanes] = grad(depth, upstream[at, lanes])

    tiles(glu.shape[1], panels, length, work)


def taps_body(flags, glu, low, high, grad, out, padded, partial, *, panels, length, taps):
    fill_padded(flags, padded, glu, low, high, panels, length)
    for chunk in range(glu.shape[1] // LANES):
        lanes = pl.ds(chunk * LANES, LANES)
        partial[...] = jnp.zeros_like(partial)

        def step(s, carry):
            rows = pl.ds(pl.multiple_of(s * length, length), length)
            g = grad[rows, lanes].astype(F32)
            for tap in range(taps):
                product = g * padded[chunk, s, pl.ds(tap + 1, length), :]
                partial[tap] += jnp.sum(product.reshape(length // 8, 8, LANES), axis=0)
            return carry

        lax.fori_loop(0, panels, step, 0)
        out[:, lanes] = jnp.sum(partial[...], axis=1)


def gated_body(flags, grad, low, high, lin, gate, weights, *refs, panels, length, taps):
    *outs, padded = refs
    fill_padded(flags, padded, grad, low, high, panels, length)

    def work(chunk, s, start, rows, lanes):
        total = shifted_sum(padded, weights, chunk, s, start, taps, True)
        sig = jax.nn.sigmoid(gate[rows, lanes])
        scaled = total * sig
        outs[0][rows, lanes] = scaled.astype(BF)
        outs[1][rows, lanes] = (scaled * lin[rows, lanes] * (1.0 - sig)).astype(BF)

    tiles(grad.shape[1], panels, length, work)


def gated(flags, grad_depth, low, high, lin, gate, kernel, block, parities, parity, sizes):
    rows, width = grad_depth.shape
    panels = sizes["panels"]
    column = lambda height: pl.BlockSpec((height, block), lambda j, idx: (0, j * parities + idx[2 * panels]))
    shapes = [jax.ShapeDtypeStruct((rows, width // parities), BF)] * 2
    return pl.pallas_call(
        functools.partial(gated_body, **sizes),
        grid_spec=pltpu.PrefetchScalarGridSpec(
            num_scalar_prefetch=1,
            grid=(width // block // parities,),
            in_specs=[column(h) for h in (rows, RIM, RIM, rows, rows, kernel.shape[0])],
            out_specs=[pl.BlockSpec((rows, block), lambda j, idx: (0, j)) for _ in shapes],
            scratch_shapes=[
                pltpu.VMEM((block // LANES, panels, sizes["length"] + 2 * RIM, LANES), F32)
            ],
        ),
        out_shape=shapes,
        compiler_params=params(1),
        name="gated",
    )(jnp.append(flags, parity), grad_depth, low, high, lin, gate, kernel)


def back_body(source, *refs, grads, block, panels, piece):
    gradients = refs[:grads]
    w_ref, x_hbm, up_hbm, gain_ref, out_hbm, gain_out, total, xs, ups, outs, sems = refs[grads:]
    step = pl.program_id(0)

    def fetch(s):
        return (
            pltpu.make_async_copy(x_hbm.at[source[s]], xs.at[s], sems.at[s]),
            pltpu.make_async_copy(up_hbm.at[s], ups.at[s], sems.at[panels + s]),
        )

    def put(s):
        return pltpu.make_async_copy(outs.at[s], out_hbm.at[source[s]], sems.at[2 * panels + s])

    @pl.when(step == 0)
    def _():
        for s in range(panels):
            for copy in fetch(s):
                copy.start()

    acc = None
    for number, grad in enumerate(gradients):
        pieces = grad.shape[1] // piece
        for i in range(pieces):
            column = (number % 2 * pieces + i) * (grads // 2) * piece
            if grads > 2:
                column = column + (source[panels] ^ (number // 2)) * piece
                column = pl.multiple_of(column, LANES)
            term = lax.dot_general(
                grad[:, i * piece : (i + 1) * piece],
                w_ref[:, pl.ds(column, piece)],
                (((1,), (1,)), ((), ())),
                preferred_element_type=F32,
            )
            acc = term if acc is None else acc + term
    total[:, pl.ds(pl.multiple_of(step * block, block), block)] = acc

    @pl.when(step == pl.num_programs(0) - 1)
    def _():
        rows = xs.shape[1]
        gain = gain_ref[...]
        gain_sum = jnp.zeros_like(gain)
        for s in range(panels):
            for copy in fetch(s):
                copy.wait()

            x = xs[s].astype(F32)
            x = x - jnp.mean(x, axis=1, keepdims=True)
            scale = lax.rsqrt(jnp.mean(x * x, axis=1, keepdims=True) + 1e-05)
            unit = x * scale
            g = total[s * rows : (s + 1) * rows, :]
            gain_sum = gain_sum + jnp.sum(g * unit, axis=0, keepdims=True)
            q = g * gain
            mean_q = jnp.mean(q, axis=1, keepdims=True)
            mean_u = jnp.mean(q * unit, axis=1, keepdims=True)
            outs[s] = (ups[s].astype(F32) + scale * (q - mean_q - unit * mean_u)).astype(BF)
            put(s).start()
        gain_out[...] = gain_sum
        for s in range(panels):
            put(s).wait()


def back(gradients, core, full_in, arrived, source, upstream, gain, piece, block):
    _, rows, width = arrived.shape
    panels = upstream.shape[0]
    constant = lambda rank: (lambda n, idx: (0,) * rank)
    hbm = pl.BlockSpec(memory_space=pl.ANY)
    panel_scratch = pltpu.VMEM((panels, rows, width), BF)
    return pl.pallas_call(
        functools.partial(back_body, grads=len(gradients), block=block, panels=panels, piece=piece),
        grid_spec=pltpu.PrefetchScalarGridSpec(
            num_scalar_prefetch=1,
            grid=(width // block,),
            in_specs=[pl.BlockSpec(g.shape, constant(2)) for g in gradients]
            + [
                pl.BlockSpec((block, full_in.shape[1]), lambda n, idx: (n, 0)),
                hbm,
                hbm,
                pl.BlockSpec((1, width), constant(2)),
            ],
            out_specs=[hbm, pl.BlockSpec((1, width), constant(2))],
            scratch_shapes=[
                pltpu.VMEM((panels * rows, width), F32),
                panel_scratch,
                panel_scratch,
                panel_scratch,
                pltpu.SemaphoreType.DMA((3 * panels,)),
            ],
        ),
        out_shape=[
            jax.ShapeDtypeStruct(arrived.shape, BF),
            jax.ShapeDtypeStruct((1, width), F32),
        ],
        compiler_params=params(1),
        name="back",
    )(jnp.append(source, core), *gradients, full_in, arrived, upstream, gain.reshape(1, width))


def outer_sum(lefts, rights):
    terms = [
        lax.dot_general(a, b, (((1,), (0,)), ((), ())), preferred_element_type=F32)
        for a, b in zip(lefts, rights)
    ]
    return (terms[0] + terms[1]).astype(BF)


def outer_halved(lefts, rights, order):
    count = lefts[0].shape[0]
    rels = sorted(range(count), key=lambda r: [(r >> bit) & 1 for bit in order])
    if rels != list(range(count)):
        lefts = [jnp.concatenate([left[r : r + 1] for r in rels]) for left in lefts]
    half = count // 2
    send = outer_sum([left[half:] for left in lefts], rights)
    keep = outer_sum([left[:half] for left in lefts], rights)
    for bit in order:
        got = lax.ppermute(send, "dp", flip_bit("dp", bit))
        half = half // 2
        add = lambda a, b: (a.astype(F32) + b.astype(F32)).astype(BF)
        if half:
            send = add(keep[half:], got[half:])
            keep = add(keep[:half], got[:half])
        else:
            keep = add(keep, got)
    return keep[0]


def sum_everywhere(values):
    steps = [("dp", bit) for bit in bits_of(lax.axis_size("dp"))] + [("tm", 0)]
    pad = -values.shape[0] % (1 << len(steps))
    rows = values.shape[0]
    values = jnp.pad(values, ((0, pad), (0, 0)))
    side = lambda axis, bit: (lax.axis_index(axis) >> bit) & 1
    for axis, bit in steps:
        halves = values.reshape(2, values.shape[0] // 2, values.shape[1])
        mine = side(axis, bit)
        send = lax.dynamic_index_in_dim(halves, 1 - mine, 0, keepdims=False)
        keep = lax.dynamic_index_in_dim(halves, mine, 0, keepdims=False)
        values = keep + lax.ppermute(send, axis, flip_bit(axis, bit))
    terms = [values]
    for mask in range(2, lax.axis_size("tm"), 2):
        terms.append(lax.ppermute(values, "tm", flip("tm", mask)))
    while len(terms) > 1:
        terms = [a + b for a, b in zip(terms[::2], terms[1::2])]
    values = terms[0]
    for axis, bit in steps[::-1]:
        got = lax.ppermute(values, axis, flip_bit(axis, bit))
        first = side(axis, bit) == 0
        values = jnp.concatenate([jnp.where(first, values, got), jnp.where(first, got, values)])
    return values[:rows]


def sum_across(share):
    count = share.shape[0]
    place = lax.axis_index("tm") // 2
    total = lax.dynamic_index_in_dim(share, place, 0, keepdims=False).astype(F32)
    for turn in range(1, count):
        piece = lax.dynamic_index_in_dim(share, place ^ turn, 0, keepdims=False)
        pairs = [(i, i ^ (2 * turn)) for i in range(2 * count)]
        total = total + lax.ppermute(piece, "tm", pairs).astype(F32)
    return total


def edges(values, width):
    count = lax.axis_size("tm")
    low = lax.ppermute(values[-width:], "tm", [(i, i + 1) for i in range(count - 1)])
    high = lax.ppermute(values[:width], "tm", [(i + 1, i) for i in range(count - 1)])
    return low, high


def local(frames, route, utterance, gain, w_in, kernel, cotangent):
    panels, length, width = frames.shape[2:]
    owners = lax.axis_size("tm")
    rows = panels * length
    taps = kernel.shape[0]
    reach = taps // 2
    assert reach < RIM and taps == 31
    loaded = frames[0, 0]
    target = route[0, 0]
    labels = utterance[0, 0]
    upstream = cotangent[0, 0]
    core = lax.axis_index("tm") % 2
    owner_of = target // panels
    pick = owner_of[None, :] == jnp.arange(owners, dtype=jnp.int32)[:, None]
    panel_of = jnp.sum(jnp.where(pick, jnp.arange(panels, dtype=jnp.int32)[None, :], 0), axis=1)
    outgoing = pick_panels(loaded, panel_of.astype(jnp.int32), owners)
    arrived = lax.all_to_all(outgoing, "tm", split_axis=0, concat_axis=0, tiled=True)
    me = lax.axis_index("tm")
    tags = jnp.stack([target, labels + 1])[None]
    tags = jnp.concatenate([tags, lax.ppermute(tags, "tm", flip_bit("tm", 0))])
    rest = [lax.ppermute(tags, "tm", flip("tm", i)) for i in range(2, owners, 2)]
    tags = jnp.concatenate([tags] + rest)
    loader = (jnp.arange(owners, dtype=jnp.int32) ^ me)[None, :, None]
    position = me * panels - 1 + jnp.arange(panels + 2, dtype=jnp.int32)
    found = tags[None, :, 0] == position[:, None, None]
    line = jnp.sum(jnp.where(found, tags[None, :, 1], 0), axis=(1, 2))
    source = jnp.sum(jnp.where(found[1:-1], loader, 0), axis=(1, 2)).astype(jnp.int32)
    flags = jnp.concatenate([line[1:-1] == line[:-2], line[1:-1] == line[2:]]).astype(jnp.int32)

    full_in = gather_weights(w_in, core)
    normed, lin, gate, glu = forward(arrived, source, gain, full_in, panels, 4 * LANES)
    other_normed = lax.ppermute(normed, "tm", flip_bit("tm", 0))
    glu_low, glu_high = edges(glu, 2 * RIM)

    lane_block = 2 * LANES
    column = lambda height: pl.BlockSpec((height, lane_block), lambda j, idx: (0, j))
    sizes = dict(panels=panels, length=length, taps=taps)
    padded_of = lambda lanes: pltpu.VMEM((lanes // LANES, panels, length + 2 * RIM, LANES), F32)
    up_rows = upstream.reshape(rows, width)
    up_low, up_high = edges(up_rows, RIM)
    grad_depth, grad_low, grad_high = pl.pallas_call(
        functools.partial(depth_body, **sizes),
        grid_spec=pltpu.PrefetchScalarGridSpec(
            num_scalar_prefetch=1,
            grid=(width // lane_block,),
            in_specs=[column(h) for h in (rows, 2 * RIM, 2 * RIM, rows, RIM, RIM, taps)],
            out_specs=[column(rows), column(RIM), column(RIM)],
            scratch_shapes=[
                padded_of(lane_block),
                pltpu.VMEM((lane_block // LANES, 2, 3 * RIM, LANES), F32),
            ],
        ),
        out_shape=[jax.ShapeDtypeStruct((h, width), BF) for h in (rows, RIM, RIM)],
        compiler_params=params(1),
        name="depth",
    )(flags, glu, glu_low, glu_high, up_rows, up_low, up_high, kernel)
    kernel_term = pl.pallas_call(
        functools.partial(taps_body, **sizes),
        grid_spec=pltpu.PrefetchScalarGridSpec(
            num_scalar_prefetch=1,
            grid=(width // lane_block,),
            in_specs=[column(h) for h in (rows, 2 * RIM, 2 * RIM, rows)],
            out_specs=column(taps + 1),
            scratch_shapes=[padded_of(lane_block), pltpu.VMEM((taps + 1, 8, LANES), F32)],
        ),
        out_shape=jax.ShapeDtypeStruct((taps + 1, width), F32),
        compiler_params=params(1),
        name="taps",
    )(flags, glu, glu_low, glu_high, grad_depth)

    piece = 2 * width // owners
    arguments = (flags, grad_depth, grad_low, grad_high, lin, gate, kernel)
    if piece % LANES == 0:
        give = gated(*arguments, piece, 2, 1 - core, sizes)
        others = [lax.ppermute(g, "tm", flip_bit("tm", 0)) for g in give]
        own = gated(*arguments, piece, 2, core, sizes)
        gradients, run = (*own, *give), piece
    else:
        gradients, run = tuple(gated(*arguments, lane_block, 1, 0, sizes)), width
        pick_parity = lambda values, parity: lax.dynamic_index_in_dim(
            values.reshape(rows, owners // 4, 2, piece), parity, 2, keepdims=False
        ).reshape(rows, width // 2)
        give = [pick_parity(g, 1 - core) for g in gradients]
        others = [lax.ppermute(g, "tm", flip_bit("tm", 0)) for g in give]
        own = [pick_parity(g, core) for g in gradients]
    grad_slots, gain_term = back(
        gradients, core, full_in, arrived, source, upstream, gain, run, 2 * LANES
    )
    returned = lax.all_to_all(grad_slots, "tm", split_axis=0, concat_axis=0, tiled=True)
    count = lax.axis_size("dp")
    bits = bits_of(count)
    shares = [
        outer_halved((normed, other_normed), (own[side], others[side]), order)
        for side, order in ((0, bits), (1, bits[::-1]))
    ]
    share = jnp.concatenate(shares, axis=1)
    share = share.reshape(width // count, owners // 2, piece).transpose(1, 0, 2)
    shard_in = sum_across(share)
    grad_loaded = pick_panels(returned, owner_of.astype(jnp.int32), panels)
    sums = sum_everywhere(jnp.concatenate([kernel_term[:taps], gain_term], axis=0))
    return (grad_loaded[None, None], shard_in, sums[:taps], sums[taps])


def solution(mesh):
    in_specs = (
        P("dp", "tm", None, None, None),
        P("dp", "tm", None),
        P("dp", "tm", None),
        P(),
        P("dp", None),
        P(),
        P("dp", "tm", None, None, None),
    )
    out_specs = (P("dp", "tm", None, None, None), P("dp", "tm"), P(), P())
    return jax.shard_map(local, mesh=mesh, in_specs=in_specs, out_specs=out_specs, check_vma=False)
```

```python
import functools

import jax
import jax.numpy as jnp
from jax import lax
from jax.experimental import pallas as pl
from jax.experimental.pallas import tpu as pltpu
from jax.sharding import PartitionSpec as P

BF = jnp.bfloat16
F32 = jnp.float32
RIM = 16
LANES = 128
TILE = 32


def params(count, mib=48):
    return pltpu.CompilerParams(
        dimension_semantics=("arbitrary",) * count, vmem_limit_bytes=mib << 20
    )


def flip(axis, mask):
    return [(i, i ^ mask) for i in range(lax.axis_size(axis))]


def flip_bit(axis, bit):
    return flip(axis, 1 << bit)


def bits_of(count):
    bits = count.bit_length() - 1
    assert 1 << bits == count
    return list(range(bits))


def pick_body(index, source, target, sems, *, count):
    copies = [
        pltpu.make_async_copy(source.at[index[i]], target.at[i], sems.at[i]) for i in range(count)
    ]
    for copy in copies:
        copy.start()
    for copy in copies:
        copy.wait()


def pick_panels(source, index, count):
    _, rows, width = source.shape
    hbm = pl.BlockSpec(memory_space=pl.ANY)
    return pl.pallas_call(
        functools.partial(pick_body, count=count),
        grid_spec=pltpu.PrefetchScalarGridSpec(
            num_scalar_prefetch=1,
            grid=(1,),
            in_specs=[hbm],
            out_specs=hbm,
            scratch_shapes=[pltpu.SemaphoreType.DMA((count,))],
        ),
        out_shape=jax.ShapeDtypeStruct((count, rows, width), source.dtype),
        compiler_params=params(1),
        name="pick_panels",
    )(index, source)


def copy_body(_, source, target):
    target[...] = source[...]


def pick_blocks(source, index, count):
    _, rows, width = source.shape
    return pl.pallas_call(
        copy_body,
        grid_spec=pltpu.PrefetchScalarGridSpec(
            num_scalar_prefetch=1,
            grid=(count,),
            in_specs=[pl.BlockSpec((1, rows, width), lambda i, idx: (idx[i], 0, 0))],
            out_specs=pl.BlockSpec((1, rows, width), lambda i, idx: (i, 0, 0)),
        ),
        out_shape=jax.ShapeDtypeStruct((count, rows, width), source.dtype),
        compiler_params=params(1),
        name="pick_blocks",
    )(index, source)


def gather_order(block, order):
    have = block[None]
    relative = [0]
    for bit in order:
        got = lax.ppermute(have, "dp", flip_bit("dp", bit))
        have = jnp.concatenate([have, got], axis=0)
        relative = relative + [r ^ (1 << bit) for r in relative]
    return have, relative


def gather_weights(w_in, core):
    shard, width = w_in.shape
    quarter = shard // 4
    count = lax.axis_size("dp")
    place = lax.axis_index("dp")
    bits = bits_of(count)
    half = lax.dynamic_slice_in_dim(w_in, core * (2 * quarter), 2 * quarter, axis=0)
    first, first_rel = gather_order(half[:quarter], bits)
    second, second_rel = gather_order(half[quarter:], bits[::-1])
    other_first = lax.ppermute(first, "tm", flip_bit("tm", 0))
    other_second = lax.ppermute(second, "tm", flip_bit("tm", 0))
    rels = [first_rel, second_rel]

    def out_index(side):
        index = []
        for source in range(2):
            for position in range(count):
                index.append(((place ^ rels[source][position]) * 2 + side) * 2 + source)
        return jnp.stack(index).astype(jnp.int32)

    def body(_, a, b, *rest):
        target = rest[-1]
        for number, ref in enumerate((a, b)):

            @pl.when(pl.program_id(0) == number)
            def _():
                target[...] = ref[...]

    def spec(number):
        def index(source, position, _):
            last = count - 1 if number == 0 else 0
            return (jnp.where(source == number, position, last), 0, 0)

        return pl.BlockSpec((1, quarter, width), index)

    def put(side, pair, *base):
        return pl.pallas_call(
            body,
            grid_spec=pltpu.PrefetchScalarGridSpec(
                num_scalar_prefetch=1,
                grid=(2, count),
                in_specs=[spec(0), spec(1)] + [pl.BlockSpec(memory_space=pl.ANY) for _ in base],
                out_specs=pl.BlockSpec(
                    (1, quarter, width),
                    lambda source, position, idx: (idx[source * count + position], 0, 0),
                ),
            ),
            out_shape=jax.ShapeDtypeStruct((4 * count, quarter, width), w_in.dtype),
            input_output_aliases={3: 0} if base else {},
            compiler_params=params(2),
            name="put_weights",
        )(out_index(side), *pair, *base)

    full = put(core, (first, second))
    full = put(1 - core, (other_first, other_second), full)
    return full.reshape(4 * quarter * count, width)


def forward_body(source, x_hbm, gain_ref, lin_w, gate_w, parts, lin_out, gate_out, glu_out, normed, xs, sems, *, panels):
    rows = xs.shape[1]

    def fetch(s):
        return pltpu.make_async_copy(x_hbm.at[source[s]], xs.at[s], sems.at[s])

    @pl.when(pl.program_id(0) == 0)
    def _():
        for s in range(panels):
            fetch(s).start()
        for s in range(panels):
            fetch(s).wait()

            x = xs[s].astype(F32)
            x = x - jnp.mean(x, axis=1, keepdims=True)
            scale = lax.rsqrt(jnp.mean(x * x, axis=1, keepdims=True) + 1e-05)
            normed[s * rows : (s + 1) * rows, :] = (x * scale * gain_ref[...]).astype(BF)

        count, _, shard = parts.shape
        for block in range(count):
            parts[block ^ source[panels]] = normed[:, block * shard : (block + 1) * shard]

    lin = jnp.dot(normed[...], lin_w[...], preferred_element_type=F32)
    lin_out[...] = lin
    gate = jnp.dot(normed[...], gate_w[...], preferred_element_type=F32)
    gate_out[...] = gate
    glu_out[...] = (lin * jax.nn.sigmoid(gate)).astype(BF)


def forward(arrived, source, gain, full_in, panels, block):
    _, rows, width = arrived.shape
    blocks = width // block
    column = pl.BlockSpec((panels * rows, block), lambda j, idx: (0, j))
    wide = lambda dtype: jax.ShapeDtypeStruct((panels * rows, width), dtype)
    count = lax.axis_size("dp")
    parts = jax.ShapeDtypeStruct((count, panels * rows, width // count), BF)
    return pl.pallas_call(
        functools.partial(forward_body, panels=panels),
        grid_spec=pltpu.PrefetchScalarGridSpec(
            num_scalar_prefetch=1,
            grid=(blocks,),
            in_specs=[
                pl.BlockSpec(memory_space=pl.ANY),
                pl.BlockSpec((1, width), lambda j, idx: (0, 0)),
                pl.BlockSpec((width, block), lambda j, idx: (0, j)),
                pl.BlockSpec((width, block), lambda j, idx: (0, blocks + j)),
            ],
            out_specs=[
                pl.BlockSpec(parts.shape, lambda j, idx: (0, 0, 0)),
                column,
                column,
                column,
            ],
            scratch_shapes=[
                pltpu.VMEM((panels * rows, width), BF),
                pltpu.VMEM((panels, rows, width), BF),
                pltpu.SemaphoreType.DMA((panels,)),
            ],
        ),
        out_shape=[parts, wide(F32), wide(F32), wide(BF)],
        compiler_params=params(1),
        name="forward",
    )(jnp.append(source, lax.axis_index("dp")), arrived, gain.reshape(1, width), full_in, full_in)


def fill_padded(flags, padded, main, low, high, panels, length):
    for s in range(panels):
        at = s * length
        middle = main[at : at + length, :].astype(F32)
        before = low[low.shape[0] - RIM :, :] if s == 0 else main[at - RIM : at, :]
        after = high[:RIM, :] if s == panels - 1 else main[at + length : at + length + RIM, :]
        before = jnp.where(flags[s] > 0, before.astype(F32), 0.0)
        after = jnp.where(flags[panels + s] > 0, after.astype(F32), 0.0)
        for chunk in range(main.shape[1] // LANES):
            lanes = slice(chunk * LANES, (chunk + 1) * LANES)
            padded[chunk, s, RIM : RIM + length, :] = middle[:, lanes]
            padded[chunk, s, 0:RIM, :] = before[:, lanes]
            padded[chunk, s, RIM + length :, :] = after[:, lanes]


def shifted_sum(padded, weights, chunk, s, start, taps, flip, height=TILE):
    lanes = pl.ds(chunk * LANES, LANES)
    total = jnp.zeros((height, LANES), F32)
    for tap in range(taps):
        offset = taps - tap if flip else tap + 1
        view = padded[chunk, s, pl.ds(start + offset, height), :]
        total = total + weights[pl.ds(tap, 1), lanes] * view
    return total


def tiles(width, panels, length, work):
    for chunk in range(width // LANES):

        def step(s, carry):
            for start in range(0, length, TILE):
                rows = pl.ds(pl.multiple_of(s * length + start, TILE), TILE)
                work(chunk, s, start, rows, pl.ds(chunk * LANES, LANES))
            return carry

        lax.fori_loop(0, panels, step, 0)


def depth_body(
    flags, glu, low, high, upstream, up_low, up_high, weights, out, out_low, out_high, padded, ends, *, panels, length, taps
):
    fill_padded(flags, padded, glu, low, high, panels, length)
    rows = panels * length

    def grad(depth, up):
        sig = jax.nn.sigmoid(depth)
        return (up.astype(F32) * sig * (1.0 + depth * (1.0 - sig))).astype(BF)

    for chunk in range(glu.shape[1] // LANES):
        lanes = slice(chunk * LANES, (chunk + 1) * LANES)
        ends[chunk, 0, 0 : 2 * RIM, :] = low[:, lanes].astype(F32)
        ends[chunk, 0, 2 * RIM :, :] = glu[0:RIM, lanes].astype(F32)
        ends[chunk, 1, 0:RIM, :] = glu[rows - RIM : rows, lanes].astype(F32)
        ends[chunk, 1, RIM:, :] = high[:, lanes].astype(F32)
        for side, up, to in ((0, up_low, out_low), (1, up_high, out_high)):
            depth = shifted_sum(ends, weights, chunk, side, 0, taps, False, RIM)
            to[:, lanes] = grad(depth, up[:, lanes])

    def work(chunk, s, start, at, lanes):
        depth = shifted_sum(padded, weights, chunk, s, start, taps, False)
        out[at, lanes] = grad(depth, upstream[at, lanes])

    tiles(glu.shape[1], panels, length, work)


def taps_body(flags, glu, low, high, grad, out, padded, partial, *, panels, length, taps):
    fill_padded(flags, padded, glu, low, high, panels, length)
    for chunk in range(glu.shape[1] // LANES):
        lanes = pl.ds(chunk * LANES, LANES)
        partial[...] = jnp.zeros_like(partial)

        def step(s, carry):
            rows = pl.ds(pl.multiple_of(s * length, length), length)
            g = grad[rows, lanes].astype(F32)
            for tap in range(taps):
                product = g * padded[chunk, s, pl.ds(tap + 1, length), :]
                partial[tap] += jnp.sum(product.reshape(length // 8, 8, LANES), axis=0)
            return carry

        lax.fori_loop(0, panels, step, 0)
        out[:, lanes] = jnp.sum(partial[...], axis=1)


def gated_body(flags, grad, low, high, lin, gate, weights, *refs, panels, length, taps):
    *outs, padded = refs
    fill_padded(flags, padded, grad, low, high, panels, length)

    def work(chunk, s, start, rows, lanes):
        total = shifted_sum(padded, weights, chunk, s, start, taps, True)
        sig = jax.nn.sigmoid(gate[rows, lanes])
        scaled = total * sig
        outs[0][rows, lanes] = scaled.astype(BF)
        outs[1][rows, lanes] = (scaled * lin[rows, lanes] * (1.0 - sig)).astype(BF)

    tiles(grad.shape[1], panels, length, work)


def gated(flags, grad_depth, low, high, lin, gate, kernel, block, parities, parity, sizes):
    rows, width = grad_depth.shape
    panels = sizes["panels"]
    column = lambda height: pl.BlockSpec((height, block), lambda j, idx: (0, j * parities + idx[2 * panels]))
    shapes = [jax.ShapeDtypeStruct((rows, width // parities), BF)] * 2
    return pl.pallas_call(
        functools.partial(gated_body, **sizes),
        grid_spec=pltpu.PrefetchScalarGridSpec(
            num_scalar_prefetch=1,
            grid=(width // block // parities,),
            in_specs=[column(h) for h in (rows, RIM, RIM, rows, rows, kernel.shape[0])],
            out_specs=[pl.BlockSpec((rows, block), lambda j, idx: (0, j)) for _ in shapes],
            scratch_shapes=[
                pltpu.VMEM((block // LANES, panels, sizes["length"] + 2 * RIM, LANES), F32)
            ],
        ),
        out_shape=shapes,
        compiler_params=params(1),
        name="gated",
    )(jnp.append(flags, parity), grad_depth, low, high, lin, gate, kernel)


def back_body(source, *refs, grads, block, panels, piece):
    gradients = refs[:grads]
    w_ref, x_hbm, up_hbm, gain_ref, out_hbm, gain_out, total, xs, ups, outs, sems = refs[grads:]
    step = pl.program_id(0)

    def fetch(s):
        return (
            pltpu.make_async_copy(x_hbm.at[source[s]], xs.at[s], sems.at[s]),
            pltpu.make_async_copy(up_hbm.at[s], ups.at[s], sems.at[panels + s]),
        )

    def put(s):
        return pltpu.make_async_copy(outs.at[s], out_hbm.at[source[s]], sems.at[2 * panels + s])

    @pl.when(step == 0)
    def _():
        for s in range(panels):
            for copy in fetch(s):
                copy.start()

    acc = None
    for number, grad in enumerate(gradients):
        pieces = grad.shape[1] // piece
        for i in range(pieces):
            column = (number % 2 * pieces + i) * (grads // 2) * piece
            if grads > 2:
                column = column + (source[panels] ^ (number // 2)) * piece
                column = pl.multiple_of(column, LANES)
            term = lax.dot_general(
                grad[:, i * piece : (i + 1) * piece],
                w_ref[:, pl.ds(column, piece)],
                (((1,), (1,)), ((), ())),
                preferred_element_type=F32,
            )
            acc = term if acc is None else acc + term
    total[:, pl.ds(pl.multiple_of(step * block, block), block)] = acc

    @pl.when(step == pl.num_programs(0) - 1)
    def _():
        rows = xs.shape[1]
        gain = gain_ref[...]
        gain_sum = jnp.zeros_like(gain)
        for s in range(panels):
            for copy in fetch(s):
                copy.wait()

            x = xs[s].astype(F32)
            x = x - jnp.mean(x, axis=1, keepdims=True)
            scale = lax.rsqrt(jnp.mean(x * x, axis=1, keepdims=True) + 1e-05)
            unit = x * scale
            g = total[s * rows : (s + 1) * rows, :]
            gain_sum = gain_sum + jnp.sum(g * unit, axis=0, keepdims=True)
            q = g * gain
            mean_q = jnp.mean(q, axis=1, keepdims=True)
            mean_u = jnp.mean(q * unit, axis=1, keepdims=True)
            outs[s] = (ups[s].astype(F32) + scale * (q - mean_q - unit * mean_u)).astype(BF)
            put(s).start()
        gain_out[...] = gain_sum
        for s in range(panels):
            put(s).wait()


def back(gradients, core, full_in, arrived, source, upstream, gain, piece, block):
    _, rows, width = arrived.shape
    panels = upstream.shape[0]
    constant = lambda rank: (lambda n, idx: (0,) * rank)
    hbm = pl.BlockSpec(memory_space=pl.ANY)
    panel_scratch = pltpu.VMEM((panels, rows, width), BF)
    return pl.pallas_call(
        functools.partial(back_body, grads=len(gradients), block=block, panels=panels, piece=piece),
        grid_spec=pltpu.PrefetchScalarGridSpec(
            num_scalar_prefetch=1,
            grid=(width // block,),
            in_specs=[pl.BlockSpec(g.shape, constant(2)) for g in gradients]
            + [
                pl.BlockSpec((block, full_in.shape[1]), lambda n, idx: (n, 0)),
                hbm,
                hbm,
                pl.BlockSpec((1, width), constant(2)),
            ],
            out_specs=[hbm, pl.BlockSpec((1, width), constant(2))],
            scratch_shapes=[
                pltpu.VMEM((panels * rows, width), F32),
                panel_scratch,
                panel_scratch,
                panel_scratch,
                pltpu.SemaphoreType.DMA((3 * panels,)),
            ],
        ),
        out_shape=[
            jax.ShapeDtypeStruct(arrived.shape, BF),
            jax.ShapeDtypeStruct((1, width), F32),
        ],
        compiler_params=params(1),
        name="back",
    )(jnp.append(source, core), *gradients, full_in, arrived, upstream, gain.reshape(1, width))


def outer_sum(lefts, rights):
    terms = [
        lax.dot_general(a, b, (((1,), (0,)), ((), ())), preferred_element_type=F32)
        for a, b in zip(lefts, rights)
    ]
    return (terms[0] + terms[1]).astype(BF)


def outer_halved(lefts, rights, order):
    count = lefts[0].shape[0]
    rels = sorted(range(count), key=lambda r: [(r >> bit) & 1 for bit in order])
    half = count // 2
    pick = lambda left, some: jnp.concatenate([left[r : r + 1] for r in some])
    send = outer_sum([pick(left, rels[half:]) for left in lefts], rights)
    keep = outer_sum([pick(left, rels[:half]) for left in lefts], rights)
    add = lambda a, b: (a.astype(F32) + b.astype(F32)).astype(BF)
    for bit in order:
        got = lax.ppermute(send, "dp", flip_bit("dp", bit))
        half = half // 2
        if half:
            send = add(keep[half:], got[half:])
            keep = add(keep[:half], got[:half])
        else:
            keep = add(keep, got)
    return keep[0]


def sum_everywhere(values):
    steps = [("dp", bit) for bit in bits_of(lax.axis_size("dp"))] + [("tm", 0)]
    pad = -values.shape[0] % (1 << len(steps))
    rows = values.shape[0]
    values = jnp.pad(values, ((0, pad), (0, 0)))
    side = lambda axis, bit: (lax.axis_index(axis) >> bit) & 1
    for axis, bit in steps:
        halves = values.reshape(2, values.shape[0] // 2, values.shape[1])
        mine = side(axis, bit)
        send = lax.dynamic_index_in_dim(halves, 1 - mine, 0, keepdims=False)
        keep = lax.dynamic_index_in_dim(halves, mine, 0, keepdims=False)
        values = keep + lax.ppermute(send, axis, flip_bit(axis, bit))
    terms = [values]
    for mask in range(2, lax.axis_size("tm"), 2):
        terms.append(lax.ppermute(values, "tm", flip("tm", mask)))
    while len(terms) > 1:
        terms = [a + b for a, b in zip(terms[::2], terms[1::2])]
    values = terms[0]
    for axis, bit in steps[::-1]:
        got = lax.ppermute(values, axis, flip_bit(axis, bit))
        first = side(axis, bit) == 0
        values = jnp.concatenate([jnp.where(first, values, got), jnp.where(first, got, values)])
    return values[:rows]


def sum_across(share):
    count = share.shape[0]
    place = lax.axis_index("tm") // 2
    total = lax.dynamic_index_in_dim(share, place, 0, keepdims=False).astype(F32)
    for turn in range(1, count):
        piece = lax.dynamic_index_in_dim(share, place ^ turn, 0, keepdims=False)
        pairs = [(i, i ^ (2 * turn)) for i in range(2 * count)]
        total = total + lax.ppermute(piece, "tm", pairs).astype(F32)
    return total


def edges(values, width):
    count = lax.axis_size("tm")
    low = lax.ppermute(values[-width:], "tm", [(i, i + 1) for i in range(count - 1)])
    high = lax.ppermute(values[:width], "tm", [(i + 1, i) for i in range(count - 1)])
    return low, high


def local(frames, route, utterance, gain, w_in, kernel, cotangent):
    panels, length, width = frames.shape[2:]
    owners = lax.axis_size("tm")
    rows = panels * length
    taps = kernel.shape[0]
    reach = taps // 2
    assert reach < RIM and taps == 31
    loaded = frames[0, 0]
    target = route[0, 0]
    labels = utterance[0, 0]
    upstream = cotangent[0, 0]
    core = lax.axis_index("tm") % 2
    owner_of = target // panels
    pick = owner_of[None, :] == jnp.arange(owners, dtype=jnp.int32)[:, None]
    panel_of = jnp.sum(jnp.where(pick, jnp.arange(panels, dtype=jnp.int32)[None, :], 0), axis=1)
    outgoing = pick_panels(loaded, panel_of.astype(jnp.int32), owners)
    arrived = lax.all_to_all(outgoing, "tm", split_axis=0, concat_axis=0, tiled=True)
    me = lax.axis_index("tm")
    tags = jnp.stack([target, labels + 1])[None]
    tags = jnp.concatenate([tags, lax.ppermute(tags, "tm", flip_bit("tm", 0))])
    rest = [lax.ppermute(tags, "tm", flip("tm", i)) for i in range(2, owners, 2)]
    tags = jnp.concatenate([tags] + rest)
    loader = (jnp.arange(owners, dtype=jnp.int32) ^ me)[None, :, None]
    position = me * panels - 1 + jnp.arange(panels + 2, dtype=jnp.int32)
    found = tags[None, :, 0] == position[:, None, None]
    line = jnp.sum(jnp.where(found, tags[None, :, 1], 0), axis=(1, 2))
    source = jnp.sum(jnp.where(found[1:-1], loader, 0), axis=(1, 2)).astype(jnp.int32)
    flags = jnp.concatenate([line[1:-1] == line[:-2], line[1:-1] == line[2:]]).astype(jnp.int32)

    full_in = gather_weights(w_in, core)
    normed, lin, gate, glu = forward(arrived, source, gain, full_in, panels, 4 * LANES)
    other_normed = lax.ppermute(normed, "tm", flip_bit("tm", 0))
    glu_low, glu_high = edges(glu, 2 * RIM)

    lane_block = 2 * LANES
    column = lambda height: pl.BlockSpec((height, lane_block), lambda j, idx: (0, j))
    sizes = dict(panels=panels, length=length, taps=taps)
    padded_of = lambda lanes: pltpu.VMEM((lanes // LANES, panels, length + 2 * RIM, LANES), F32)
    up_rows = upstream.reshape(rows, width)
    up_low, up_high = edges(up_rows, RIM)
    grad_depth, grad_low, grad_high = pl.pallas_call(
        functools.partial(depth_body, **sizes),
        grid_spec=pltpu.PrefetchScalarGridSpec(
            num_scalar_prefetch=1,
            grid=(width // lane_block,),
            in_specs=[column(h) for h in (rows, 2 * RIM, 2 * RIM, rows, RIM, RIM, taps)],
            out_specs=[column(rows), column(RIM), column(RIM)],
            scratch_shapes=[
                padded_of(lane_block),
                pltpu.VMEM((lane_block // LANES, 2, 3 * RIM, LANES), F32),
            ],
        ),
        out_shape=[jax.ShapeDtypeStruct((h, width), BF) for h in (rows, RIM, RIM)],
        compiler_params=params(1),
        name="depth",
    )(flags, glu, glu_low, glu_high, up_rows, up_low, up_high, kernel)
    kernel_term = pl.pallas_call(
        functools.partial(taps_body, **sizes),
        grid_spec=pltpu.PrefetchScalarGridSpec(
            num_scalar_prefetch=1,
            grid=(width // lane_block,),
            in_specs=[column(h) for h in (rows, 2 * RIM, 2 * RIM, rows)],
            out_specs=column(taps + 1),
            scratch_shapes=[padded_of(lane_block), pltpu.VMEM((taps + 1, 8, LANES), F32)],
        ),
        out_shape=jax.ShapeDtypeStruct((taps + 1, width), F32),
        compiler_params=params(1),
        name="taps",
    )(flags, glu, glu_low, glu_high, grad_depth)

    piece = 2 * width // owners
    arguments = (flags, grad_depth, grad_low, grad_high, lin, gate, kernel)
    if piece % LANES == 0:
        give = gated(*arguments, piece, 2, 1 - core, sizes)
        others = [lax.ppermute(g, "tm", flip_bit("tm", 0)) for g in give]
        own = gated(*arguments, piece, 2, core, sizes)
        gradients, run = (*own, *give), piece
    else:
        gradients, run = tuple(gated(*arguments, lane_block, 1, 0, sizes)), width
        pick_parity = lambda values, parity: lax.dynamic_index_in_dim(
            values.reshape(rows, owners // 4, 2, piece), parity, 2, keepdims=False
        ).reshape(rows, width // 2)
        give = [pick_parity(g, 1 - core) for g in gradients]
        others = [lax.ppermute(g, "tm", flip_bit("tm", 0)) for g in give]
        own = [pick_parity(g, core) for g in gradients]
    grad_slots, gain_term = back(
        gradients, core, full_in, arrived, source, upstream, gain, run, 2 * LANES
    )
    returned = lax.all_to_all(grad_slots, "tm", split_axis=0, concat_axis=0, tiled=True)
    count = lax.axis_size("dp")
    bits = bits_of(count)
    shares = [
        outer_halved((normed, other_normed), (own[side], others[side]), order)
        for side, order in ((0, bits), (1, bits[::-1]))
    ]
    share = jnp.concatenate(shares, axis=1)
    share = share.reshape(width // count, owners // 2, piece).transpose(1, 0, 2)
    shard_in = sum_across(share)
    grad_loaded = pick_blocks(returned, owner_of.astype(jnp.int32), panels)
    sums = sum_everywhere(jnp.concatenate([kernel_term[:taps], gain_term], axis=0))
    return (grad_loaded[None, None], shard_in, sums[:taps], sums[taps])


def solution(mesh):
    in_specs = (
        P("dp", "tm", None, None, None),
        P("dp", "tm", None),
        P("dp", "tm", None),
        P(),
        P("dp", None),
        P(),
        P("dp", "tm", None, None, None),
    )
    out_specs = (P("dp", "tm", None, None, None), P("dp", "tm"), P(), P())
    return jax.shard_map(local, mesh=mesh, in_specs=in_specs, out_specs=out_specs, check_vma=False)
```

```python
import functools

import jax
import jax.numpy as jnp
from jax import lax
from jax.experimental import pallas as pl
from jax.experimental.pallas import tpu as pltpu
from jax.sharding import PartitionSpec as P

BF = jnp.bfloat16
F32 = jnp.float32
RIM = 16
LANES = 128
TILE = 32


def params(count, mib):
    return pltpu.CompilerParams(
        dimension_semantics=("arbitrary",) * count, vmem_limit_bytes=mib << 20
    )


def flip(axis, mask):
    return [(i, i ^ mask) for i in range(lax.axis_size(axis))]


def flip_bit(axis, bit):
    return flip(axis, 1 << bit)


def bits_of(count):
    bits = count.bit_length() - 1
    assert 1 << bits == count
    return list(range(bits))


def pick_body(index, source, target, sems, *, count):
    copies = [
        pltpu.make_async_copy(source.at[index[i]], target.at[i], sems.at[i]) for i in range(count)
    ]
    for copy in copies:
        copy.start()
    for copy in copies:
        copy.wait()


def pick_panels(source, index, count):
    _, rows, width = source.shape
    hbm = pl.BlockSpec(memory_space=pltpu.HBM)
    return pl.pallas_call(
        functools.partial(pick_body, count=count),
        grid_spec=pltpu.PrefetchScalarGridSpec(
            num_scalar_prefetch=1,
            grid=(1,),
            in_specs=[hbm],
            out_specs=hbm,
            scratch_shapes=[pltpu.SemaphoreType.DMA((count,))],
        ),
        out_shape=jax.ShapeDtypeStruct((count, rows, width), source.dtype),
        compiler_params=params(1, 58),
        name="pick_panels",
    )(index, source)


def copy_body(_, source, target):
    target[...] = source[...]


def pick_blocks(source, index, count):
    _, rows, width = source.shape
    return pl.pallas_call(
        copy_body,
        grid_spec=pltpu.PrefetchScalarGridSpec(
            num_scalar_prefetch=1,
            grid=(count,),
            in_specs=[pl.BlockSpec((1, rows, width), lambda i, idx: (idx[i], 0, 0))],
            out_specs=pl.BlockSpec((1, rows, width), lambda i, idx: (i, 0, 0)),
        ),
        out_shape=jax.ShapeDtypeStruct((count, rows, width), source.dtype),
        compiler_params=params(1, 8),
        name="pick_blocks",
    )(index, source)


def gather_order(block, order):
    have = block[None]
    relative = [0]
    for bit in order:
        got = lax.ppermute(have, "dp", flip_bit("dp", bit))
        have = jnp.concatenate([have, got], axis=0)
        relative = relative + [r ^ (1 << bit) for r in relative]
    return have, relative


def gather_weights(w_in, core):
    shard, width = w_in.shape
    quarter = shard // 4
    count = lax.axis_size("dp")
    place = lax.axis_index("dp")
    bits = bits_of(count)
    half = lax.dynamic_slice_in_dim(w_in, core * (2 * quarter), 2 * quarter, axis=0)
    first, first_rel = gather_order(half[:quarter], bits)
    second, second_rel = gather_order(half[quarter:], bits[::-1])
    other_first = lax.ppermute(first, "tm", flip_bit("tm", 0))
    other_second = lax.ppermute(second, "tm", flip_bit("tm", 0))
    rels = [first_rel, second_rel]

    def out_index(side):
        index = []
        for source in range(2):
            for position in range(count):
                index.append(((place ^ rels[source][position]) * 2 + side) * 2 + source)
        return jnp.stack(index).astype(jnp.int32)

    def body(_, a, b, *rest):
        target = rest[-1]
        for number, ref in enumerate((a, b)):

            @pl.when(pl.program_id(0) == number)
            def _():
                target[...] = ref[...]

    def spec(number):
        def index(source, position, _):
            last = count - 1 if number == 0 else 0
            return (jnp.where(source == number, position, last), 0, 0)

        return pl.BlockSpec((1, quarter, width), index)

    def put(side, pair, *base):
        return pl.pallas_call(
            body,
            grid_spec=pltpu.PrefetchScalarGridSpec(
                num_scalar_prefetch=1,
                grid=(2, count),
                in_specs=[spec(0), spec(1)] + [pl.BlockSpec(memory_space=pl.ANY) for _ in base],
                out_specs=pl.BlockSpec(
                    (1, quarter, width),
                    lambda source, position, idx: (idx[source * count + position], 0, 0),
                ),
            ),
            out_shape=jax.ShapeDtypeStruct((4 * count, quarter, width), w_in.dtype),
            input_output_aliases={3: 0} if base else {},
            compiler_params=params(2, 48),
            name="put_weights",
        )(out_index(side), *pair, *base)

    full = put(core, (first, second))
    full = put(1 - core, (other_first, other_second), full)
    return full.reshape(4 * quarter * count, width)


def forward_body(source, x_hbm, gain_ref, lin_w, gate_w, parts, lin_out, gate_out, glu_out, normed, xs, sems, *, panels):
    rows = xs.shape[1]

    def fetch(s):
        return pltpu.make_async_copy(x_hbm.at[source[s]], xs.at[s], sems.at[s])

    @pl.when(pl.program_id(0) == 0)
    def _():
        for s in range(panels):
            fetch(s).start()
        for s in range(panels):
            fetch(s).wait()

            x = xs[s].astype(F32)
            x = x - jnp.mean(x, axis=1, keepdims=True)
            scale = lax.rsqrt(jnp.mean(x * x, axis=1, keepdims=True) + 1e-05)
            normed[s * rows : (s + 1) * rows, :] = (x * scale * gain_ref[...]).astype(BF)

        count, _, shard = parts.shape
        for block in range(count):
            parts[block ^ source[panels]] = normed[:, block * shard : (block + 1) * shard]

    lin = jnp.dot(normed[...], lin_w[...], preferred_element_type=F32)
    lin_out[...] = lin
    gate = jnp.dot(normed[...], gate_w[...], preferred_element_type=F32)
    gate_out[...] = gate
    glu_out[...] = (lin * jax.nn.sigmoid(gate)).astype(BF)


def forward(arrived, source, gain, full_in, panels, block):
    _, rows, width = arrived.shape
    blocks = width // block
    column = pl.BlockSpec((panels * rows, block), lambda j, idx: (0, j))
    wide = lambda dtype: jax.ShapeDtypeStruct((panels * rows, width), dtype)
    count = lax.axis_size("dp")
    parts = jax.ShapeDtypeStruct((count, panels * rows, width // count), BF)
    return pl.pallas_call(
        functools.partial(forward_body, panels=panels),
        grid_spec=pltpu.PrefetchScalarGridSpec(
            num_scalar_prefetch=1,
            grid=(blocks,),
            in_specs=[
                pl.BlockSpec(memory_space=pl.ANY),
                pl.BlockSpec((1, width), lambda j, idx: (0, 0)),
                pl.BlockSpec((width, block), lambda j, idx: (0, j)),
                pl.BlockSpec((width, block), lambda j, idx: (0, blocks + j)),
            ],
            out_specs=[
                pl.BlockSpec(parts.shape, lambda j, idx: (0, 0, 0)),
                column,
                column,
                column,
            ],
            scratch_shapes=[
                pltpu.VMEM((panels * rows, width), BF),
                pltpu.VMEM((panels, rows, width), BF),
                pltpu.SemaphoreType.DMA((panels,)),
            ],
        ),
        out_shape=[parts, wide(F32), wide(F32), wide(BF)],
        compiler_params=params(1, 58),
        name="forward",
    )(jnp.append(source, lax.axis_index("dp")), arrived, gain.reshape(1, width), full_in, full_in)


def fill_padded(flags, padded, main, low, high, panels, length):
    for s in range(panels):
        at = s * length
        middle = main[at : at + length, :].astype(F32)
        before = low[low.shape[0] - RIM :, :] if s == 0 else main[at - RIM : at, :]
        after = high[:RIM, :] if s == panels - 1 else main[at + length : at + length + RIM, :]
        before = jnp.where(flags[s] > 0, before.astype(F32), 0.0)
        after = jnp.where(flags[panels + s] > 0, after.astype(F32), 0.0)
        for chunk in range(main.shape[1] // LANES):
            lanes = slice(chunk * LANES, (chunk + 1) * LANES)
            padded[chunk, s, RIM : RIM + length, :] = middle[:, lanes]
            padded[chunk, s, 0:RIM, :] = before[:, lanes]
            padded[chunk, s, RIM + length :, :] = after[:, lanes]


def shifted_sum(padded, weights, chunk, s, start, taps, flip, height=TILE):
    lanes = pl.ds(chunk * LANES, LANES)
    total = jnp.zeros((height, LANES), F32)
    for tap in range(taps):
        offset = taps - tap if flip else tap + 1
        view = padded[chunk, s, pl.ds(start + offset, height), :]
        total = total + weights[pl.ds(tap, 1), lanes] * view
    return total


def tiles(width, panels, length, work):
    for chunk in range(width // LANES):

        def step(s, carry):
            for start in range(0, length, TILE):
                rows = pl.ds(pl.multiple_of(s * length + start, TILE), TILE)
                work(chunk, s, start, rows, pl.ds(chunk * LANES, LANES))
            return carry

        lax.fori_loop(0, panels, step, 0)


def depth_body(
    flags, glu, low, high, upstream, up_low, up_high, weights, out, out_low, out_high, padded, ends, *, panels, length, taps
):
    fill_padded(flags, padded, glu, low, high, panels, length)
    rows = panels * length

    def grad(depth, up):
        sig = jax.nn.sigmoid(depth)
        return (up.astype(F32) * sig * (1.0 + depth * (1.0 - sig))).astype(BF)

    for chunk in range(glu.shape[1] // LANES):
        lanes = slice(chunk * LANES, (chunk + 1) * LANES)
        ends[chunk, 0, 0 : 2 * RIM, :] = low[:, lanes].astype(F32)
        ends[chunk, 0, 2 * RIM :, :] = glu[0:RIM, lanes].astype(F32)
        ends[chunk, 1, 0:RIM, :] = glu[rows - RIM : rows, lanes].astype(F32)
        ends[chunk, 1, RIM:, :] = high[:, lanes].astype(F32)
        for side, up, to in ((0, up_low, out_low), (1, up_high, out_high)):
            depth = shifted_sum(ends, weights, chunk, side, 0, taps, False, RIM)
            to[:, lanes] = grad(depth, up[:, lanes])

    def work(chunk, s, start, at, lanes):
        depth = shifted_sum(padded, weights, chunk, s, start, taps, False)
        out[at, lanes] = grad(depth, upstream[at, lanes])

    tiles(glu.shape[1], panels, length, work)


def taps_body(flags, glu, low, high, grad, out, padded, partial, *, panels, length, taps):
    fill_padded(flags, padded, glu, low, high, panels, length)
    for chunk in range(glu.shape[1] // LANES):
        lanes = pl.ds(chunk * LANES, LANES)
        partial[...] = jnp.zeros_like(partial)

        def step(s, carry):
            rows = pl.ds(pl.multiple_of(s * length, length), length)
            g = grad[rows, lanes].astype(F32)
            for tap in range(taps):
                product = g * padded[chunk, s, pl.ds(tap + 1, length), :]
                partial[tap] += jnp.sum(product.reshape(length // 8, 8, LANES), axis=0)
            return carry

        lax.fori_loop(0, panels, step, 0)
        out[:, lanes] = jnp.sum(partial[...], axis=1)


def gated_body(flags, grad, low, high, lin, gate, weights, *refs, panels, length, taps):
    *outs, padded = refs
    fill_padded(flags, padded, grad, low, high, panels, length)

    def work(chunk, s, start, rows, lanes):
        total = shifted_sum(padded, weights, chunk, s, start, taps, True)
        sig = jax.nn.sigmoid(gate[rows, lanes])
        scaled = total * sig
        outs[0][rows, lanes] = scaled.astype(BF)
        outs[1][rows, lanes] = (scaled * lin[rows, lanes] * (1.0 - sig)).astype(BF)

    tiles(grad.shape[1], panels, length, work)


def gated(flags, grad_depth, low, high, lin, gate, kernel, block, parities, parity, sizes):
    rows, width = grad_depth.shape
    panels = sizes["panels"]
    column = lambda height: pl.BlockSpec((height, block), lambda j, idx: (0, j * parities + idx[2 * panels]))
    shapes = [jax.ShapeDtypeStruct((rows, width // parities), BF)] * 2
    return pl.pallas_call(
        functools.partial(gated_body, **sizes),
        grid_spec=pltpu.PrefetchScalarGridSpec(
            num_scalar_prefetch=1,
            grid=(width // block // parities,),
            in_specs=[column(h) for h in (rows, RIM, RIM, rows, rows, kernel.shape[0])],
            out_specs=[pl.BlockSpec((rows, block), lambda j, idx: (0, j)) for _ in shapes],
            scratch_shapes=[
                pltpu.VMEM((block // LANES, panels, sizes["length"] + 2 * RIM, LANES), F32)
            ],
        ),
        out_shape=shapes,
        compiler_params=params(1, 58),
        name="gated",
    )(jnp.append(flags, parity), grad_depth, low, high, lin, gate, kernel)


def back_body(source, *refs, grads, block, panels, piece):
    gradients = refs[:grads]
    w_ref, x_hbm, up_hbm, gain_ref, out_hbm, gain_out, total, xs, ups, outs, sems = refs[grads:]
    step = pl.program_id(0)

    def fetch(s):
        return (
            pltpu.make_async_copy(x_hbm.at[source[s]], xs.at[s], sems.at[s]),
            pltpu.make_async_copy(up_hbm.at[s], ups.at[s], sems.at[panels + s]),
        )

    def put(s):
        return pltpu.make_async_copy(outs.at[s], out_hbm.at[source[s]], sems.at[2 * panels + s])

    @pl.when(step == 0)
    def _():
        for s in range(panels):
            for copy in fetch(s):
                copy.start()

    acc = None
    for number, grad in enumerate(gradients):
        pieces = grad.shape[1] // piece
        for i in range(pieces):
            column = (number % 2 * pieces + i) * (grads // 2) * piece
            if grads > 2:
                column = column + (source[panels] ^ (number // 2)) * piece
                column = pl.multiple_of(column, LANES)
            term = lax.dot_general(
                grad[:, i * piece : (i + 1) * piece],
                w_ref[:, pl.ds(column, piece)],
                (((1,), (1,)), ((), ())),
                preferred_element_type=F32,
            )
            acc = term if acc is None else acc + term
    total[:, pl.ds(pl.multiple_of(step * block, block), block)] = acc

    @pl.when(step == pl.num_programs(0) - 1)
    def _():
        rows = xs.shape[1]
        gain = gain_ref[...]
        gain_sum = jnp.zeros_like(gain)
        for s in range(panels):
            for copy in fetch(s):
                copy.wait()

            x = xs[s].astype(F32)
            x = x - jnp.mean(x, axis=1, keepdims=True)
            scale = lax.rsqrt(jnp.mean(x * x, axis=1, keepdims=True) + 1e-05)
            unit = x * scale
            g = total[s * rows : (s + 1) * rows, :]
            gain_sum = gain_sum + jnp.sum(g * unit, axis=0, keepdims=True)
            q = g * gain
            mean_q = jnp.mean(q, axis=1, keepdims=True)
            mean_u = jnp.mean(q * unit, axis=1, keepdims=True)
            outs[s] = (ups[s].astype(F32) + scale * (q - mean_q - unit * mean_u)).astype(BF)
            put(s).start()
        gain_out[...] = gain_sum
        for s in range(panels):
            put(s).wait()


def back(gradients, core, full_in, arrived, source, upstream, gain, piece, block):
    _, rows, width = arrived.shape
    panels = upstream.shape[0]
    constant = lambda rank: (lambda n, idx: (0,) * rank)
    hbm = pl.BlockSpec(memory_space=pl.ANY)
    panel_scratch = pltpu.VMEM((panels, rows, width), BF)
    return pl.pallas_call(
        functools.partial(back_body, grads=len(gradients), block=block, panels=panels, piece=piece),
        grid_spec=pltpu.PrefetchScalarGridSpec(
            num_scalar_prefetch=1,
            grid=(width // block,),
            in_specs=[pl.BlockSpec(g.shape, constant(2)) for g in gradients]
            + [
                pl.BlockSpec((block, full_in.shape[1]), lambda n, idx: (n, 0)),
                hbm,
                hbm,
                pl.BlockSpec((1, width), constant(2)),
            ],
            out_specs=[hbm, pl.BlockSpec((1, width), constant(2))],
            scratch_shapes=[
                pltpu.VMEM((panels * rows, width), F32),
                panel_scratch,
                panel_scratch,
                panel_scratch,
                pltpu.SemaphoreType.DMA((3 * panels,)),
            ],
        ),
        out_shape=[
            jax.ShapeDtypeStruct(arrived.shape, BF),
            jax.ShapeDtypeStruct((1, width), F32),
        ],
        compiler_params=params(1, 58),
        name="back",
    )(jnp.append(source, core), *gradients, full_in, arrived, upstream, gain.reshape(1, width))


def outer_sum(lefts, rights):
    terms = [
        lax.dot_general(a, b, (((1,), (0,)), ((), ())), preferred_element_type=F32)
        for a, b in zip(lefts, rights)
    ]
    return (terms[0] + terms[1]).astype(BF)


def outer_halved(lefts, rights, order):
    count = lefts[0].shape[0]
    rels = sorted(range(count), key=lambda r: [(r >> bit) & 1 for bit in order])
    half = count // 2
    pick = lambda left, some: jnp.concatenate([left[r : r + 1] for r in some])
    send = outer_sum([pick(left, rels[half:]) for left in lefts], rights)
    keep = outer_sum([pick(left, rels[:half]) for left in lefts], rights)
    add = lambda a, b: (a.astype(F32) + b.astype(F32)).astype(BF)
    for bit in order:
        got = lax.ppermute(send, "dp", flip_bit("dp", bit))
        half = half // 2
        if half:
            send = add(keep[half:], got[half:])
            keep = add(keep[:half], got[:half])
        else:
            keep = add(keep, got)
    return keep[0]


def sum_everywhere(values):
    for bit in bits_of(lax.axis_size("dp")):
        values = values + lax.ppermute(values, "dp", flip_bit("dp", bit))
    halves = values.reshape(2, values.shape[0] // 2, values.shape[1])
    core = lax.axis_index("tm") % 2
    send = lax.dynamic_index_in_dim(halves, 1 - core, 0, keepdims=False)
    keep = lax.dynamic_index_in_dim(halves, core, 0, keepdims=False)
    values = (keep + lax.ppermute(send, "tm", flip_bit("tm", 0))).astype(BF)
    terms = [values]
    for mask in range(2, lax.axis_size("tm"), 2):
        terms.append(lax.ppermute(values, "tm", flip("tm", mask)))
    terms = [term.astype(F32) for term in terms]
    while len(terms) > 1:
        terms = [a + b for a, b in zip(terms[::2], terms[1::2])]
    values = terms[0]
    got = lax.ppermute(values, "tm", flip_bit("tm", 0))
    return jnp.concatenate([jnp.where(core == 0, values, got), jnp.where(core == 0, got, values)])


def sum_across(share):
    count = share.shape[0]
    place = lax.axis_index("tm") // 2
    total = lax.dynamic_index_in_dim(share, place, 0, keepdims=False).astype(F32)
    for turn in range(1, count):
        piece = lax.dynamic_index_in_dim(share, place ^ turn, 0, keepdims=False)
        pairs = [(i, i ^ (2 * turn)) for i in range(2 * count)]
        total = total + lax.ppermute(piece, "tm", pairs).astype(F32)
    return total


def edges(values, width):
    count = lax.axis_size("tm")
    low = lax.ppermute(values[-width:], "tm", [(i, i + 1) for i in range(count - 1)])
    high = lax.ppermute(values[:width], "tm", [(i + 1, i) for i in range(count - 1)])
    return low, high


def local(frames, route, utterance, gain, w_in, kernel, cotangent):
    panels, length, width = frames.shape[2:]
    owners = lax.axis_size("tm")
    rows = panels * length
    taps = kernel.shape[0]
    reach = taps // 2
    assert reach < RIM and taps == 31
    loaded = frames[0, 0]
    target = route[0, 0]
    labels = utterance[0, 0]
    upstream = cotangent[0, 0]
    core = lax.axis_index("tm") % 2
    owner_of = target // panels
    pick = owner_of[None, :] == jnp.arange(owners, dtype=jnp.int32)[:, None]
    panel_of = jnp.sum(jnp.where(pick, jnp.arange(panels, dtype=jnp.int32)[None, :], 0), axis=1)
    outgoing = pick_panels(loaded, panel_of.astype(jnp.int32), owners)
    arrived = lax.all_to_all(outgoing, "tm", split_axis=0, concat_axis=0, tiled=True)
    me = lax.axis_index("tm")
    tags = jnp.stack([target, labels + 1])[None]
    tags = jnp.concatenate([tags, lax.ppermute(tags, "tm", flip_bit("tm", 0))])
    rest = [lax.ppermute(tags, "tm", flip("tm", i)) for i in range(2, owners, 2)]
    tags = jnp.concatenate([tags] + rest)
    loader = (jnp.arange(owners, dtype=jnp.int32) ^ me)[None, :, None]
    position = me * panels - 1 + jnp.arange(panels + 2, dtype=jnp.int32)
    found = tags[None, :, 0] == position[:, None, None]
    line = jnp.sum(jnp.where(found, tags[None, :, 1], 0), axis=(1, 2))
    source = jnp.sum(jnp.where(found[1:-1], loader, 0), axis=(1, 2)).astype(jnp.int32)
    flags = jnp.concatenate([line[1:-1] == line[:-2], line[1:-1] == line[2:]]).astype(jnp.int32)

    full_in = gather_weights(w_in, core)
    normed, lin, gate, glu = forward(arrived, source, gain, full_in, panels, 4 * LANES)
    other_normed = lax.ppermute(normed, "tm", flip_bit("tm", 0))
    glu_low, glu_high = edges(glu, 2 * RIM)

    lane_block = 2 * LANES
    column = lambda height: pl.BlockSpec((height, lane_block), lambda j, idx: (0, j))
    sizes = dict(panels=panels, length=length, taps=taps)
    padded_of = lambda lanes: pltpu.VMEM((lanes // LANES, panels, length + 2 * RIM, LANES), F32)
    up_rows = upstream.reshape(rows, width)
    up_low, up_high = edges(up_rows, RIM)
    grad_depth, grad_low, grad_high = pl.pallas_call(
        functools.partial(depth_body, **sizes),
        grid_spec=pltpu.PrefetchScalarGridSpec(
            num_scalar_prefetch=1,
            grid=(width // lane_block,),
            in_specs=[column(h) for h in (rows, 2 * RIM, 2 * RIM, rows, RIM, RIM, taps)],
            out_specs=[column(rows), column(RIM), column(RIM)],
            scratch_shapes=[
                padded_of(lane_block),
                pltpu.VMEM((lane_block // LANES, 2, 3 * RIM, LANES), F32),
            ],
        ),
        out_shape=[jax.ShapeDtypeStruct((h, width), BF) for h in (rows, RIM, RIM)],
        compiler_params=params(1, 58),
        name="depth",
    )(flags, glu, glu_low, glu_high, up_rows, up_low, up_high, kernel)
    kernel_term = pl.pallas_call(
        functools.partial(taps_body, **sizes),
        grid_spec=pltpu.PrefetchScalarGridSpec(
            num_scalar_prefetch=1,
            grid=(width // lane_block,),
            in_specs=[column(h) for h in (rows, 2 * RIM, 2 * RIM, rows)],
            out_specs=column(taps + 1),
            scratch_shapes=[padded_of(lane_block), pltpu.VMEM((taps + 1, 8, LANES), F32)],
        ),
        out_shape=jax.ShapeDtypeStruct((taps + 1, width), F32),
        compiler_params=params(1, 48),
        name="taps",
    )(flags, glu, glu_low, glu_high, grad_depth)

    piece = 2 * width // owners
    arguments = (flags, grad_depth, grad_low, grad_high, lin, gate, kernel)
    if piece % LANES == 0:
        give = gated(*arguments, piece, 2, 1 - core, sizes)
        others = [lax.ppermute(g, "tm", flip_bit("tm", 0)) for g in give]
        own = gated(*arguments, piece, 2, core, sizes)
        gradients, run = (*own, *give), piece
    else:
        gradients, run = tuple(gated(*arguments, lane_block, 1, 0, sizes)), width
        pick_parity = lambda values, parity: lax.dynamic_index_in_dim(
            values.reshape(rows, owners // 4, 2, piece), parity, 2, keepdims=False
        ).reshape(rows, width // 2)
        give = [pick_parity(g, 1 - core) for g in gradients]
        others = [lax.ppermute(g, "tm", flip_bit("tm", 0)) for g in give]
        own = [pick_parity(g, core) for g in gradients]
    grad_slots, gain_term = back(
        gradients, core, full_in, arrived, source, upstream, gain, run, 2 * LANES
    )
    returned = lax.all_to_all(grad_slots, "tm", split_axis=0, concat_axis=0, tiled=True)
    count = lax.axis_size("dp")
    bits = bits_of(count)
    shares = [
        outer_halved((normed, other_normed), (own[side], others[side]), order)
        for side, order in ((0, bits), (1, bits[::-1]))
    ]
    share = jnp.concatenate(shares, axis=1)
    share = share.reshape(width // count, owners // 2, piece).transpose(1, 0, 2)
    shard_in = sum_across(share)
    grad_loaded = pick_blocks(returned, owner_of.astype(jnp.int32), panels)
    sums = sum_everywhere(jnp.concatenate([kernel_term[:taps], gain_term], axis=0))
    return (grad_loaded[None, None], shard_in, sums[:taps], sums[taps])


def solution(mesh):
    in_specs = (
        P("dp", "tm", None, None, None),
        P("dp", "tm", None),
        P("dp", "tm", None),
        P(),
        P("dp", None),
        P(),
        P("dp", "tm", None, None, None),
    )
    out_specs = (P("dp", "tm", None, None, None), P("dp", "tm"), P(), P())
    return jax.shard_map(local, mesh=mesh, in_specs=in_specs, out_specs=out_specs, check_vma=False)
```

```python
import functools

import jax
import jax.numpy as jnp
from jax import lax
from jax.experimental import pallas as pl
from jax.experimental.pallas import tpu as pltpu
from jax.sharding import PartitionSpec as P

BF = jnp.bfloat16
F32 = jnp.float32
RIM = 16
LANES = 128
TILE = 32


def params(count, mib):
    return pltpu.CompilerParams(
        dimension_semantics=("arbitrary",) * count, vmem_limit_bytes=mib << 20
    )


def flip(axis, mask):
    return [(i, i ^ mask) for i in range(lax.axis_size(axis))]


def flip_bit(axis, bit):
    return flip(axis, 1 << bit)


def bits_of(count):
    bits = count.bit_length() - 1
    assert 1 << bits == count
    return list(range(bits))


def pick_body(index, source, target, sems, *, count):
    copies = [
        pltpu.make_async_copy(source.at[index[i]], target.at[i], sems.at[i]) for i in range(count)
    ]
    for copy in copies:
        copy.start()
    for copy in copies:
        copy.wait()


def pick_panels(source, index, count):
    _, rows, width = source.shape
    return pl.pallas_call(
        functools.partial(pick_body, count=count),
        grid_spec=pltpu.PrefetchScalarGridSpec(
            num_scalar_prefetch=1,
            grid=(1,),
            in_specs=[pl.BlockSpec(source.shape, lambda i, idx: (0, 0, 0))],
            out_specs=pl.BlockSpec(memory_space=pltpu.HBM),
            scratch_shapes=[pltpu.SemaphoreType.DMA((count,))],
        ),
        out_shape=jax.ShapeDtypeStruct((count, rows, width), source.dtype),
        compiler_params=params(1, 48),
        name="pick_panels",
    )(index, source)


def copy_body(_, source, target):
    target[...] = source[...]


def pick_blocks(source, index, count):
    _, rows, width = source.shape
    return pl.pallas_call(
        copy_body,
        grid_spec=pltpu.PrefetchScalarGridSpec(
            num_scalar_prefetch=1,
            grid=(count,),
            in_specs=[pl.BlockSpec((1, rows, width), lambda i, idx: (idx[i], 0, 0))],
            out_specs=pl.BlockSpec((1, rows, width), lambda i, idx: (i, 0, 0)),
        ),
        out_shape=jax.ShapeDtypeStruct((count, rows, width), source.dtype),
        compiler_params=params(1, 48),
        name="pick_blocks",
    )(index, source)


def gather_order(block, order):
    have = block[None]
    relative = [0]
    for bit in order:
        got = lax.ppermute(have, "dp", flip_bit("dp", bit))
        have = jnp.concatenate([have, got], axis=0)
        relative = relative + [r ^ (1 << bit) for r in relative]
    return have, relative


def gather_weights(w_in, core):
    shard, width = w_in.shape
    quarter = shard // 4
    count = lax.axis_size("dp")
    place = lax.axis_index("dp")
    bits = bits_of(count)
    half = lax.dynamic_slice_in_dim(w_in, core * (2 * quarter), 2 * quarter, axis=0)
    first, first_rel = gather_order(half[:quarter], bits)
    second, second_rel = gather_order(half[quarter:], bits[::-1])
    other_first = lax.ppermute(first, "tm", flip_bit("tm", 0))
    other_second = lax.ppermute(second, "tm", flip_bit("tm", 0))
    rels = [first_rel, second_rel]

    def out_index(side):
        index = []
        for source in range(2):
            for position in range(count):
                index.append(((place ^ rels[source][position]) * 2 + side) * 2 + source)
        return jnp.stack(index).astype(jnp.int32)

    def body(_, a, b, *rest):
        target = rest[-1]
        for number, ref in enumerate((a, b)):

            @pl.when(pl.program_id(0) == number)
            def _():
                target[...] = ref[...]

    def spec(number):
        def index(source, position, _):
            last = count - 1 if number == 0 else 0
            return (jnp.where(source == number, position, last), 0, 0)

        return pl.BlockSpec((1, quarter, width), index)

    def put(side, pair, *base):
        return pl.pallas_call(
            body,
            grid_spec=pltpu.PrefetchScalarGridSpec(
                num_scalar_prefetch=1,
                grid=(2, count),
                in_specs=[spec(0), spec(1)] + [pl.BlockSpec(memory_space=pl.ANY) for _ in base],
                out_specs=pl.BlockSpec(
                    (1, quarter, width),
                    lambda source, position, idx: (idx[source * count + position], 0, 0),
                ),
            ),
            out_shape=jax.ShapeDtypeStruct((4 * count, quarter, width), w_in.dtype),
            input_output_aliases={3: 0} if base else {},
            compiler_params=params(2, 48),
            name="put_weights",
        )(out_index(side), *pair, *base)

    full = put(core, (first, second))
    full = put(1 - core, (other_first, other_second), full)
    return full.reshape(4 * quarter * count, width)


def forward_body(source, x_hbm, gain_ref, lin_w, gate_w, parts, lin_out, gate_out, glu_out, normed, xs, sems, *, panels):
    rows = xs.shape[1]

    def fetch(s):
        return pltpu.make_async_copy(x_hbm.at[source[s]], xs.at[s], sems.at[s])

    @pl.when(pl.program_id(0) == 0)
    def _():
        for s in range(panels):
            fetch(s).start()
        for s in range(panels):
            fetch(s).wait()

            x = xs[s].astype(F32)
            x = x - jnp.mean(x, axis=1, keepdims=True)
            scale = lax.rsqrt(jnp.mean(x * x, axis=1, keepdims=True) + 1e-05)
            normed[s * rows : (s + 1) * rows, :] = (x * scale * gain_ref[...]).astype(BF)

        count, _, shard = parts.shape
        for block in range(count):
            parts[block ^ source[panels]] = normed[:, block * shard : (block + 1) * shard]

    lin = jnp.dot(normed[...], lin_w[...], preferred_element_type=F32)
    lin_out[...] = lin
    gate = jnp.dot(normed[...], gate_w[...], preferred_element_type=F32)
    gate_out[...] = gate
    glu_out[...] = (lin * jax.nn.sigmoid(gate)).astype(BF)


def forward(arrived, source, gain, full_in, panels, block):
    _, rows, width = arrived.shape
    blocks = width // block
    column = pl.BlockSpec((panels * rows, block), lambda j, idx: (0, j))
    wide = lambda dtype: jax.ShapeDtypeStruct((panels * rows, width), dtype)
    count = lax.axis_size("dp")
    parts = jax.ShapeDtypeStruct((count, panels * rows, width // count), BF)
    return pl.pallas_call(
        functools.partial(forward_body, panels=panels),
        grid_spec=pltpu.PrefetchScalarGridSpec(
            num_scalar_prefetch=1,
            grid=(blocks,),
            in_specs=[
                pl.BlockSpec(memory_space=pl.ANY),
                pl.BlockSpec((1, width), lambda j, idx: (0, 0)),
                pl.BlockSpec((width, block), lambda j, idx: (0, j)),
                pl.BlockSpec((width, block), lambda j, idx: (0, blocks + j)),
            ],
            out_specs=[
                pl.BlockSpec(parts.shape, lambda j, idx: (0, 0, 0)),
                column,
                column,
                column,
            ],
            scratch_shapes=[
                pltpu.VMEM((panels * rows, width), BF),
                pltpu.VMEM((panels, rows, width), BF),
                pltpu.SemaphoreType.DMA((panels,)),
            ],
        ),
        out_shape=[parts, wide(F32), wide(F32), wide(BF)],
        compiler_params=params(1, 48),
        name="forward",
    )(jnp.append(source, lax.axis_index("dp")), arrived, gain.reshape(1, width), full_in, full_in)


def fill_padded(flags, padded, main, low, high, panels, length):
    for s in range(panels):
        at = s * length
        middle = main[at : at + length, :].astype(F32)
        before = low[low.shape[0] - RIM :, :] if s == 0 else main[at - RIM : at, :]
        after = high[:RIM, :] if s == panels - 1 else main[at + length : at + length + RIM, :]
        before = jnp.where(flags[s] > 0, before.astype(F32), 0.0)
        after = jnp.where(flags[panels + s] > 0, after.astype(F32), 0.0)
        for chunk in range(main.shape[1] // LANES):
            lanes = slice(chunk * LANES, (chunk + 1) * LANES)
            padded[chunk, s, RIM : RIM + length, :] = middle[:, lanes]
            padded[chunk, s, 0:RIM, :] = before[:, lanes]
            padded[chunk, s, RIM + length :, :] = after[:, lanes]


def shifted_sum(padded, weights, chunk, s, start, taps, flip, height=TILE):
    lanes = pl.ds(chunk * LANES, LANES)
    total = jnp.zeros((height, LANES), F32)
    for tap in range(taps):
        offset = taps - tap if flip else tap + 1
        view = padded[chunk, s, pl.ds(start + offset, height), :]
        total = total + weights[pl.ds(tap, 1), lanes] * view
    return total


def tiles(width, panels, length, work):
    for chunk in range(width // LANES):

        def step(s, carry):
            for start in range(0, length, TILE):
                rows = pl.ds(pl.multiple_of(s * length + start, TILE), TILE)
                work(chunk, s, start, rows, pl.ds(chunk * LANES, LANES))
            return carry

        lax.fori_loop(0, panels, step, 0)


def depth_body(
    flags, glu, low, high, upstream, up_low, up_high, weights, out, out_low, out_high, padded, ends, *, panels, length, taps
):
    fill_padded(flags, padded, glu, low, high, panels, length)
    rows = panels * length

    def grad(depth, up):
        sig = jax.nn.sigmoid(depth)
        return (up.astype(F32) * sig * (1.0 + depth * (1.0 - sig))).astype(BF)

    for chunk in range(glu.shape[1] // LANES):
        lanes = slice(chunk * LANES, (chunk + 1) * LANES)
        ends[chunk, 0, 0 : 2 * RIM, :] = low[:, lanes].astype(F32)
        ends[chunk, 0, 2 * RIM :, :] = glu[0:RIM, lanes].astype(F32)
        ends[chunk, 1, 0:RIM, :] = glu[rows - RIM : rows, lanes].astype(F32)
        ends[chunk, 1, RIM:, :] = high[:, lanes].astype(F32)
        for side, up, to in ((0, up_low, out_low), (1, up_high, out_high)):
            depth = shifted_sum(ends, weights, chunk, side, 0, taps, False, RIM)
            to[:, lanes] = grad(depth, up[:, lanes])

    def work(chunk, s, start, at, lanes):
        depth = shifted_sum(padded, weights, chunk, s, start, taps, False)
        out[at, lanes] = grad(depth, upstream[at, lanes])

    tiles(glu.shape[1], panels, length, work)


def taps_body(flags, glu, low, high, grad, out, padded, partial, *, panels, length, taps):
    fill_padded(flags, padded, glu, low, high, panels, length)
    for chunk in range(glu.shape[1] // LANES):
        lanes = pl.ds(chunk * LANES, LANES)
        partial[...] = jnp.zeros_like(partial)

        def step(s, carry):
            rows = pl.ds(pl.multiple_of(s * length, length), length)
            g = grad[rows, lanes].astype(F32)
            for tap in range(taps):
                product = g * padded[chunk, s, pl.ds(tap + 1, length), :]
                partial[tap] += jnp.sum(product.reshape(length // 8, 8, LANES), axis=0)
            return carry

        lax.fori_loop(0, panels, step, 0)
        out[:, lanes] = jnp.sum(partial[...], axis=1)


def gated_body(flags, grad, low, high, lin, gate, weights, *refs, panels, length, taps):
    *outs, padded = refs
    fill_padded(flags, padded, grad, low, high, panels, length)

    def work(chunk, s, start, rows, lanes):
        total = shifted_sum(padded, weights, chunk, s, start, taps, True)
        sig = jax.nn.sigmoid(gate[rows, lanes])
        scaled = total * sig
        outs[0][rows, lanes] = scaled.astype(BF)
        outs[1][rows, lanes] = (scaled * lin[rows, lanes] * (1.0 - sig)).astype(BF)

    tiles(grad.shape[1], panels, length, work)


def gated(flags, grad_depth, low, high, lin, gate, kernel, block, parities, parity, sizes):
    rows, width = grad_depth.shape
    panels = sizes["panels"]
    column = lambda height: pl.BlockSpec((height, block), lambda j, idx: (0, j * parities + idx[2 * panels]))
    shapes = [jax.ShapeDtypeStruct((rows, width // parities), BF)] * 2
    return pl.pallas_call(
        functools.partial(gated_body, **sizes),
        grid_spec=pltpu.PrefetchScalarGridSpec(
            num_scalar_prefetch=1,
            grid=(width // block // parities,),
            in_specs=[column(h) for h in (rows, RIM, RIM, rows, rows, kernel.shape[0])],
            out_specs=[pl.BlockSpec((rows, block), lambda j, idx: (0, j)) for _ in shapes],
            scratch_shapes=[
                pltpu.VMEM((block // LANES, panels, sizes["length"] + 2 * RIM, LANES), F32)
            ],
        ),
        out_shape=shapes,
        compiler_params=params(1, 48),
        name="gated",
    )(jnp.append(flags, parity), grad_depth, low, high, lin, gate, kernel)


def back_body(source, *refs, grads, block, panels, piece):
    gradients = refs[:grads]
    w_ref, x_hbm, up_hbm, gain_ref, out_hbm, gain_out, total, xs, ups, outs, sems = refs[grads:]
    step = pl.program_id(0)

    def fetch(s):
        return (
            pltpu.make_async_copy(x_hbm.at[source[s]], xs.at[s], sems.at[s]),
            pltpu.make_async_copy(up_hbm.at[s], ups.at[s], sems.at[panels + s]),
        )

    def put(s):
        return pltpu.make_async_copy(outs.at[s], out_hbm.at[source[s]], sems.at[2 * panels + s])

    @pl.when(step == 0)
    def _():
        for s in range(panels):
            for copy in fetch(s):
                copy.start()

    acc = None
    for number, grad in enumerate(gradients):
        pieces = grad.shape[1] // piece
        for i in range(pieces):
            column = (number % 2 * pieces + i) * (grads // 2) * piece
            if grads > 2:
                column = column + (source[panels] ^ (number // 2)) * piece
                column = pl.multiple_of(column, LANES)
            term = lax.dot_general(
                grad[:, i * piece : (i + 1) * piece],
                w_ref[:, pl.ds(column, piece)],
                (((1,), (1,)), ((), ())),
                preferred_element_type=F32,
            )
            acc = term if acc is None else acc + term
    total[:, pl.ds(pl.multiple_of(step * block, block), block)] = acc

    @pl.when(step == pl.num_programs(0) - 1)
    def _():
        rows = xs.shape[1]
        gain = gain_ref[...]
        gain_sum = jnp.zeros_like(gain)
        for s in range(panels):
            for copy in fetch(s):
                copy.wait()

            x = xs[s].astype(F32)
            x = x - jnp.mean(x, axis=1, keepdims=True)
            scale = lax.rsqrt(jnp.mean(x * x, axis=1, keepdims=True) + 1e-05)
            unit = x * scale
            g = total[s * rows : (s + 1) * rows, :]
            gain_sum = gain_sum + jnp.sum(g * unit, axis=0, keepdims=True)
            q = g * gain
            mean_q = jnp.mean(q, axis=1, keepdims=True)
            mean_u = jnp.mean(q * unit, axis=1, keepdims=True)
            outs[s] = (ups[s].astype(F32) + scale * (q - mean_q - unit * mean_u)).astype(BF)
            put(s).start()
        gain_out[...] = gain_sum
        for s in range(panels):
            put(s).wait()


def back(gradients, core, full_in, arrived, source, upstream, gain, piece, block):
    _, rows, width = arrived.shape
    panels = upstream.shape[0]
    constant = lambda rank: (lambda n, idx: (0,) * rank)
    hbm = pl.BlockSpec(memory_space=pl.ANY)
    panel_scratch = pltpu.VMEM((panels, rows, width), BF)
    return pl.pallas_call(
        functools.partial(back_body, grads=len(gradients), block=block, panels=panels, piece=piece),
        grid_spec=pltpu.PrefetchScalarGridSpec(
            num_scalar_prefetch=1,
            grid=(width // block,),
            in_specs=[pl.BlockSpec(g.shape, constant(2)) for g in gradients]
            + [
                pl.BlockSpec((block, full_in.shape[1]), lambda n, idx: (n, 0)),
                hbm,
                hbm,
                pl.BlockSpec((1, width), constant(2)),
            ],
            out_specs=[hbm, pl.BlockSpec((1, width), constant(2))],
            scratch_shapes=[
                pltpu.VMEM((panels * rows, width), F32),
                panel_scratch,
                panel_scratch,
                panel_scratch,
                pltpu.SemaphoreType.DMA((3 * panels,)),
            ],
        ),
        out_shape=[
            jax.ShapeDtypeStruct(arrived.shape, BF),
            jax.ShapeDtypeStruct((1, width), F32),
        ],
        compiler_params=params(1, 48),
        name="back",
    )(jnp.append(source, core), *gradients, full_in, arrived, upstream, gain.reshape(1, width))


def outer_sum(lefts, rights):
    terms = [
        lax.dot_general(a, b, (((1,), (0,)), ((), ())), preferred_element_type=F32)
        for a, b in zip(lefts, rights)
    ]
    return (terms[0] + terms[1]).astype(BF)


def outer_halved(lefts, rights, order):
    count = lefts[0].shape[0]
    rels = sorted(range(count), key=lambda r: [(r >> bit) & 1 for bit in order])
    half = count // 2
    pick = lambda left, some: jnp.concatenate([left[r : r + 1] for r in some])
    send = outer_sum([pick(left, rels[half:]) for left in lefts], rights)
    keep = outer_sum([pick(left, rels[:half]) for left in lefts], rights)
    add = lambda a, b: (a.astype(F32) + b.astype(F32)).astype(BF)
    for bit in order:
        got = lax.ppermute(send, "dp", flip_bit("dp", bit))
        half = half // 2
        if half:
            send = add(keep[half:], got[half:])
            keep = add(keep[:half], got[:half])
        else:
            keep = add(keep, got)
    return keep[0]


def sum_everywhere(values):
    for bit in bits_of(lax.axis_size("dp")):
        values = values + lax.ppermute(values, "dp", flip_bit("dp", bit))
    halves = values.reshape(2, values.shape[0] // 2, values.shape[1])
    core = lax.axis_index("tm") % 2
    send = lax.dynamic_index_in_dim(halves, 1 - core, 0, keepdims=False)
    keep = lax.dynamic_index_in_dim(halves, core, 0, keepdims=False)
    values = (keep + lax.ppermute(send, "tm", flip_bit("tm", 0))).astype(BF)
    terms = [values]
    for mask in range(2, lax.axis_size("tm"), 2):
        terms.append(lax.ppermute(values, "tm", flip("tm", mask)))
    terms = [term.astype(F32) for term in terms]
    while len(terms) > 1:
        terms = [a + b for a, b in zip(terms[::2], terms[1::2])]
    values = terms[0]
    got = lax.ppermute(values, "tm", flip_bit("tm", 0))
    return jnp.concatenate([jnp.where(core == 0, values, got), jnp.where(core == 0, got, values)])


def sum_across(share):
    count = share.shape[0]
    place = lax.axis_index("tm") // 2
    total = lax.dynamic_index_in_dim(share, place, 0, keepdims=False).astype(F32)
    for turn in range(1, count):
        piece = lax.dynamic_index_in_dim(share, place ^ turn, 0, keepdims=False)
        pairs = [(i, i ^ (2 * turn)) for i in range(2 * count)]
        total = total + lax.ppermute(piece, "tm", pairs).astype(F32)
    return total


def edges(values, width):
    count = lax.axis_size("tm")
    low = lax.ppermute(values[-width:], "tm", [(i, i + 1) for i in range(count - 1)])
    high = lax.ppermute(values[:width], "tm", [(i + 1, i) for i in range(count - 1)])
    return low, high


def local(frames, route, utterance, gain, w_in, kernel, cotangent):
    panels, length, width = frames.shape[2:]
    owners = lax.axis_size("tm")
    rows = panels * length
    taps = kernel.shape[0]
    reach = taps // 2
    assert reach < RIM and taps == 31
    loaded = frames[0, 0]
    target = route[0, 0]
    labels = utterance[0, 0]
    upstream = cotangent[0, 0]
    core = lax.axis_index("tm") % 2
    owner_of = target // panels
    pick = owner_of[None, :] == jnp.arange(owners, dtype=jnp.int32)[:, None]
    panel_of = jnp.sum(jnp.where(pick, jnp.arange(panels, dtype=jnp.int32)[None, :], 0), axis=1)
    outgoing = pick_panels(loaded, panel_of.astype(jnp.int32), owners)
    arrived = lax.all_to_all(outgoing, "tm", split_axis=0, concat_axis=0, tiled=True)
    me = lax.axis_index("tm")
    tags = jnp.stack([target, labels + 1])[None]
    tags = jnp.concatenate([tags, lax.ppermute(tags, "tm", flip_bit("tm", 0))])
    rest = [lax.ppermute(tags, "tm", flip("tm", i)) for i in range(2, owners, 2)]
    tags = jnp.concatenate([tags] + rest)
    loader = (jnp.arange(owners, dtype=jnp.int32) ^ me)[None, :, None]
    position = me * panels - 1 + jnp.arange(panels + 2, dtype=jnp.int32)
    found = tags[None, :, 0] == position[:, None, None]
    line = jnp.sum(jnp.where(found, tags[None, :, 1], 0), axis=(1, 2))
    source = jnp.sum(jnp.where(found[1:-1], loader, 0), axis=(1, 2)).astype(jnp.int32)
    flags = jnp.concatenate([line[1:-1] == line[:-2], line[1:-1] == line[2:]]).astype(jnp.int32)

    full_in = gather_weights(w_in, core)
    normed, lin, gate, glu = forward(arrived, source, gain, full_in, panels, 4 * LANES)
    other_normed = lax.ppermute(normed, "tm", flip_bit("tm", 0))
    glu_low, glu_high = edges(glu, 2 * RIM)

    lane_block = 2 * LANES
    column = lambda height: pl.BlockSpec((height, lane_block), lambda j, idx: (0, j))
    sizes = dict(panels=panels, length=length, taps=taps)
    padded_of = lambda lanes: pltpu.VMEM((lanes // LANES, panels, length + 2 * RIM, LANES), F32)
    up_rows = upstream.reshape(rows, width)
    up_low, up_high = edges(up_rows, RIM)
    grad_depth, grad_low, grad_high = pl.pallas_call(
        functools.partial(depth_body, **sizes),
        grid_spec=pltpu.PrefetchScalarGridSpec(
            num_scalar_prefetch=1,
            grid=(width // lane_block,),
            in_specs=[column(h) for h in (rows, 2 * RIM, 2 * RIM, rows, RIM, RIM, taps)],
            out_specs=[column(rows), column(RIM), column(RIM)],
            scratch_shapes=[
                padded_of(lane_block),
                pltpu.VMEM((lane_block // LANES, 2, 3 * RIM, LANES), F32),
            ],
        ),
        out_shape=[jax.ShapeDtypeStruct((h, width), BF) for h in (rows, RIM, RIM)],
        compiler_params=params(1, 48),
        name="depth",
    )(flags, glu, glu_low, glu_high, up_rows, up_low, up_high, kernel)
    kernel_term = pl.pallas_call(
        functools.partial(taps_body, **sizes),
        grid_spec=pltpu.PrefetchScalarGridSpec(
            num_scalar_prefetch=1,
            grid=(width // lane_block,),
            in_specs=[column(h) for h in (rows, 2 * RIM, 2 * RIM, rows)],
            out_specs=column(taps + 1),
            scratch_shapes=[padded_of(lane_block), pltpu.VMEM((taps + 1, 8, LANES), F32)],
        ),
        out_shape=jax.ShapeDtypeStruct((taps + 1, width), F32),
        compiler_params=params(1, 48),
        name="taps",
    )(flags, glu, glu_low, glu_high, grad_depth)

    piece = 2 * width // owners
    arguments = (flags, grad_depth, grad_low, grad_high, lin, gate, kernel)
    if piece % LANES == 0:
        give = gated(*arguments, piece, 2, 1 - core, sizes)
        others = [lax.ppermute(g, "tm", flip_bit("tm", 0)) for g in give]
        own = gated(*arguments, piece, 2, core, sizes)
        gradients, run = (*own, *give), piece
    else:
        gradients, run = tuple(gated(*arguments, lane_block, 1, 0, sizes)), width
        pick_parity = lambda values, parity: lax.dynamic_index_in_dim(
            values.reshape(rows, owners // 4, 2, piece), parity, 2, keepdims=False
        ).reshape(rows, width // 2)
        give = [pick_parity(g, 1 - core) for g in gradients]
        others = [lax.ppermute(g, "tm", flip_bit("tm", 0)) for g in give]
        own = [pick_parity(g, core) for g in gradients]
    grad_slots, gain_term = back(
        gradients, core, full_in, arrived, source, upstream, gain, run, 2 * LANES
    )
    returned = lax.all_to_all(grad_slots, "tm", split_axis=0, concat_axis=0, tiled=True)
    count = lax.axis_size("dp")
    bits = bits_of(count)
    shares = [
        outer_halved((normed, other_normed), (own[side], others[side]), order)
        for side, order in ((0, bits), (1, bits[::-1]))
    ]
    share = jnp.concatenate(shares, axis=1)
    share = share.reshape(width // count, owners // 2, piece).transpose(1, 0, 2)
    shard_in = sum_across(share)
    grad_loaded = pick_blocks(returned, owner_of.astype(jnp.int32), panels)
    sums = sum_everywhere(jnp.concatenate([kernel_term[:taps], gain_term], axis=0))
    return (grad_loaded[None, None], shard_in, sums[:taps], sums[taps])


def solution(mesh):
    in_specs = (
        P("dp", "tm", None, None, None),
        P("dp", "tm", None),
        P("dp", "tm", None),
        P(),
        P("dp", None),
        P(),
        P("dp", "tm", None, None, None),
    )
    out_specs = (P("dp", "tm", None, None, None), P("dp", "tm"), P(), P())
    return jax.shard_map(local, mesh=mesh, in_specs=in_specs, out_specs=out_specs, check_vma=False)
```

```python
import functools

import jax
import jax.numpy as jnp
from jax import lax
from jax.experimental import pallas as pl
from jax.experimental.pallas import tpu as pltpu
from jax.sharding import PartitionSpec as P

BF = jnp.bfloat16
F32 = jnp.float32
RIM = 16
LANES = 128
TILE = 32


def params(count, mib):
    return pltpu.CompilerParams(
        dimension_semantics=("arbitrary",) * count, vmem_limit_bytes=mib << 20
    )


def flip(axis, mask):
    return [(i, i ^ mask) for i in range(lax.axis_size(axis))]


def flip_bit(axis, bit):
    return flip(axis, 1 << bit)


def bits_of(count):
    bits = count.bit_length() - 1
    assert 1 << bits == count
    return list(range(bits))


def pick_body(index, source, target, sems, *, count):
    copies = [
        pltpu.make_async_copy(source.at[index[i]], target.at[i], sems.at[i]) for i in range(count)
    ]
    for copy in copies:
        copy.start()
    for copy in copies:
        copy.wait()


def pick_panels(source, index, count):
    _, rows, width = source.shape
    return pl.pallas_call(
        functools.partial(pick_body, count=count),
        grid_spec=pltpu.PrefetchScalarGridSpec(
            num_scalar_prefetch=1,
            grid=(1,),
            in_specs=[pl.BlockSpec(source.shape, lambda i, idx: (0, 0, 0))],
            out_specs=pl.BlockSpec(memory_space=pltpu.HBM),
            scratch_shapes=[pltpu.SemaphoreType.DMA((count,))],
        ),
        out_shape=jax.ShapeDtypeStruct((count, rows, width), source.dtype),
        compiler_params=params(1, 48),
        name="pick_panels",
    )(index, source)


def copy_body(_, source, target):
    target[...] = source[...]


def pick_blocks(source, index, count):
    _, rows, width = source.shape
    return pl.pallas_call(
        copy_body,
        grid_spec=pltpu.PrefetchScalarGridSpec(
            num_scalar_prefetch=1,
            grid=(count,),
            in_specs=[pl.BlockSpec((1, rows, width), lambda i, idx: (idx[i], 0, 0))],
            out_specs=pl.BlockSpec((1, rows, width), lambda i, idx: (i, 0, 0)),
        ),
        out_shape=jax.ShapeDtypeStruct((count, rows, width), source.dtype),
        compiler_params=params(1, 48),
        name="pick_blocks",
    )(index, source)


def gather_order(block, order):
    have = block[None]
    relative = [0]
    for bit in order:
        got = lax.ppermute(have, "dp", flip_bit("dp", bit))
        have = jnp.concatenate([have, got], axis=0)
        relative = relative + [r ^ (1 << bit) for r in relative]
    return have, relative


def gather_weights(w_in, core):
    shard, width = w_in.shape
    quarter = shard // 4
    count = lax.axis_size("dp")
    place = lax.axis_index("dp")
    bits = bits_of(count)
    half = lax.dynamic_slice_in_dim(w_in, core * (2 * quarter), 2 * quarter, axis=0)
    first, first_rel = gather_order(half[:quarter], bits)
    second, second_rel = gather_order(half[quarter:], bits[::-1])
    other_first = lax.ppermute(first, "tm", flip_bit("tm", 0))
    other_second = lax.ppermute(second, "tm", flip_bit("tm", 0))
    rels = [first_rel, second_rel]

    def out_index(side):
        index = []
        for source in range(2):
            for position in range(count):
                index.append(((place ^ rels[source][position]) * 2 + side) * 2 + source)
        return jnp.stack(index).astype(jnp.int32)

    def body(_, a, b, *rest):
        target = rest[-1]
        for number, ref in enumerate((a, b)):

            @pl.when(pl.program_id(0) == number)
            def _():
                target[...] = ref[...]

    def spec(number):
        def index(source, position, _):
            last = count - 1 if number == 0 else 0
            return (jnp.where(source == number, position, last), 0, 0)

        return pl.BlockSpec((1, quarter, width), index)

    def put(side, pair, *base):
        return pl.pallas_call(
            body,
            grid_spec=pltpu.PrefetchScalarGridSpec(
                num_scalar_prefetch=1,
                grid=(2, count),
                in_specs=[spec(0), spec(1)] + [pl.BlockSpec(memory_space=pl.ANY) for _ in base],
                out_specs=pl.BlockSpec(
                    (1, quarter, width),
                    lambda source, position, idx: (idx[source * count + position], 0, 0),
                ),
            ),
            out_shape=jax.ShapeDtypeStruct((4 * count, quarter, width), w_in.dtype),
            input_output_aliases={3: 0} if base else {},
            compiler_params=params(2, 48),
            name="put_weights",
        )(out_index(side), *pair, *base)

    full = put(core, (first, second))
    full = put(1 - core, (other_first, other_second), full)
    return full.reshape(4 * quarter * count, width)


def forward_body(source, x_hbm, gain_ref, lin_w, gate_w, parts, lin_out, gate_out, glu_out, normed, xs, sems, *, panels):
    rows = xs.shape[1]

    def fetch(s):
        return pltpu.make_async_copy(x_hbm.at[source[s]], xs.at[s], sems.at[s])

    @pl.when(pl.program_id(0) == 0)
    def _():
        for s in range(panels):
            fetch(s).start()
        for s in range(panels):
            fetch(s).wait()

            x = xs[s].astype(F32)
            x = x - jnp.mean(x, axis=1, keepdims=True)
            scale = lax.rsqrt(jnp.mean(x * x, axis=1, keepdims=True) + 1e-05)
            normed[s * rows : (s + 1) * rows, :] = (x * scale * gain_ref[...]).astype(BF)

        count, _, shard = parts.shape
        for block in range(count):
            parts[block ^ source[panels]] = normed[:, block * shard : (block + 1) * shard]

    lin = jnp.dot(normed[...], lin_w[...], preferred_element_type=F32)
    lin_out[...] = lin
    gate = jnp.dot(normed[...], gate_w[...], preferred_element_type=F32)
    gate_out[...] = gate
    glu_out[...] = (lin * jax.nn.sigmoid(gate)).astype(BF)


def forward(arrived, source, gain, full_in, panels, block):
    _, rows, width = arrived.shape
    blocks = width // block
    column = pl.BlockSpec((panels * rows, block), lambda j, idx: (0, j))
    wide = lambda dtype: jax.ShapeDtypeStruct((panels * rows, width), dtype)
    count = lax.axis_size("dp")
    parts = jax.ShapeDtypeStruct((count, panels * rows, width // count), BF)
    return pl.pallas_call(
        functools.partial(forward_body, panels=panels),
        grid_spec=pltpu.PrefetchScalarGridSpec(
            num_scalar_prefetch=1,
            grid=(blocks,),
            in_specs=[
                pl.BlockSpec(memory_space=pl.ANY),
                pl.BlockSpec((1, width), lambda j, idx: (0, 0)),
                pl.BlockSpec((width, block), lambda j, idx: (0, j)),
                pl.BlockSpec((width, block), lambda j, idx: (0, blocks + j)),
            ],
            out_specs=[
                pl.BlockSpec(parts.shape, lambda j, idx: (0, 0, 0)),
                column,
                column,
                column,
            ],
            scratch_shapes=[
                pltpu.VMEM((panels * rows, width), BF),
                pltpu.VMEM((panels, rows, width), BF),
                pltpu.SemaphoreType.DMA((panels,)),
            ],
        ),
        out_shape=[parts, wide(F32), wide(F32), wide(BF)],
        compiler_params=params(1, 48),
        name="forward",
    )(jnp.append(source, lax.axis_index("dp")), arrived, gain.reshape(1, width), full_in, full_in)


def fill_padded(flags, padded, main, low, high, panels, length):
    for s in range(panels):
        at = s * length
        middle = main[at : at + length, :].astype(F32)
        before = low[low.shape[0] - RIM :, :] if s == 0 else main[at - RIM : at, :]
        after = high[:RIM, :] if s == panels - 1 else main[at + length : at + length + RIM, :]
        before = jnp.where(flags[s] > 0, before.astype(F32), 0.0)
        after = jnp.where(flags[panels + s] > 0, after.astype(F32), 0.0)
        for chunk in range(main.shape[1] // LANES):
            lanes = slice(chunk * LANES, (chunk + 1) * LANES)
            padded[chunk, s, RIM : RIM + length, :] = middle[:, lanes]
            padded[chunk, s, 0:RIM, :] = before[:, lanes]
            padded[chunk, s, RIM + length :, :] = after[:, lanes]


def shifted_sum(padded, weights, chunk, s, start, taps, flip, height=TILE):
    lanes = pl.ds(chunk * LANES, LANES)
    total = jnp.zeros((height, LANES), F32)
    for tap in range(taps):
        offset = taps - tap if flip else tap + 1
        view = padded[chunk, s, pl.ds(start + offset, height), :]
        total = total + weights[pl.ds(tap, 1), lanes] * view
    return total


def tiles(width, panels, length, work):
    for chunk in range(width // LANES):

        def step(s, carry):
            for start in range(0, length, TILE):
                rows = pl.ds(pl.multiple_of(s * length + start, TILE), TILE)
                work(chunk, s, start, rows, pl.ds(chunk * LANES, LANES))
            return carry

        lax.fori_loop(0, panels, step, 0)


def depth_body(
    flags, glu, low, high, upstream, up_low, up_high, weights, out, out_low, out_high, padded, ends, *, panels, length, taps
):
    fill_padded(flags, padded, glu, low, high, panels, length)
    rows = panels * length

    def grad(depth, up):
        sig = jax.nn.sigmoid(depth)
        return (up.astype(F32) * sig * (1.0 + depth * (1.0 - sig))).astype(BF)

    for chunk in range(glu.shape[1] // LANES):
        lanes = slice(chunk * LANES, (chunk + 1) * LANES)
        ends[chunk, 0, 0 : 2 * RIM, :] = low[:, lanes].astype(F32)
        ends[chunk, 0, 2 * RIM :, :] = glu[0:RIM, lanes].astype(F32)
        ends[chunk, 1, 0:RIM, :] = glu[rows - RIM : rows, lanes].astype(F32)
        ends[chunk, 1, RIM:, :] = high[:, lanes].astype(F32)
        for side, up, to in ((0, up_low, out_low), (1, up_high, out_high)):
            depth = shifted_sum(ends, weights, chunk, side, 0, taps, False, RIM)
            to[:, lanes] = grad(depth, up[:, lanes])

    def work(chunk, s, start, at, lanes):
        depth = shifted_sum(padded, weights, chunk, s, start, taps, False)
        out[at, lanes] = grad(depth, upstream[at, lanes])

    tiles(glu.shape[1], panels, length, work)


def taps_body(flags, glu, low, high, grad, out, padded, partial, *, panels, length, taps):
    fill_padded(flags, padded, glu, low, high, panels, length)
    for chunk in range(glu.shape[1] // LANES):
        lanes = pl.ds(chunk * LANES, LANES)
        partial[...] = jnp.zeros_like(partial)

        def step(s, carry):
            rows = pl.ds(pl.multiple_of(s * length, length), length)
            g = grad[rows, lanes].astype(F32)
            for tap in range(taps):
                product = g * padded[chunk, s, pl.ds(tap + 1, length), :]
                partial[tap] += jnp.sum(product.reshape(length // 8, 8, LANES), axis=0)
            return carry

        lax.fori_loop(0, panels, step, 0)
        out[:, lanes] = jnp.sum(partial[...], axis=1)


def gated_body(flags, grad, low, high, lin, gate, weights, *refs, panels, length, taps, steps):
    *outs, padded = refs
    fill_padded(flags, padded, grad, low, high, panels, length)

    def run(first, second):
        def work(chunk, s, start, rows, lanes):
            total = shifted_sum(padded, weights, chunk, s, start, taps, True)
            sig = jax.nn.sigmoid(gate[rows, lanes])
            scaled = total * sig
            first[rows, lanes] = scaled.astype(BF)
            second[rows, lanes] = (scaled * lin[rows, lanes] * (1.0 - sig)).astype(BF)

        tiles(grad.shape[1], panels, length, work)

    for part in range(len(outs) // 2):

        @pl.when(pl.program_id(0) // steps == part)
        def _():
            run(*outs[2 * part : 2 * part + 2])


def gated(flags, grad_depth, low, high, lin, gate, kernel, block, parts, core, sizes):
    rows, width = grad_depth.shape
    panels = sizes["panels"]
    steps = width // block // parts

    def column(height):
        def index(j, idx):
            if parts == 1:
                return (0, j)
            parity = jnp.where(j < steps, 1 - idx[2 * panels], idx[2 * panels])
            return (0, 2 * (j % steps) + parity)

        return pl.BlockSpec((height, block), index)

    def out(part):
        return pl.BlockSpec((rows, block), lambda j, idx: (0, jnp.clip(j - part * steps, 0, steps - 1)))

    return pl.pallas_call(
        functools.partial(gated_body, steps=steps, **sizes),
        grid_spec=pltpu.PrefetchScalarGridSpec(
            num_scalar_prefetch=1,
            grid=(parts * steps,),
            in_specs=[column(h) for h in (rows, RIM, RIM, rows, rows, kernel.shape[0])],
            out_specs=[out(part) for part in range(parts) for _ in range(2)],
            scratch_shapes=[
                pltpu.VMEM((block // LANES, panels, sizes["length"] + 2 * RIM, LANES), F32)
            ],
        ),
        out_shape=[jax.ShapeDtypeStruct((rows, width // parts), BF)] * (2 * parts),
        compiler_params=params(1, 48),
        name="gated",
    )(jnp.append(flags, core), grad_depth, low, high, lin, gate, kernel)


def back_body(source, *refs, grads, block, panels, piece):
    gradients = refs[:grads]
    w_ref, x_hbm, up_hbm, gain_ref, out_hbm, gain_out, total, xs, ups, outs, sems = refs[grads:]
    step = pl.program_id(0)

    def fetch(s):
        return (
            pltpu.make_async_copy(x_hbm.at[source[s]], xs.at[s], sems.at[s]),
            pltpu.make_async_copy(up_hbm.at[s], ups.at[s], sems.at[panels + s]),
        )

    def put(s):
        return pltpu.make_async_copy(outs.at[s], out_hbm.at[source[s]], sems.at[2 * panels + s])

    @pl.when(step == 0)
    def _():
        for s in range(panels):
            for copy in fetch(s):
                copy.start()

    acc = None
    for number, grad in enumerate(gradients):
        pieces = grad.shape[1] // piece
        for i in range(pieces):
            column = (number % 2 * pieces + i) * (grads // 2) * piece
            if grads > 2:
                column = column + (source[panels] ^ (number // 2)) * piece
                column = pl.multiple_of(column, LANES)
            term = lax.dot_general(
                grad[:, i * piece : (i + 1) * piece],
                w_ref[:, pl.ds(column, piece)],
                (((1,), (1,)), ((), ())),
                preferred_element_type=F32,
            )
            acc = term if acc is None else acc + term
    total[:, pl.ds(pl.multiple_of(step * block, block), block)] = acc

    @pl.when(step == pl.num_programs(0) - 1)
    def _():
        rows = xs.shape[1]
        gain = gain_ref[...]
        gain_sum = jnp.zeros_like(gain)
        for s in range(panels):
            for copy in fetch(s):
                copy.wait()

            x = xs[s].astype(F32)
            x = x - jnp.mean(x, axis=1, keepdims=True)
            scale = lax.rsqrt(jnp.mean(x * x, axis=1, keepdims=True) + 1e-05)
            unit = x * scale
            g = total[s * rows : (s + 1) * rows, :]
            gain_sum = gain_sum + jnp.sum(g * unit, axis=0, keepdims=True)
            q = g * gain
            mean_q = jnp.mean(q, axis=1, keepdims=True)
            mean_u = jnp.mean(q * unit, axis=1, keepdims=True)
            outs[s] = (ups[s].astype(F32) + scale * (q - mean_q - unit * mean_u)).astype(BF)
            put(s).start()
        gain_out[...] = gain_sum
        for s in range(panels):
            put(s).wait()


def back(gradients, core, full_in, arrived, source, upstream, gain, piece, block):
    _, rows, width = arrived.shape
    panels = upstream.shape[0]
    constant = lambda rank: (lambda n, idx: (0,) * rank)
    hbm = pl.BlockSpec(memory_space=pl.ANY)
    panel_scratch = pltpu.VMEM((panels, rows, width), BF)
    return pl.pallas_call(
        functools.partial(back_body, grads=len(gradients), block=block, panels=panels, piece=piece),
        grid_spec=pltpu.PrefetchScalarGridSpec(
            num_scalar_prefetch=1,
            grid=(width // block,),
            in_specs=[pl.BlockSpec(g.shape, constant(2)) for g in gradients]
            + [
                pl.BlockSpec((block, full_in.shape[1]), lambda n, idx: (n, 0)),
                hbm,
                hbm,
                pl.BlockSpec((1, width), constant(2)),
            ],
            out_specs=[hbm, pl.BlockSpec((1, width), constant(2))],
            scratch_shapes=[
                pltpu.VMEM((panels * rows, width), F32),
                panel_scratch,
                panel_scratch,
                panel_scratch,
                pltpu.SemaphoreType.DMA((3 * panels,)),
            ],
        ),
        out_shape=[
            jax.ShapeDtypeStruct(arrived.shape, BF),
            jax.ShapeDtypeStruct((1, width), F32),
        ],
        compiler_params=params(1, 48),
        name="back",
    )(jnp.append(source, core), *gradients, full_in, arrived, upstream, gain.reshape(1, width))


def outer_sum(lefts, rights):
    terms = [
        lax.dot_general(a, b, (((1,), (0,)), ((), ())), preferred_element_type=F32)
        for a, b in zip(lefts, rights)
    ]
    return (terms[0] + terms[1]).astype(BF)


def outer_halved(lefts, rights, order):
    count = lefts[0].shape[0]
    rels = sorted(range(count), key=lambda r: [(r >> bit) & 1 for bit in order])
    half = count // 2
    pick = lambda left, some: jnp.concatenate([left[r : r + 1] for r in some])
    send = outer_sum([pick(left, rels[half:]) for left in lefts], rights)
    keep = outer_sum([pick(left, rels[:half]) for left in lefts], rights)
    add = lambda a, b: (a.astype(F32) + b.astype(F32)).astype(BF)
    for bit in order:
        got = lax.ppermute(send, "dp", flip_bit("dp", bit))
        half = half // 2
        if half:
            send = add(keep[half:], got[half:])
            keep = add(keep[:half], got[:half])
        else:
            keep = add(keep, got)
    return keep[0]


def sum_everywhere(values):
    for bit in bits_of(lax.axis_size("dp")):
        values = values + lax.ppermute(values, "dp", flip_bit("dp", bit))
    halves = values.reshape(2, values.shape[0] // 2, values.shape[1])
    core = lax.axis_index("tm") % 2
    send = lax.dynamic_index_in_dim(halves, 1 - core, 0, keepdims=False)
    keep = lax.dynamic_index_in_dim(halves, core, 0, keepdims=False)
    values = (keep + lax.ppermute(send, "tm", flip_bit("tm", 0))).astype(BF)
    terms = [values]
    for mask in range(2, lax.axis_size("tm"), 2):
        terms.append(lax.ppermute(values, "tm", flip("tm", mask)))
    terms = [term.astype(F32) for term in terms]
    while len(terms) > 1:
        terms = [a + b for a, b in zip(terms[::2], terms[1::2])]
    values = terms[0]
    got = lax.ppermute(values, "tm", flip_bit("tm", 0))
    return jnp.concatenate([jnp.where(core == 0, values, got), jnp.where(core == 0, got, values)])


def sum_across(share):
    place = lax.axis_index("tm") // 2
    for bit in bits_of(share.shape[0]):
        pairs = share.reshape(share.shape[0] // 2, 2, *share.shape[1:])
        mine = (place >> bit) & 1
        send = lax.dynamic_index_in_dim(pairs, 1 - mine, 1, keepdims=False).astype(BF)
        keep = lax.dynamic_index_in_dim(pairs, mine, 1, keepdims=False)
        got = lax.ppermute(send, "tm", flip("tm", 2 << bit))
        share = keep.astype(F32) + got.astype(F32)
    return share[0]


def edges(values, width):
    count = lax.axis_size("tm")
    low = lax.ppermute(values[-width:], "tm", [(i, i + 1) for i in range(count - 1)])
    high = lax.ppermute(values[:width], "tm", [(i + 1, i) for i in range(count - 1)])
    return low, high


def local(frames, route, utterance, gain, w_in, kernel, cotangent):
    panels, length, width = frames.shape[2:]
    owners = lax.axis_size("tm")
    rows = panels * length
    taps = kernel.shape[0]
    reach = taps // 2
    assert reach < RIM and taps == 31
    loaded = frames[0, 0]
    target = route[0, 0]
    labels = utterance[0, 0]
    upstream = cotangent[0, 0]
    core = lax.axis_index("tm") % 2
    owner_of = target // panels
    pick = owner_of[None, :] == jnp.arange(owners, dtype=jnp.int32)[:, None]
    panel_of = jnp.sum(jnp.where(pick, jnp.arange(panels, dtype=jnp.int32)[None, :], 0), axis=1)
    outgoing = pick_panels(loaded, panel_of.astype(jnp.int32), owners)
    arrived = lax.all_to_all(outgoing, "tm", split_axis=0, concat_axis=0, tiled=True)
    me = lax.axis_index("tm")
    tags = jnp.stack([target, labels + 1])[None]
    tags = jnp.concatenate([tags, lax.ppermute(tags, "tm", flip_bit("tm", 0))])
    rest = [lax.ppermute(tags, "tm", flip("tm", i)) for i in range(2, owners, 2)]
    tags = jnp.concatenate([tags] + rest)
    loader = (jnp.arange(owners, dtype=jnp.int32) ^ me)[None, :, None]
    position = me * panels - 1 + jnp.arange(panels + 2, dtype=jnp.int32)
    found = tags[None, :, 0] == position[:, None, None]
    line = jnp.sum(jnp.where(found, tags[None, :, 1], 0), axis=(1, 2))
    source = jnp.sum(jnp.where(found[1:-1], loader, 0), axis=(1, 2)).astype(jnp.int32)
    flags = jnp.concatenate([line[1:-1] == line[:-2], line[1:-1] == line[2:]]).astype(jnp.int32)

    full_in = gather_weights(w_in, core)
    normed, lin, gate, glu = forward(arrived, source, gain, full_in, panels, 4 * LANES)
    other_normed = lax.ppermute(normed, "tm", flip_bit("tm", 0))
    glu_low, glu_high = edges(glu, 2 * RIM)

    lane_block = 2 * LANES
    column = lambda height: pl.BlockSpec((height, lane_block), lambda j, idx: (0, j))
    sizes = dict(panels=panels, length=length, taps=taps)
    padded_of = lambda lanes: pltpu.VMEM((lanes // LANES, panels, length + 2 * RIM, LANES), F32)
    up_rows = upstream.reshape(rows, width)
    up_low, up_high = edges(up_rows, RIM)
    grad_depth, grad_low, grad_high = pl.pallas_call(
        functools.partial(depth_body, **sizes),
        grid_spec=pltpu.PrefetchScalarGridSpec(
            num_scalar_prefetch=1,
            grid=(width // lane_block,),
            in_specs=[column(h) for h in (rows, 2 * RIM, 2 * RIM, rows, RIM, RIM, taps)],
            out_specs=[column(rows), column(RIM), column(RIM)],
            scratch_shapes=[
                padded_of(lane_block),
                pltpu.VMEM((lane_block // LANES, 2, 3 * RIM, LANES), F32),
            ],
        ),
        out_shape=[jax.ShapeDtypeStruct((h, width), BF) for h in (rows, RIM, RIM)],
        compiler_params=params(1, 48),
        name="depth",
    )(flags, glu, glu_low, glu_high, up_rows, up_low, up_high, kernel)
    kernel_term = pl.pallas_call(
        functools.partial(taps_body, **sizes),
        grid_spec=pltpu.PrefetchScalarGridSpec(
            num_scalar_prefetch=1,
            grid=(width // lane_block,),
            in_specs=[column(h) for h in (rows, 2 * RIM, 2 * RIM, rows)],
            out_specs=column(taps + 1),
            scratch_shapes=[padded_of(lane_block), pltpu.VMEM((taps + 1, 8, LANES), F32)],
        ),
        out_shape=jax.ShapeDtypeStruct((taps + 1, width), F32),
        compiler_params=params(1, 48),
        name="taps",
    )(flags, glu, glu_low, glu_high, grad_depth)

    piece = 2 * width // owners
    arguments = (flags, grad_depth, grad_low, grad_high, lin, gate, kernel)
    if piece % LANES == 0:
        *give, own_lin, own_gate = gated(*arguments, piece, 2, core, sizes)
        own = (own_lin, own_gate)
        others = [lax.ppermute(g, "tm", flip_bit("tm", 0)) for g in give]
        gradients, run = (*own, *give), piece
    else:
        gradients, run = tuple(gated(*arguments, lane_block, 1, core, sizes)), width
        pick_parity = lambda values, parity: lax.dynamic_index_in_dim(
            values.reshape(rows, owners // 4, 2, piece), parity, 2, keepdims=False
        ).reshape(rows, width // 2)
        give = [pick_parity(g, 1 - core) for g in gradients]
        others = [lax.ppermute(g, "tm", flip_bit("tm", 0)) for g in give]
        own = [pick_parity(g, core) for g in gradients]
    grad_slots, gain_term = back(
        gradients, core, full_in, arrived, source, upstream, gain, run, 2 * LANES
    )
    returned = lax.all_to_all(grad_slots, "tm", split_axis=0, concat_axis=0, tiled=True)
    count = lax.axis_size("dp")
    bits = bits_of(count)
    shares = [
        outer_halved((normed, other_normed), (own[side], others[side]), order)
        for side, order in ((0, bits), (1, bits[::-1]))
    ]
    share = jnp.concatenate(shares, axis=1)
    share = share.reshape(width // count, owners // 2, piece).transpose(1, 0, 2)
    shard_in = sum_across(share)
    grad_loaded = pick_blocks(returned, owner_of.astype(jnp.int32), panels)
    sums = sum_everywhere(jnp.concatenate([kernel_term[:taps], gain_term], axis=0))
    return (grad_loaded[None, None], shard_in, sums[:taps], sums[taps])


def solution(mesh):
    in_specs = (
        P("dp", "tm", None, None, None),
        P("dp", "tm", None),
        P("dp", "tm", None),
        P(),
        P("dp", None),
        P(),
        P("dp", "tm", None, None, None),
    )
    out_specs = (P("dp", "tm", None, None, None), P("dp", "tm"), P(), P())
    return jax.shard_map(local, mesh=mesh, in_specs=in_specs, out_specs=out_specs, check_vma=False)
```

```python
import functools

import jax
import jax.numpy as jnp
from jax import lax
from jax.experimental import pallas as pl
from jax.experimental.pallas import tpu as pltpu
from jax.sharding import PartitionSpec as P

BF = jnp.bfloat16
F32 = jnp.float32
RIM = 16
LANES = 128
TILE = 32


def params(count, mib):
    return pltpu.CompilerParams(
        dimension_semantics=("arbitrary",) * count, vmem_limit_bytes=mib << 20
    )


def flip(axis, mask):
    return [(i, i ^ mask) for i in range(lax.axis_size(axis))]


def flip_bit(axis, bit):
    return flip(axis, 1 << bit)


def bits_of(count):
    bits = count.bit_length() - 1
    assert 1 << bits == count
    return list(range(bits))


def pick_body(index, source, target, sems, *, count):
    copies = [
        pltpu.make_async_copy(source.at[index[i]], target.at[i], sems.at[i]) for i in range(count)
    ]
    for copy in copies:
        copy.start()
    for copy in copies:
        copy.wait()


def pick_panels(source, index, count):
    _, rows, width = source.shape
    return pl.pallas_call(
        functools.partial(pick_body, count=count),
        grid_spec=pltpu.PrefetchScalarGridSpec(
            num_scalar_prefetch=1,
            grid=(1,),
            in_specs=[pl.BlockSpec(source.shape, lambda i, idx: (0, 0, 0))],
            out_specs=pl.BlockSpec(memory_space=pltpu.HBM),
            scratch_shapes=[pltpu.SemaphoreType.DMA((count,))],
        ),
        out_shape=jax.ShapeDtypeStruct((count, rows, width), source.dtype),
        compiler_params=params(1, 48),
        name="pick_panels",
    )(index, source)


def copy_body(_, source, target):
    target[...] = source[...]


def pick_blocks(source, index, count):
    _, rows, width = source.shape
    return pl.pallas_call(
        copy_body,
        grid_spec=pltpu.PrefetchScalarGridSpec(
            num_scalar_prefetch=1,
            grid=(count,),
            in_specs=[pl.BlockSpec((1, rows, width), lambda i, idx: (idx[i], 0, 0))],
            out_specs=pl.BlockSpec((1, rows, width), lambda i, idx: (i, 0, 0)),
        ),
        out_shape=jax.ShapeDtypeStruct((count, rows, width), source.dtype),
        compiler_params=params(1, 48),
        name="pick_blocks",
    )(index, source)


def gather_order(block, order):
    have = block[None]
    relative = [0]
    for bit in order:
        got = lax.ppermute(have, "dp", flip_bit("dp", bit))
        have = jnp.concatenate([have, got], axis=0)
        relative = relative + [r ^ (1 << bit) for r in relative]
    return have, relative


def gather_weights(w_in, core):
    shard, width = w_in.shape
    quarter = shard // 4
    count = lax.axis_size("dp")
    place = lax.axis_index("dp")
    bits = bits_of(count)
    half = lax.dynamic_slice_in_dim(w_in, core * (2 * quarter), 2 * quarter, axis=0)
    first, first_rel = gather_order(half[:quarter], bits)
    second, second_rel = gather_order(half[quarter:], bits[::-1])
    other_first = lax.ppermute(first, "tm", flip_bit("tm", 0))
    other_second = lax.ppermute(second, "tm", flip_bit("tm", 0))
    rels = [first_rel, second_rel]

    def out_index(side):
        index = []
        for source in range(2):
            for position in range(count):
                index.append(((place ^ rels[source][position]) * 2 + side) * 2 + source)
        return jnp.stack(index).astype(jnp.int32)

    def body(_, a, b, *rest):
        target = rest[-1]
        for number, ref in enumerate((a, b)):

            @pl.when(pl.program_id(0) == number)
            def _():
                target[...] = ref[...]

    def spec(number):
        def index(source, position, _):
            last = count - 1 if number == 0 else 0
            return (jnp.where(source == number, position, last), 0, 0)

        return pl.BlockSpec((1, quarter, width), index)

    def put(side, pair, *base):
        return pl.pallas_call(
            body,
            grid_spec=pltpu.PrefetchScalarGridSpec(
                num_scalar_prefetch=1,
                grid=(2, count),
                in_specs=[spec(0), spec(1)] + [pl.BlockSpec(memory_space=pl.ANY) for _ in base],
                out_specs=pl.BlockSpec(
                    (1, quarter, width),
                    lambda source, position, idx: (idx[source * count + position], 0, 0),
                ),
            ),
            out_shape=jax.ShapeDtypeStruct((4 * count, quarter, width), w_in.dtype),
            input_output_aliases={3: 0} if base else {},
            compiler_params=params(2, 48),
            name="put_weights",
        )(out_index(side), *pair, *base)

    full = put(core, (first, second))
    full = put(1 - core, (other_first, other_second), full)
    return full.reshape(4 * quarter * count, width)


def forward_body(source, x_hbm, gain_ref, lin_w, gate_w, parts, lin_out, gate_out, glu_out, normed, xs, sems, *, panels):
    rows = xs.shape[1]

    def fetch(s):
        return pltpu.make_async_copy(x_hbm.at[source[s]], xs.at[s], sems.at[s])

    @pl.when(pl.program_id(0) == 0)
    def _():
        for s in range(panels):
            fetch(s).start()
        for s in range(panels):
            fetch(s).wait()

            x = xs[s].astype(F32)
            x = x - jnp.mean(x, axis=1, keepdims=True)
            scale = lax.rsqrt(jnp.mean(x * x, axis=1, keepdims=True) + 1e-05)
            normed[s * rows : (s + 1) * rows, :] = (x * scale * gain_ref[...]).astype(BF)

        count, _, shard = parts.shape
        for block in range(count):
            parts[block ^ source[panels]] = normed[:, block * shard : (block + 1) * shard]

    lin = jnp.dot(normed[...], lin_w[...], preferred_element_type=F32)
    lin_out[...] = lin
    gate = jnp.dot(normed[...], gate_w[...], preferred_element_type=F32)
    gate_out[...] = gate
    glu_out[...] = (lin * jax.nn.sigmoid(gate)).astype(BF)


def forward(arrived, source, gain, full_in, panels, block):
    _, rows, width = arrived.shape
    blocks = width // block
    column = pl.BlockSpec((panels * rows, block), lambda j, idx: (0, j))
    wide = lambda dtype: jax.ShapeDtypeStruct((panels * rows, width), dtype)
    count = lax.axis_size("dp")
    parts = jax.ShapeDtypeStruct((count, panels * rows, width // count), BF)
    return pl.pallas_call(
        functools.partial(forward_body, panels=panels),
        grid_spec=pltpu.PrefetchScalarGridSpec(
            num_scalar_prefetch=1,
            grid=(blocks,),
            in_specs=[
                pl.BlockSpec(memory_space=pl.ANY),
                pl.BlockSpec((1, width), lambda j, idx: (0, 0)),
                pl.BlockSpec((width, block), lambda j, idx: (0, j)),
                pl.BlockSpec((width, block), lambda j, idx: (0, blocks + j)),
            ],
            out_specs=[
                pl.BlockSpec(parts.shape, lambda j, idx: (0, 0, 0)),
                column,
                column,
                column,
            ],
            scratch_shapes=[
                pltpu.VMEM((panels * rows, width), BF),
                pltpu.VMEM((panels, rows, width), BF),
                pltpu.SemaphoreType.DMA((panels,)),
            ],
        ),
        out_shape=[parts, wide(F32), wide(F32), wide(BF)],
        compiler_params=params(1, 48),
        name="forward",
    )(jnp.append(source, lax.axis_index("dp")), arrived, gain.reshape(1, width), full_in, full_in)


def fill_padded(flags, padded, main, low, high, panels, length):
    for s in range(panels):
        at = s * length
        middle = main[at : at + length, :].astype(F32)
        before = low[low.shape[0] - RIM :, :] if s == 0 else main[at - RIM : at, :]
        after = high[:RIM, :] if s == panels - 1 else main[at + length : at + length + RIM, :]
        before = jnp.where(flags[s] > 0, before.astype(F32), 0.0)
        after = jnp.where(flags[panels + s] > 0, after.astype(F32), 0.0)
        for chunk in range(main.shape[1] // LANES):
            lanes = slice(chunk * LANES, (chunk + 1) * LANES)
            padded[chunk, s, RIM : RIM + length, :] = middle[:, lanes]
            padded[chunk, s, 0:RIM, :] = before[:, lanes]
            padded[chunk, s, RIM + length :, :] = after[:, lanes]


def shifted_sum(padded, weights, chunk, s, start, taps, flip, height=TILE):
    lanes = pl.ds(chunk * LANES, LANES)
    total = jnp.zeros((height, LANES), F32)
    for tap in range(taps):
        offset = taps - tap if flip else tap + 1
        view = padded[chunk, s, pl.ds(start + offset, height), :]
        total = total + weights[pl.ds(tap, 1), lanes] * view
    return total


def tiles(width, panels, length, work):
    for chunk in range(width // LANES):

        def step(s, carry):
            for start in range(0, length, TILE):
                rows = pl.ds(pl.multiple_of(s * length + start, TILE), TILE)
                work(chunk, s, start, rows, pl.ds(chunk * LANES, LANES))
            return carry

        lax.fori_loop(0, panels, step, 0)


def depth_body(
    flags, glu, low, high, upstream, up_low, up_high, weights, out, out_low, out_high, padded, ends, *, panels, length, taps
):
    fill_padded(flags, padded, glu, low, high, panels, length)
    rows = panels * length

    def grad(depth, up):
        sig = jax.nn.sigmoid(depth)
        return (up.astype(F32) * sig * (1.0 + depth * (1.0 - sig))).astype(BF)

    for chunk in range(glu.shape[1] // LANES):
        lanes = slice(chunk * LANES, (chunk + 1) * LANES)
        ends[chunk, 0, 0 : 2 * RIM, :] = low[:, lanes].astype(F32)
        ends[chunk, 0, 2 * RIM :, :] = glu[0:RIM, lanes].astype(F32)
        ends[chunk, 1, 0:RIM, :] = glu[rows - RIM : rows, lanes].astype(F32)
        ends[chunk, 1, RIM:, :] = high[:, lanes].astype(F32)
        for side, up, to in ((0, up_low, out_low), (1, up_high, out_high)):
            depth = shifted_sum(ends, weights, chunk, side, 0, taps, False, RIM)
            to[:, lanes] = grad(depth, up[:, lanes])

    def work(chunk, s, start, at, lanes):
        depth = shifted_sum(padded, weights, chunk, s, start, taps, False)
        out[at, lanes] = grad(depth, upstream[at, lanes])

    tiles(glu.shape[1], panels, length, work)


def taps_body(flags, glu, low, high, grad, out, padded, partial, *, panels, length, taps):
    fill_padded(flags, padded, glu, low, high, panels, length)
    for chunk in range(glu.shape[1] // LANES):
        lanes = pl.ds(chunk * LANES, LANES)
        partial[...] = jnp.zeros_like(partial)

        def step(s, carry):
            rows = pl.ds(pl.multiple_of(s * length, length), length)
            g = grad[rows, lanes].astype(F32)
            for tap in range(taps):
                product = g * padded[chunk, s, pl.ds(tap + 1, length), :]
                partial[tap] += jnp.sum(product.reshape(length // 8, 8, LANES), axis=0)
            return carry

        lax.fori_loop(0, panels, step, 0)
        out[:, lanes] = jnp.sum(partial[...], axis=1)


def gated_body(flags, grad, low, high, lin, gate, weights, *refs, panels, length, taps, steps):
    *outs, padded = refs
    fill_padded(flags, padded, grad, low, high, panels, length)

    def run(first, second):
        def work(chunk, s, start, rows, lanes):
            total = shifted_sum(padded, weights, chunk, s, start, taps, True)
            sig = jax.nn.sigmoid(gate[rows, lanes])
            scaled = total * sig
            first[rows, lanes] = scaled.astype(BF)
            second[rows, lanes] = (scaled * lin[rows, lanes] * (1.0 - sig)).astype(BF)

        tiles(grad.shape[1], panels, length, work)

    for part in range(len(outs) // 2):

        @pl.when(pl.program_id(0) // steps == part)
        def _():
            run(*outs[2 * part : 2 * part + 2])


def gated(flags, grad_depth, low, high, lin, gate, kernel, block, parts, core, sizes):
    rows, width = grad_depth.shape
    panels = sizes["panels"]
    steps = width // block // parts

    def column(height):
        def index(j, idx):
            if parts == 1:
                return (0, j)
            parity = jnp.where(j < steps, 1 - idx[2 * panels], idx[2 * panels])
            return (0, 2 * (j % steps) + parity)

        return pl.BlockSpec((height, block), index)

    def out(part):
        return pl.BlockSpec((rows, block), lambda j, idx: (0, jnp.clip(j - part * steps, 0, steps - 1)))

    return pl.pallas_call(
        functools.partial(gated_body, steps=steps, **sizes),
        grid_spec=pltpu.PrefetchScalarGridSpec(
            num_scalar_prefetch=1,
            grid=(parts * steps,),
            in_specs=[column(h) for h in (rows, RIM, RIM, rows, rows, kernel.shape[0])],
            out_specs=[out(part) for part in range(parts) for _ in range(2)],
            scratch_shapes=[
                pltpu.VMEM((block // LANES, panels, sizes["length"] + 2 * RIM, LANES), F32)
            ],
        ),
        out_shape=[jax.ShapeDtypeStruct((rows, width // parts), BF)] * (2 * parts),
        compiler_params=params(1, 48),
        name="gated",
    )(jnp.append(flags, core), grad_depth, low, high, lin, gate, kernel)


def back_body(source, *refs, grads, block, panels, piece):
    gradients = refs[:grads]
    w_ref, x_hbm, up_hbm, gain_ref, out_hbm, gain_out, total, xs, ups, outs, sems = refs[grads:]
    step = pl.program_id(0)

    def fetch(s):
        return (
            pltpu.make_async_copy(x_hbm.at[source[s]], xs.at[s], sems.at[s]),
            pltpu.make_async_copy(up_hbm.at[s], ups.at[s], sems.at[panels + s]),
        )

    def put(s):
        return pltpu.make_async_copy(outs.at[s], out_hbm.at[source[s]], sems.at[2 * panels + s])

    @pl.when(step == 0)
    def _():
        for s in range(panels):
            for copy in fetch(s):
                copy.start()

    acc = None
    for number, grad in enumerate(gradients):
        pieces = grad.shape[1] // piece
        for i in range(pieces):
            column = (number % 2 * pieces + i) * (grads // 2) * piece
            if grads > 2:
                column = column + (source[panels] ^ (number // 2)) * piece
                column = pl.multiple_of(column, LANES)
            term = lax.dot_general(
                grad[:, i * piece : (i + 1) * piece],
                w_ref[:, pl.ds(column, piece)],
                (((1,), (1,)), ((), ())),
                preferred_element_type=F32,
            )
            acc = term if acc is None else acc + term
    total[:, pl.ds(pl.multiple_of(step * block, block), block)] = acc

    @pl.when(step == pl.num_programs(0) - 1)
    def _():
        rows = xs.shape[1]
        gain = gain_ref[...]
        gain_sum = jnp.zeros_like(gain)
        for s in range(panels):
            for copy in fetch(s):
                copy.wait()

            x = xs[s].astype(F32)
            x = x - jnp.mean(x, axis=1, keepdims=True)
            scale = lax.rsqrt(jnp.mean(x * x, axis=1, keepdims=True) + 1e-05)
            unit = x * scale
            g = total[s * rows : (s + 1) * rows, :]
            gain_sum = gain_sum + jnp.sum(g * unit, axis=0, keepdims=True)
            q = g * gain
            mean_q = jnp.mean(q, axis=1, keepdims=True)
            mean_u = jnp.mean(q * unit, axis=1, keepdims=True)
            outs[s] = (ups[s].astype(F32) + scale * (q - mean_q - unit * mean_u)).astype(BF)
            put(s).start()
        gain_out[...] = gain_sum
        for s in range(panels):
            put(s).wait()


def back(gradients, core, full_in, arrived, source, upstream, gain, piece, block):
    _, rows, width = arrived.shape
    panels = upstream.shape[0]
    constant = lambda rank: (lambda n, idx: (0,) * rank)
    hbm = pl.BlockSpec(memory_space=pl.ANY)
    panel_scratch = pltpu.VMEM((panels, rows, width), BF)
    return pl.pallas_call(
        functools.partial(back_body, grads=len(gradients), block=block, panels=panels, piece=piece),
        grid_spec=pltpu.PrefetchScalarGridSpec(
            num_scalar_prefetch=1,
            grid=(width // block,),
            in_specs=[pl.BlockSpec(g.shape, constant(2)) for g in gradients]
            + [
                pl.BlockSpec((block, full_in.shape[1]), lambda n, idx: (n, 0)),
                hbm,
                hbm,
                pl.BlockSpec((1, width), constant(2)),
            ],
            out_specs=[hbm, pl.BlockSpec((1, width), constant(2))],
            scratch_shapes=[
                pltpu.VMEM((panels * rows, width), F32),
                panel_scratch,
                panel_scratch,
                panel_scratch,
                pltpu.SemaphoreType.DMA((3 * panels,)),
            ],
        ),
        out_shape=[
            jax.ShapeDtypeStruct(arrived.shape, BF),
            jax.ShapeDtypeStruct((1, width), F32),
        ],
        compiler_params=params(1, 48),
        name="back",
    )(jnp.append(source, core), *gradients, full_in, arrived, upstream, gain.reshape(1, width))


def outer_sum(lefts, rights):
    terms = [
        lax.dot_general(a, b, (((1,), (0,)), ((), ())), preferred_element_type=F32)
        for a, b in zip(lefts, rights)
    ]
    return (terms[0] + terms[1]).astype(BF)


def outer_halved(lefts, rights, order):
    count = lefts[0].shape[0]
    rels = sorted(range(count), key=lambda r: [(r >> bit) & 1 for bit in order])
    half = count // 2
    pick = lambda left, some: jnp.concatenate([left[r : r + 1] for r in some])
    send = outer_sum([pick(left, rels[half:]) for left in lefts], rights)
    keep = outer_sum([pick(left, rels[:half]) for left in lefts], rights)
    add = lambda a, b: (a.astype(F32) + b.astype(F32)).astype(BF)
    for bit in order:
        got = lax.ppermute(send, "dp", flip_bit("dp", bit))
        half = half // 2
        if half:
            send = add(keep[half:], got[half:])
            keep = add(keep[:half], got[:half])
        else:
            keep = add(keep, got)
    return keep[0]


def sum_everywhere(values):
    for bit in bits_of(lax.axis_size("dp")):
        values = values + lax.ppermute(values, "dp", flip_bit("dp", bit))
    halves = values.reshape(2, values.shape[0] // 2, values.shape[1])
    core = lax.axis_index("tm") % 2
    send = lax.dynamic_index_in_dim(halves, 1 - core, 0, keepdims=False)
    keep = lax.dynamic_index_in_dim(halves, core, 0, keepdims=False)
    values = (keep + lax.ppermute(send, "tm", flip_bit("tm", 0))).astype(BF)
    terms = [values]
    for mask in range(2, lax.axis_size("tm"), 2):
        terms.append(lax.ppermute(values, "tm", flip("tm", mask)))
    terms = [term.astype(F32) for term in terms]
    while len(terms) > 1:
        terms = [a + b for a, b in zip(terms[::2], terms[1::2])]
    values = terms[0]
    got = lax.ppermute(values, "tm", flip_bit("tm", 0))
    return jnp.concatenate([jnp.where(core == 0, values, got), jnp.where(core == 0, got, values)])


def sum_across(sides, piece):
    place = lax.axis_index("tm") // 2
    each = sides[0].shape[1] // piece
    lists = [[side[:, i * piece : (i + 1) * piece] for i in range(each)] for side in sides]

    def exchange(blocks, bit):
        upper = (place >> bit) & 1 == 1
        send = [jnp.where(upper, a, b).astype(BF) for a, b in zip(blocks[::2], blocks[1::2])]
        keep = [jnp.where(upper, b, a) for a, b in zip(blocks[::2], blocks[1::2])]
        got = [lax.ppermute(block, "tm", flip("tm", 2 << bit)) for block in send]
        return [k.astype(F32) + g.astype(F32) for k, g in zip(keep, got)]

    *inner, last = bits_of(2 * each)
    for bit in inner:
        lists = [exchange(blocks, bit) for blocks in lists]
    return exchange([lists[0][0], lists[1][0]], last)[0]


def edges(values, width):
    count = lax.axis_size("tm")
    low = lax.ppermute(values[-width:], "tm", [(i, i + 1) for i in range(count - 1)])
    high = lax.ppermute(values[:width], "tm", [(i + 1, i) for i in range(count - 1)])
    return low, high


def local(frames, route, utterance, gain, w_in, kernel, cotangent):
    panels, length, width = frames.shape[2:]
    owners = lax.axis_size("tm")
    rows = panels * length
    taps = kernel.shape[0]
    reach = taps // 2
    assert reach < RIM and taps == 31
    loaded = frames[0, 0]
    target = route[0, 0]
    labels = utterance[0, 0]
    upstream = cotangent[0, 0]
    core = lax.axis_index("tm") % 2
    owner_of = target // panels
    pick = owner_of[None, :] == jnp.arange(owners, dtype=jnp.int32)[:, None]
    panel_of = jnp.sum(jnp.where(pick, jnp.arange(panels, dtype=jnp.int32)[None, :], 0), axis=1)
    outgoing = pick_panels(loaded, panel_of.astype(jnp.int32), owners)
    arrived = lax.all_to_all(outgoing, "tm", split_axis=0, concat_axis=0, tiled=True)
    me = lax.axis_index("tm")
    tags = jnp.stack([target, labels + 1])[None]
    tags = jnp.concatenate([tags, lax.ppermute(tags, "tm", flip_bit("tm", 0))])
    rest = [lax.ppermute(tags, "tm", flip("tm", i)) for i in range(2, owners, 2)]
    tags = jnp.concatenate([tags] + rest)
    loader = (jnp.arange(owners, dtype=jnp.int32) ^ me)[None, :, None]
    position = me * panels - 1 + jnp.arange(panels + 2, dtype=jnp.int32)
    found = tags[None, :, 0] == position[:, None, None]
    line = jnp.sum(jnp.where(found, tags[None, :, 1], 0), axis=(1, 2))
    source = jnp.sum(jnp.where(found[1:-1], loader, 0), axis=(1, 2)).astype(jnp.int32)
    flags = jnp.concatenate([line[1:-1] == line[:-2], line[1:-1] == line[2:]]).astype(jnp.int32)

    full_in = gather_weights(w_in, core)
    normed, lin, gate, glu = forward(arrived, source, gain, full_in, panels, 4 * LANES)
    other_normed = lax.ppermute(normed, "tm", flip_bit("tm", 0))
    glu_low, glu_high = edges(glu, 2 * RIM)

    lane_block = 2 * LANES
    column = lambda height: pl.BlockSpec((height, lane_block), lambda j, idx: (0, j))
    sizes = dict(panels=panels, length=length, taps=taps)
    padded_of = lambda lanes: pltpu.VMEM((lanes // LANES, panels, length + 2 * RIM, LANES), F32)
    up_rows = upstream.reshape(rows, width)
    up_low, up_high = edges(up_rows, RIM)
    grad_depth, grad_low, grad_high = pl.pallas_call(
        functools.partial(depth_body, **sizes),
        grid_spec=pltpu.PrefetchScalarGridSpec(
            num_scalar_prefetch=1,
            grid=(width // lane_block,),
            in_specs=[column(h) for h in (rows, 2 * RIM, 2 * RIM, rows, RIM, RIM, taps)],
            out_specs=[column(rows), column(RIM), column(RIM)],
            scratch_shapes=[
                padded_of(lane_block),
                pltpu.VMEM((lane_block // LANES, 2, 3 * RIM, LANES), F32),
            ],
        ),
        out_shape=[jax.ShapeDtypeStruct((h, width), BF) for h in (rows, RIM, RIM)],
        compiler_params=params(1, 48),
        name="depth",
    )(flags, glu, glu_low, glu_high, up_rows, up_low, up_high, kernel)
    kernel_term = pl.pallas_call(
        functools.partial(taps_body, **sizes),
        grid_spec=pltpu.PrefetchScalarGridSpec(
            num_scalar_prefetch=1,
            grid=(width // lane_block,),
            in_specs=[column(h) for h in (rows, 2 * RIM, 2 * RIM, rows)],
            out_specs=column(taps + 1),
            scratch_shapes=[padded_of(lane_block), pltpu.VMEM((taps + 1, 8, LANES), F32)],
        ),
        out_shape=jax.ShapeDtypeStruct((taps + 1, width), F32),
        compiler_params=params(1, 48),
        name="taps",
    )(flags, glu, glu_low, glu_high, grad_depth)

    piece = 2 * width // owners
    arguments = (flags, grad_depth, grad_low, grad_high, lin, gate, kernel)
    if piece % LANES == 0:
        *give, own_lin, own_gate = gated(*arguments, piece, 2, core, sizes)
        own = (own_lin, own_gate)
        others = [lax.ppermute(g, "tm", flip_bit("tm", 0)) for g in give]
        gradients, run = (*own, *give), piece
    else:
        gradients, run = tuple(gated(*arguments, lane_block, 1, core, sizes)), width
        pick_parity = lambda values, parity: lax.dynamic_index_in_dim(
            values.reshape(rows, owners // 4, 2, piece), parity, 2, keepdims=False
        ).reshape(rows, width // 2)
        give = [pick_parity(g, 1 - core) for g in gradients]
        others = [lax.ppermute(g, "tm", flip_bit("tm", 0)) for g in give]
        own = [pick_parity(g, core) for g in gradients]
    grad_slots, gain_term = back(
        gradients, core, full_in, arrived, source, upstream, gain, run, 2 * LANES
    )
    returned = lax.all_to_all(grad_slots, "tm", split_axis=0, concat_axis=0, tiled=True)
    count = lax.axis_size("dp")
    bits = bits_of(count)
    shares = [
        outer_halved((normed, other_normed), (own[side], others[side]), order)
        for side, order in ((0, bits), (1, bits[::-1]))
    ]
    shard_in = sum_across(shares, piece)
    grad_loaded = pick_blocks(returned, owner_of.astype(jnp.int32), panels)
    sums = sum_everywhere(jnp.concatenate([kernel_term[:taps], gain_term], axis=0))
    return (grad_loaded[None, None], shard_in, sums[:taps], sums[taps])


def solution(mesh):
    in_specs = (
        P("dp", "tm", None, None, None),
        P("dp", "tm", None),
        P("dp", "tm", None),
        P(),
        P("dp", None),
        P(),
        P("dp", "tm", None, None, None),
    )
    out_specs = (P("dp", "tm", None, None, None), P("dp", "tm"), P(), P())
    return jax.shard_map(local, mesh=mesh, in_specs=in_specs, out_specs=out_specs, check_vma=False)
```

```python
import functools

import jax
import jax.numpy as jnp
from jax import lax
from jax.experimental import pallas as pl
from jax.experimental.pallas import tpu as pltpu
from jax.sharding import PartitionSpec as P

BF = jnp.bfloat16
F32 = jnp.float32
RIM = 16
LANES = 128
TILE = 32


def params(count, mib):
    return pltpu.CompilerParams(
        dimension_semantics=("arbitrary",) * count, vmem_limit_bytes=mib << 20
    )


def flip(axis, mask):
    return [(i, i ^ mask) for i in range(lax.axis_size(axis))]


def flip_bit(axis, bit):
    return flip(axis, 1 << bit)


def bits_of(count):
    bits = count.bit_length() - 1
    assert 1 << bits == count
    return list(range(bits))


def pick_body(index, source, target, sems, *, count):
    copies = [
        pltpu.make_async_copy(source.at[index[i]], target.at[i], sems.at[i]) for i in range(count)
    ]
    for copy in copies:
        copy.start()
    for copy in copies:
        copy.wait()


def pick_panels(source, index, count):
    _, rows, width = source.shape
    return pl.pallas_call(
        functools.partial(pick_body, count=count),
        grid_spec=pltpu.PrefetchScalarGridSpec(
            num_scalar_prefetch=1,
            grid=(1,),
            in_specs=[pl.BlockSpec(source.shape, lambda i, idx: (0, 0, 0))],
            out_specs=pl.BlockSpec(memory_space=pltpu.HBM),
            scratch_shapes=[pltpu.SemaphoreType.DMA((count,))],
        ),
        out_shape=jax.ShapeDtypeStruct((count, rows, width), source.dtype),
        compiler_params=params(1, 48),
    )(index, source)


def copy_body(_, source, target):
    target[...] = source[...]


def pick_blocks(source, index, count):
    _, rows, width = source.shape
    return pl.pallas_call(
        copy_body,
        grid_spec=pltpu.PrefetchScalarGridSpec(
            num_scalar_prefetch=1,
            grid=(count,),
            in_specs=[pl.BlockSpec((1, rows, width), lambda i, idx: (idx[i], 0, 0))],
            out_specs=pl.BlockSpec((1, rows, width), lambda i, idx: (i, 0, 0)),
        ),
        out_shape=jax.ShapeDtypeStruct((count, rows, width), source.dtype),
        compiler_params=params(1, 48),
    )(index, source)


def gather_order(block, order):
    have = block[None]
    relative = [0]
    for bit in order:
        got = lax.ppermute(have, "dp", flip_bit("dp", bit))
        have = jnp.concatenate([have, got], axis=0)
        relative = relative + [r ^ (1 << bit) for r in relative]
    return have, relative


def gather_weights(w_in, core):
    shard, width = w_in.shape
    quarter = shard // 4
    count = lax.axis_size("dp")
    place = lax.axis_index("dp")
    bits = bits_of(count)
    half = lax.dynamic_slice_in_dim(w_in, core * (2 * quarter), 2 * quarter, axis=0)
    first, first_rel = gather_order(half[:quarter], bits)
    second, second_rel = gather_order(half[quarter:], bits[::-1])
    other_first = lax.ppermute(first, "tm", flip_bit("tm", 0))
    other_second = lax.ppermute(second, "tm", flip_bit("tm", 0))
    rels = [first_rel, second_rel]

    def out_index(side):
        index = []
        for source in range(2):
            for position in range(count):
                index.append(((place ^ rels[source][position]) * 2 + side) * 2 + source)
        return jnp.stack(index).astype(jnp.int32)

    def body(_, a, b, *rest):
        target = rest[-1]
        for number, ref in enumerate((a, b)):

            @pl.when(pl.program_id(0) == number)
            def _():
                target[...] = ref[...]

    def spec(number):
        def index(source, position, _):
            last = count - 1 if number == 0 else 0
            return (jnp.where(source == number, position, last), 0, 0)

        return pl.BlockSpec((1, quarter, width), index)

    def put(side, pair, *base):
        return pl.pallas_call(
            body,
            grid_spec=pltpu.PrefetchScalarGridSpec(
                num_scalar_prefetch=1,
                grid=(2, count),
                in_specs=[spec(0), spec(1)] + [pl.BlockSpec(memory_space=pl.ANY) for _ in base],
                out_specs=pl.BlockSpec(
                    (1, quarter, width),
                    lambda source, position, idx: (idx[source * count + position], 0, 0),
                ),
            ),
            out_shape=jax.ShapeDtypeStruct((4 * count, quarter, width), w_in.dtype),
            input_output_aliases={3: 0} if base else {},
            compiler_params=params(2, 48),
        )(out_index(side), *pair, *base)

    full = put(core, (first, second))
    full = put(1 - core, (other_first, other_second), full)
    return full.reshape(4 * quarter * count, width)


def forward_body(source, x_hbm, gain_ref, lin_w, gate_w, parts, lin_out, gate_out, glu_out, normed, xs, sems, *, panels):
    rows = xs.shape[1]

    def fetch(s):
        return pltpu.make_async_copy(x_hbm.at[source[s]], xs.at[s], sems.at[s])

    @pl.when(pl.program_id(0) == 0)
    def _():
        for s in range(panels):
            fetch(s).start()
        for s in range(panels):
            fetch(s).wait()

            x = xs[s].astype(F32)
            x = x - jnp.mean(x, axis=1, keepdims=True)
            scale = lax.rsqrt(jnp.mean(x * x, axis=1, keepdims=True) + 1e-05)
            normed[s * rows : (s + 1) * rows, :] = (x * scale * gain_ref[...]).astype(BF)

        count, _, shard = parts.shape
        for block in range(count):
            parts[block ^ source[panels]] = normed[:, block * shard : (block + 1) * shard]

    lin = jnp.dot(normed[...], lin_w[...], preferred_element_type=F32)
    lin_out[...] = lin
    gate = jnp.dot(normed[...], gate_w[...], preferred_element_type=F32)
    gate_out[...] = gate
    glu_out[...] = (lin * jax.nn.sigmoid(gate)).astype(BF)


def forward(arrived, source, gain, full_in, panels, block):
    _, rows, width = arrived.shape
    blocks = width // block
    column = pl.BlockSpec((panels * rows, block), lambda j, idx: (0, j))
    wide = lambda dtype: jax.ShapeDtypeStruct((panels * rows, width), dtype)
    count = lax.axis_size("dp")
    parts = jax.ShapeDtypeStruct((count, panels * rows, width // count), BF)
    return pl.pallas_call(
        functools.partial(forward_body, panels=panels),
        grid_spec=pltpu.PrefetchScalarGridSpec(
            num_scalar_prefetch=1,
            grid=(blocks,),
            in_specs=[
                pl.BlockSpec(memory_space=pl.ANY),
                pl.BlockSpec((1, width), lambda j, idx: (0, 0)),
                pl.BlockSpec((width, block), lambda j, idx: (0, j)),
                pl.BlockSpec((width, block), lambda j, idx: (0, blocks + j)),
            ],
            out_specs=[
                pl.BlockSpec(parts.shape, lambda j, idx: (0, 0, 0)),
                column,
                column,
                column,
            ],
            scratch_shapes=[
                pltpu.VMEM((panels * rows, width), BF),
                pltpu.VMEM((panels, rows, width), BF),
                pltpu.SemaphoreType.DMA((panels,)),
            ],
        ),
        out_shape=[parts, wide(F32), wide(F32), wide(BF)],
        compiler_params=params(1, 48),
    )(jnp.append(source, lax.axis_index("dp")), arrived, gain.reshape(1, width), full_in, full_in)


def fill_padded(flags, padded, main, low, high, panels, length):
    for s in range(panels):
        at = s * length
        middle = main[at : at + length, :].astype(F32)
        before = low[low.shape[0] - RIM :, :] if s == 0 else main[at - RIM : at, :]
        after = high[:RIM, :] if s == panels - 1 else main[at + length : at + length + RIM, :]
        before = jnp.where(flags[s] > 0, before.astype(F32), 0.0)
        after = jnp.where(flags[panels + s] > 0, after.astype(F32), 0.0)
        for chunk in range(main.shape[1] // LANES):
            lanes = slice(chunk * LANES, (chunk + 1) * LANES)
            padded[chunk, s, RIM : RIM + length, :] = middle[:, lanes]
            padded[chunk, s, 0:RIM, :] = before[:, lanes]
            padded[chunk, s, RIM + length :, :] = after[:, lanes]


def shifted_sum(padded, weights, chunk, s, start, taps, flip, height=TILE):
    lanes = pl.ds(chunk * LANES, LANES)
    total = jnp.zeros((height, LANES), F32)
    for tap in range(taps):
        offset = taps - tap if flip else tap + 1
        view = padded[chunk, s, pl.ds(start + offset, height), :]
        total = total + weights[pl.ds(tap, 1), lanes] * view
    return total


def tiles(width, panels, length, work):
    for chunk in range(width // LANES):

        def step(s, carry):
            for start in range(0, length, TILE):
                rows = pl.ds(pl.multiple_of(s * length + start, TILE), TILE)
                work(chunk, s, start, rows, pl.ds(chunk * LANES, LANES))
            return carry

        lax.fori_loop(0, panels, step, 0)


def depth_body(
    flags, glu, low, high, upstream, up_low, up_high, weights, out, out_low, out_high, padded, ends, *, panels, length, taps
):
    fill_padded(flags, padded, glu, low, high, panels, length)
    rows = panels * length

    def grad(depth, up):
        sig = jax.nn.sigmoid(depth)
        return (up.astype(F32) * sig * (1.0 + depth * (1.0 - sig))).astype(BF)

    for chunk in range(glu.shape[1] // LANES):
        lanes = slice(chunk * LANES, (chunk + 1) * LANES)
        ends[chunk, 0, 0 : 2 * RIM, :] = low[:, lanes].astype(F32)
        ends[chunk, 0, 2 * RIM :, :] = glu[0:RIM, lanes].astype(F32)
        ends[chunk, 1, 0:RIM, :] = glu[rows - RIM : rows, lanes].astype(F32)
        ends[chunk, 1, RIM:, :] = high[:, lanes].astype(F32)
        for side, up, to in ((0, up_low, out_low), (1, up_high, out_high)):
            depth = shifted_sum(ends, weights, chunk, side, 0, taps, False, RIM)
            to[:, lanes] = grad(depth, up[:, lanes])

    def work(chunk, s, start, at, lanes):
        depth = shifted_sum(padded, weights, chunk, s, start, taps, False)
        out[at, lanes] = grad(depth, upstream[at, lanes])

    tiles(glu.shape[1], panels, length, work)


def taps_body(flags, glu, low, high, grad, out, padded, partial, *, panels, length, taps):
    fill_padded(flags, padded, glu, low, high, panels, length)
    for chunk in range(glu.shape[1] // LANES):
        lanes = pl.ds(chunk * LANES, LANES)
        partial[...] = jnp.zeros_like(partial)

        def step(s, carry):
            rows = pl.ds(pl.multiple_of(s * length, length), length)
            g = grad[rows, lanes].astype(F32)
            for tap in range(taps):
                product = g * padded[chunk, s, pl.ds(tap + 1, length), :]
                partial[tap] += jnp.sum(product.reshape(length // 8, 8, LANES), axis=0)
            return carry

        lax.fori_loop(0, panels, step, 0)
        out[:, lanes] = jnp.sum(partial[...], axis=1)


def gated_body(flags, grad, low, high, lin, gate, weights, *refs, panels, length, taps, steps):
    *outs, padded = refs
    fill_padded(flags, padded, grad, low, high, panels, length)

    def run(first, second):
        def work(chunk, s, start, rows, lanes):
            total = shifted_sum(padded, weights, chunk, s, start, taps, True)
            sig = jax.nn.sigmoid(gate[rows, lanes])
            scaled = total * sig
            first[rows, lanes] = scaled.astype(BF)
            second[rows, lanes] = (scaled * lin[rows, lanes] * (1.0 - sig)).astype(BF)

        tiles(grad.shape[1], panels, length, work)

    for part in range(len(outs) // 2):

        @pl.when(pl.program_id(0) // steps == part)
        def _():
            run(*outs[2 * part : 2 * part + 2])


def gated(flags, grad_depth, low, high, lin, gate, kernel, block, parts, core, sizes):
    rows, width = grad_depth.shape
    panels = sizes["panels"]
    steps = width // block // parts

    def column(height):
        def index(j, idx):
            if parts == 1:
                return (0, j)
            parity = jnp.where(j < steps, 1 - idx[2 * panels], idx[2 * panels])
            return (0, 2 * (j % steps) + parity)

        return pl.BlockSpec((height, block), index)

    def out(part):
        return pl.BlockSpec((rows, block), lambda j, idx: (0, jnp.clip(j - part * steps, 0, steps - 1)))

    return pl.pallas_call(
        functools.partial(gated_body, steps=steps, **sizes),
        grid_spec=pltpu.PrefetchScalarGridSpec(
            num_scalar_prefetch=1,
            grid=(parts * steps,),
            in_specs=[column(h) for h in (rows, RIM, RIM, rows, rows, kernel.shape[0])],
            out_specs=[out(part) for part in range(parts) for _ in range(2)],
            scratch_shapes=[
                pltpu.VMEM((block // LANES, panels, sizes["length"] + 2 * RIM, LANES), F32)
            ],
        ),
        out_shape=[jax.ShapeDtypeStruct((rows, width // parts), BF)] * (2 * parts),
        compiler_params=params(1, 48),
    )(jnp.append(flags, core), grad_depth, low, high, lin, gate, kernel)


def back_body(source, *refs, grads, block, panels, piece):
    gradients = refs[:grads]
    w_ref, x_hbm, up_hbm, gain_ref, out_hbm, gain_out, total, xs, ups, outs, sems = refs[grads:]
    step = pl.program_id(0)

    def fetch(s):
        return (
            pltpu.make_async_copy(x_hbm.at[source[s]], xs.at[s], sems.at[s]),
            pltpu.make_async_copy(up_hbm.at[s], ups.at[s], sems.at[panels + s]),
        )

    def put(s):
        return pltpu.make_async_copy(outs.at[s], out_hbm.at[source[s]], sems.at[2 * panels + s])

    @pl.when(step == 0)
    def _():
        for s in range(panels):
            for copy in fetch(s):
                copy.start()

    acc = None
    for number, grad in enumerate(gradients):
        pieces = grad.shape[1] // piece
        for i in range(pieces):
            column = (number % 2 * pieces + i) * (grads // 2) * piece
            if grads > 2:
                column = column + (source[panels] ^ (number // 2)) * piece
                column = pl.multiple_of(column, LANES)
            term = lax.dot_general(
                grad[:, i * piece : (i + 1) * piece],
                w_ref[:, pl.ds(column, piece)],
                (((1,), (1,)), ((), ())),
                preferred_element_type=F32,
            )
            acc = term if acc is None else acc + term
    total[:, pl.ds(pl.multiple_of(step * block, block), block)] = acc

    @pl.when(step == pl.num_programs(0) - 1)
    def _():
        rows = xs.shape[1]
        gain = gain_ref[...]
        gain_sum = jnp.zeros_like(gain)
        for s in range(panels):
            for copy in fetch(s):
                copy.wait()

            x = xs[s].astype(F32)
            x = x - jnp.mean(x, axis=1, keepdims=True)
            scale = lax.rsqrt(jnp.mean(x * x, axis=1, keepdims=True) + 1e-05)
            unit = x * scale
            g = total[s * rows : (s + 1) * rows, :]
            gain_sum = gain_sum + jnp.sum(g * unit, axis=0, keepdims=True)
            q = g * gain
            mean_q = jnp.mean(q, axis=1, keepdims=True)
            mean_u = jnp.mean(q * unit, axis=1, keepdims=True)
            outs[s] = (ups[s].astype(F32) + scale * (q - mean_q - unit * mean_u)).astype(BF)
            put(s).start()
        gain_out[...] = gain_sum
        for s in range(panels):
            put(s).wait()


def back(gradients, core, full_in, arrived, source, upstream, gain, piece, block):
    _, rows, width = arrived.shape
    panels = upstream.shape[0]
    constant = lambda rank: (lambda n, idx: (0,) * rank)
    hbm = pl.BlockSpec(memory_space=pl.ANY)
    panel_scratch = pltpu.VMEM((panels, rows, width), BF)
    return pl.pallas_call(
        functools.partial(back_body, grads=len(gradients), block=block, panels=panels, piece=piece),
        grid_spec=pltpu.PrefetchScalarGridSpec(
            num_scalar_prefetch=1,
            grid=(width // block,),
            in_specs=[pl.BlockSpec(g.shape, constant(2)) for g in gradients]
            + [
                pl.BlockSpec((block, full_in.shape[1]), lambda n, idx: (n, 0)),
                hbm,
                hbm,
                pl.BlockSpec((1, width), constant(2)),
            ],
            out_specs=[hbm, pl.BlockSpec((1, width), constant(2))],
            scratch_shapes=[
                pltpu.VMEM((panels * rows, width), F32),
                panel_scratch,
                panel_scratch,
                panel_scratch,
                pltpu.SemaphoreType.DMA((3 * panels,)),
            ],
        ),
        out_shape=[
            jax.ShapeDtypeStruct(arrived.shape, BF),
            jax.ShapeDtypeStruct((1, width), F32),
        ],
        compiler_params=params(1, 48),
    )(jnp.append(source, core), *gradients, full_in, arrived, upstream, gain.reshape(1, width))


def outer_sum(lefts, rights):
    terms = [
        lax.dot_general(a, b, (((1,), (0,)), ((), ())), preferred_element_type=F32)
        for a, b in zip(lefts, rights)
    ]
    return (terms[0] + terms[1]).astype(BF)


def outer_halved(lefts, rights, order):
    count = lefts[0].shape[0]
    rels = sorted(range(count), key=lambda r: [(r >> bit) & 1 for bit in order])
    half = count // 2
    pick = lambda left, some: jnp.concatenate([left[r : r + 1] for r in some])
    send = outer_sum([pick(left, rels[half:]) for left in lefts], rights)
    keep = outer_sum([pick(left, rels[:half]) for left in lefts], rights)
    add = lambda a, b: (a.astype(F32) + b.astype(F32)).astype(BF)
    for bit in order:
        got = lax.ppermute(send, "dp", flip_bit("dp", bit))
        half = half // 2
        if half:
            send = add(keep[half:], got[half:])
            keep = add(keep[:half], got[:half])
        else:
            keep = add(keep, got)
    return keep[0]


def sum_everywhere(values):
    for bit in bits_of(lax.axis_size("dp")):
        values = values + lax.ppermute(values, "dp", flip_bit("dp", bit))
    halves = values.reshape(2, values.shape[0] // 2, values.shape[1])
    core = lax.axis_index("tm") % 2
    send = lax.dynamic_index_in_dim(halves, 1 - core, 0, keepdims=False)
    keep = lax.dynamic_index_in_dim(halves, core, 0, keepdims=False)
    values = (keep + lax.ppermute(send, "tm", flip_bit("tm", 0))).astype(BF)
    terms = [values]
    for mask in range(2, lax.axis_size("tm"), 2):
        terms.append(lax.ppermute(values, "tm", flip("tm", mask)))
    terms = [term.astype(F32) for term in terms]
    while len(terms) > 1:
        terms = [a + b for a, b in zip(terms[::2], terms[1::2])]
    values = terms[0]
    got = lax.ppermute(values, "tm", flip_bit("tm", 0))
    return jnp.concatenate([jnp.where(core == 0, values, got), jnp.where(core == 0, got, values)])


def sum_across(share):
    count = share.shape[0]
    place = lax.axis_index("tm") // 2
    total = lax.dynamic_index_in_dim(share, place, 0, keepdims=False).astype(F32)
    for turn in range(1, count):
        piece = lax.dynamic_index_in_dim(share, place ^ turn, 0, keepdims=False)
        total = total + lax.ppermute(piece, "tm", flip("tm", 2 * turn)).astype(F32)
    return total


def edges(values, width):
    count = lax.axis_size("tm")
    low = lax.ppermute(values[-width:], "tm", [(i, i + 1) for i in range(count - 1)])
    high = lax.ppermute(values[:width], "tm", [(i + 1, i) for i in range(count - 1)])
    return low, high


def local(frames, route, utterance, gain, w_in, kernel, cotangent):
    panels, length, width = frames.shape[2:]
    owners = lax.axis_size("tm")
    rows = panels * length
    taps = kernel.shape[0]
    reach = taps // 2
    assert reach < RIM and taps == 31
    loaded = frames[0, 0]
    target = route[0, 0]
    labels = utterance[0, 0]
    upstream = cotangent[0, 0]
    core = lax.axis_index("tm") % 2
    owner_of = target // panels
    pick = owner_of[None, :] == jnp.arange(owners, dtype=jnp.int32)[:, None]
    panel_of = jnp.sum(jnp.where(pick, jnp.arange(panels, dtype=jnp.int32)[None, :], 0), axis=1)
    outgoing = pick_panels(loaded, panel_of.astype(jnp.int32), owners)
    arrived = lax.all_to_all(outgoing, "tm", split_axis=0, concat_axis=0, tiled=True)
    me = lax.axis_index("tm")
    tags = jnp.stack([target, labels + 1])[None]
    tags = jnp.concatenate([tags, lax.ppermute(tags, "tm", flip_bit("tm", 0))])
    rest = [lax.ppermute(tags, "tm", flip("tm", i)) for i in range(2, owners, 2)]
    tags = jnp.concatenate([tags] + rest)
    loader = (jnp.arange(owners, dtype=jnp.int32) ^ me)[None, :, None]
    position = me * panels - 1 + jnp.arange(panels + 2, dtype=jnp.int32)
    found = tags[None, :, 0] == position[:, None, None]
    line = jnp.sum(jnp.where(found, tags[None, :, 1], 0), axis=(1, 2))
    source = jnp.sum(jnp.where(found[1:-1], loader, 0), axis=(1, 2)).astype(jnp.int32)
    flags = jnp.concatenate([line[1:-1] == line[:-2], line[1:-1] == line[2:]]).astype(jnp.int32)

    full_in = gather_weights(w_in, core)
    normed, lin, gate, glu = forward(arrived, source, gain, full_in, panels, 4 * LANES)
    other_normed = lax.ppermute(normed, "tm", flip_bit("tm", 0))
    glu_low, glu_high = edges(glu, 2 * RIM)

    lane_block = 2 * LANES
    column = lambda height: pl.BlockSpec((height, lane_block), lambda j, idx: (0, j))
    sizes = dict(panels=panels, length=length, taps=taps)
    padded_of = lambda lanes: pltpu.VMEM((lanes // LANES, panels, length + 2 * RIM, LANES), F32)
    up_rows = upstream.reshape(rows, width)
    up_low, up_high = edges(up_rows, RIM)
    grad_depth, grad_low, grad_high = pl.pallas_call(
        functools.partial(depth_body, **sizes),
        grid_spec=pltpu.PrefetchScalarGridSpec(
            num_scalar_prefetch=1,
            grid=(width // lane_block,),
            in_specs=[column(h) for h in (rows, 2 * RIM, 2 * RIM, rows, RIM, RIM, taps)],
            out_specs=[column(rows), column(RIM), column(RIM)],
            scratch_shapes=[
                padded_of(lane_block),
                pltpu.VMEM((lane_block // LANES, 2, 3 * RIM, LANES), F32),
            ],
        ),
        out_shape=[jax.ShapeDtypeStruct((h, width), BF) for h in (rows, RIM, RIM)],
        compiler_params=params(1, 48),
    )(flags, glu, glu_low, glu_high, up_rows, up_low, up_high, kernel)
    kernel_term = pl.pallas_call(
        functools.partial(taps_body, **sizes),
        grid_spec=pltpu.PrefetchScalarGridSpec(
            num_scalar_prefetch=1,
            grid=(width // lane_block,),
            in_specs=[column(h) for h in (rows, 2 * RIM, 2 * RIM, rows)],
            out_specs=column(taps + 1),
            scratch_shapes=[padded_of(lane_block), pltpu.VMEM((taps + 1, 8, LANES), F32)],
        ),
        out_shape=jax.ShapeDtypeStruct((taps + 1, width), F32),
        compiler_params=params(1, 48),
        name="taps",
    )(flags, glu, glu_low, glu_high, grad_depth)

    piece = 2 * width // owners
    arguments = (flags, grad_depth, grad_low, grad_high, lin, gate, kernel)
    if piece % LANES == 0:
        *give, own_lin, own_gate = gated(*arguments, piece, 2, core, sizes)
        own = (own_lin, own_gate)
        others = [lax.ppermute(g, "tm", flip_bit("tm", 0)) for g in give]
        gradients, run = (*own, *give), piece
    else:
        gradients, run = tuple(gated(*arguments, lane_block, 1, core, sizes)), width
        pick_parity = lambda values, parity: lax.dynamic_index_in_dim(
            values.reshape(rows, owners // 4, 2, piece), parity, 2, keepdims=False
        ).reshape(rows, width // 2)
        give = [pick_parity(g, 1 - core) for g in gradients]
        others = [lax.ppermute(g, "tm", flip_bit("tm", 0)) for g in give]
        own = [pick_parity(g, core) for g in gradients]
    grad_slots, gain_term = back(
        gradients, core, full_in, arrived, source, upstream, gain, run, 2 * LANES
    )
    returned = lax.all_to_all(grad_slots, "tm", split_axis=0, concat_axis=0, tiled=True)
    count = lax.axis_size("dp")
    bits = bits_of(count)
    shares = [
        outer_halved((normed, other_normed), (own[side], others[side]), order)
        for side, order in ((0, bits), (1, bits[::-1]))
    ]
    share = jnp.concatenate(shares, axis=1)
    share = share.reshape(width // count, owners // 2, piece).transpose(1, 0, 2)
    shard_in = sum_across(share)
    grad_loaded = pick_blocks(returned, owner_of.astype(jnp.int32), panels)
    sums = sum_everywhere(jnp.concatenate([kernel_term[:taps], gain_term], axis=0))
    return (grad_loaded[None, None], shard_in, sums[:taps], sums[taps])


def solution(mesh):
    in_specs = (
        P("dp", "tm", None, None, None),
        P("dp", "tm", None),
        P("dp", "tm", None),
        P(),
        P("dp", None),
        P(),
        P("dp", "tm", None, None, None),
    )
    out_specs = (P("dp", "tm", None, None, None), P("dp", "tm"), P(), P())
    return jax.shard_map(local, mesh=mesh, in_specs=in_specs, out_specs=out_specs, check_vma=False)
```
